32 devices in a mesh: expert: 4 (over x, core), fsdp: 8 (over z, y).
Axes of the slice: x: 2, y: 2, z: 4, core: 2. Of those that a mesh axis runs over, the one named last changes fastest.
Arguments:
- hidden_in: bfloat16 [32, 1024, 768], P(('expert', 'fsdp')), may hold values from -6 to 6
- prev_logits: bfloat16 [32, 1024, 8], P(('expert', 'fsdp')), may hold values from -6 to 6
- seq_lengths: int32 [32], replicated, may hold values from 256 to 1024, as said below
- seq_order: int32 [32], replicated, may hold values from 0 to 31, as said below
- routes: int32 [32, 1024, 2], P(('expert', 'fsdp')), may hold values from 0 to 7, all different within a row; in each aligned block of 1024 rows (0 to 1023, 1024 to 2047, ..., all dimensions but the last counted through in order) at most 256 rows name the same one
- w_query: bfloat16 [768, 768], P(None, 'fsdp'), may hold values from -0.21875 to 0.21875
- w_key: bfloat16 [768, 768], P(None, 'fsdp'), may hold values from -0.21875 to 0.21875
- w_value: bfloat16 [768, 768], P(None, 'fsdp'), may hold values from -0.21875 to 0.21875
- w_output: bfloat16 [768, 768], P('fsdp'), may hold values from -1.75 to 1.75
- gain_attn: bfloat16 [768], P('fsdp'), may hold values from 0.5 to 1.5
- gain_moe: bfloat16 [768], P('fsdp'), may hold values from 0.5 to 1.5
- w_router: bfloat16 [768, 8], P('fsdp'), may hold values from -0.109375 to 0.109375
- w_gating: bfloat16 [8, 8], replicated, may hold values from -1 to 1
- w_const: bfloat16 [768, 4], P('fsdp'), may hold values from -0.21875 to 0.21875
- v_const: bfloat16 [2, 768], P(None, 'fsdp'), may hold values from -6 to 6
- w_gate: bfloat16 [4, 768, 2048], P('expert', None, 'fsdp'), may hold values from -0.21875 to 0.21875
- w_up: bfloat16 [4, 768, 2048], P('expert', None, 'fsdp'), may hold values from -0.21875 to 0.21875
- w_down: bfloat16 [4, 2048, 768], P('expert', 'fsdp'), may hold values from -1.5 to 1.5
- out_grad: bfloat16 [32, 1024, 768], P(('expert', 'fsdp')), may hold values from -6 to 6
Outputs:
- hidden_out: bfloat16 [32, 1024, 768], P(('expert', 'fsdp'))
- grad_hidden: float32 [32, 1024, 768], P(('expert', 'fsdp'))
- grad_prev: float32 [32, 1024, 8], P(('expert', 'fsdp'))
- grad_w_query: float32 [768, 768], P(None, 'fsdp')
- grad_w_key: float32 [768, 768], P(None, 'fsdp')
- grad_w_value: float32 [768, 768], P(None, 'fsdp')
- grad_w_output: float32 [768, 768], P('fsdp')
- grad_gain_attn: float32 [768], P('fsdp')
- grad_gain_moe: float32 [768], P('fsdp')
- grad_w_router: float32 [768, 8], P('fsdp')
- grad_w_gating: float32 [8, 8], replicated
- grad_w_const: float32 [768, 4], P('fsdp')
- grad_v_const: float32 [2, 768], P(None, 'fsdp')
- grad_w_gate: float32 [4, 768, 2048], P('expert', None, 'fsdp')
- grad_w_up: float32 [4, 768, 2048], P('expert', None, 'fsdp')
- grad_w_down: float32 [4, 2048, 768], P('expert', 'fsdp')
The draws below stay inside these ranges and needn't reach their ends.
Inputs may be any that keep to these rules, and one draw needn't show every extreme that they name: `seq_lengths`: some sequence has all 1024 positions live. `seq_order`: A permutation: slot i takes a sequence whose slot of the same index along fsdp and the same place among a device's 1 slots differs from i at most in its index along expert. Each position names two different choices: ids below 4 are feed-forward experts, 4 the zero expert, 5 the copy expert, 6 and 7 the constant experts. Within the rows of one device no id is named by more than 256 routes, a bound that some block reaches.
All inputs are finite; a program needn't handle non-finite values.
Results may differ from the reference program's by a relative error of at most 0.022.
Values may be sent and summed in bfloat16 or wider, within the bound.
No kernel may reach another device: no remote copies, remote signals or barrier semaphores. Data moves between devices by JAX's collectives and lax.ppermute only.
A program may use at most 320 MiB of HBM per device.

```python
import math
import jax
import jax.numpy as jnp
import numpy as np
from jax import lax

D = 768
HEADS = 12
HD = 64
FF = 2048
LMAX = 1024
EXP_DEV = 1
SEQ_DEV = 1
NFFN = 4
NE = 8
NSEQ = 32
CAP = 256


def draw_seq_lengths(key, part):
    first_key = jax.random.fold_in(key, 11)
    second_key = jax.random.fold_in(key, 23)
    drawn_lengths = jax.random.randint(first_key, (NSEQ,), LMAX // 4, LMAX + 1)
    chosen = jax.random.randint(second_key, (), 0, NSEQ)
    return jnp.where(jnp.arange(NSEQ) == chosen, LMAX, drawn_lengths).astype(jnp.int32)


def draw_seq_order(key, part):
    experts_here = NFFN // EXP_DEV
    groups = NSEQ // (SEQ_DEV * experts_here)
    group_keys = jax.random.split(jax.random.fold_in(key, 37), groups * SEQ_DEV)

    def one_order(group_key):
        return jax.random.permutation(group_key, experts_here)
    orders = jax.vmap(one_order)(group_keys)
    slot_ids = jnp.arange(NSEQ, dtype=jnp.int32)
    place = slot_ids % SEQ_DEV
    column = slot_ids // SEQ_DEV % groups
    row_index = slot_ids // (SEQ_DEV * groups)
    target = orders[column * SEQ_DEV + place, row_index]
    return ((target * groups + column) * SEQ_DEV + place).astype(jnp.int32)


def level_of(key, dims, cuts, smallest, largest):
    gain, own = 1.0, jax.random.fold_in(key, 6)
    for axis_at, parts in cuts:
        steps = jnp.exp(jax.random.uniform(jax.random.fold_in(own, axis_at), (parts,), jnp.float32, smallest / len(cuts), largest / len(cuts)))
        gain = gain * jnp.repeat(steps, dims[axis_at] // parts).reshape([-1 if axis == axis_at else 1 for axis in range(len(dims))])
    return gain


def assign_block(rng, own, number, rows, count, top, reach, slope):
    order = jax.random.permutation(rng, count)
    crowded, ordinary = load_shares(count, rows * top, reach, slope, True), load_shares(count, rows * top, reach, slope, False)
    places = jnp.arange(count)

    def named(lengths, rotation):
        used = int((lengths > 0).sum())
        fixed = max(1, used // 4)
        passed = fixed + (places - fixed + rotation * (used - fixed)) % max(1, count - fixed)
        return jnp.zeros((count,), jnp.int32).at[order[jnp.where(places < fixed, places, passed)]].set(jnp.asarray(lengths, jnp.int32))

    lengths = jnp.where(number % 4 == 0, named(crowded, number // 4), named(ordinary, number - number // 4 - 1))
    mixed = jax.random.permutation(jax.random.fold_in(own, 3), count)
    giver, taker = mixed[0:count // 2 * 2:2], mixed[1:count // 2 * 2:2]
    slack = jnp.minimum(lengths[giver] - 1, reach - lengths[taker]) // 2
    slack = jnp.where((giver == order[0]) | (taker == order[0]) | (lengths[taker] == 0), 0, jnp.maximum(slack, 0))
    passed = jax.random.randint(jax.random.fold_in(own, 4), (count // 2,), 0, 1 << 20) % (slack + 1)
    lengths = lengths.at[giver].add(-passed).at[taker].add(passed)
    members = jnp.searchsorted(jnp.cumsum(lengths), jnp.arange(rows * top), side="right").astype(jnp.int32)
    table = members.reshape(top, rows).T
    table = table[jax.random.permutation(jax.random.fold_in(own, 1), rows)]
    rotation = jax.random.randint(jax.random.fold_in(own, 2), (rows, 1), 0, top)
    return jnp.take_along_axis(table, (jnp.arange(top)[None, :] + rotation) % top, axis=1)


def load_shares(count, total, most, slope, full):
    weights = [(1 << 20) // math.isqrt(standing ** slope) + 1 for standing in range(1, count + 1)]
    largest = most if full else min(most, max(-(-total // count), total * weights[0] // sum(weights)))
    least = 1 if total - largest >= count - 1 else 0
    counts, spare = [largest] + [least] * (count - 1), total - largest - least * (count - 1)
    while spare > 0:
        free = [i for i in range(1, count) if counts[i] < largest] or [i for i in range(1, count) if counts[i] < most]
        pool, budget = sum([weights[i] for i in free]), spare
        for i in free:
            more = min(most - counts[i], max(1, budget * weights[i] // pool), spare)
            counts[i] = counts[i] + more
            spare = spare - more
    return np.array(counts)


def centred(key, dims, width, limit, cuts=(), kind=jnp.bfloat16):
    loudness = level_of(key, dims, cuts, -0.22, 0.18) if cuts else 1.0
    entries = jax.random.normal(key, dims, jnp.float32) * width * loudness
    return jnp.minimum(jnp.maximum(entries, -limit), limit).astype(kind)


def setup_inputs(seed: int = 0) -> dict:
    key_list = jax.random.split(jax.random.key(seed), 20)
    hidden_in = centred(key_list[0], (NSEQ, LMAX, D), 1.0, 6.0, ((0, 32),))
    prev_logits = centred(key_list[1], (NSEQ, LMAX, NE), 1.0, 6.0, ((0, 32),))
    seq_lengths = draw_seq_lengths(jax.random.fold_in(key_list[19], 71), 0)
    seq_order = draw_seq_order(jax.random.fold_in(key_list[19], 71), 0)
    routes_keys = jax.random.split(jax.random.fold_in(key_list[4], 1), NSEQ * LMAX // (SEQ_DEV * LMAX))
    routes_turns = jax.random.permutation(jax.random.fold_in(key_list[4], 3), NSEQ * LMAX // (SEQ_DEV * LMAX))
    routes = jax.vmap(lambda own, number: assign_block(jax.random.fold_in(key_list[4], 2), own, number, SEQ_DEV * LMAX, NE, 2, CAP, 1))(routes_keys, routes_turns).reshape((NSEQ, LMAX, 2))
    w_query = centred(key_list[5], (D, D), D ** -0.5, 0.21875, ((1, 8),))
    w_key = centred(key_list[6], (D, D), D ** -0.5, 0.21875, ((1, 8),))
    w_value = centred(key_list[7], (D, D), D ** -0.5, 0.21875, ((1, 8),))
    w_output = centred(key_list[8], (D, D), (max(D // 64, 1)) ** -0.5, 1.75, ((0, 8),))
    gain_attn = jnp.clip(1.0 + 0.1 * jax.random.normal(key_list[9], (D,), jnp.float32), 0.5, 1.5).astype(jnp.bfloat16)
    gain_moe = jnp.clip(1.0 + 0.1 * jax.random.normal(key_list[10], (D,), jnp.float32), 0.5, 1.5).astype(jnp.bfloat16)
    w_router = centred(key_list[11], (D, NE), (4 * D) ** -0.5, 0.109375, ((0, 8),))
    w_gating = centred(key_list[12], (NE, NE), (4 * NE) ** -0.5, 1.0)
    w_const = centred(key_list[13], (D, 4), D ** -0.5, 0.21875, ((0, 8),))
    v_const = centred(key_list[14], (2, D), 1.0, 6.0, ((1, 8),))
    w_gate = centred(key_list[15], (NFFN, D, FF), D ** -0.5, 0.21875, ((0, 4), (2, 8)))
    w_up = centred(key_list[16], (NFFN, D, FF), D ** -0.5, 0.21875, ((0, 4), (2, 8)))
    w_down = centred(key_list[17], (NFFN, FF, D), (max(FF // 128, 1)) ** -0.5, 1.5, ((0, 4), (1, 8)))
    out_grad = centred(key_list[18], (NSEQ, LMAX, D), 1.0, 6.0, ((0, 32),))
    return {"hidden_in": hidden_in, "prev_logits": prev_logits, "seq_lengths": seq_lengths, "seq_order": seq_order, "routes": routes, "w_query": w_query, "w_key": w_key, "w_value": w_value, "w_output": w_output, "gain_attn": gain_attn, "gain_moe": gain_moe, "w_router": w_router, "w_gating": w_gating, "w_const": w_const, "v_const": v_const, "w_gate": w_gate, "w_up": w_up, "w_down": w_down, "out_grad": out_grad}


@jax.custom_vjp
def low(v):
    return lax.optimization_barrier(v.astype(jnp.bfloat16)).astype(jnp.float32)

@jax.custom_vjp
def low_back(v):
    return v

def low_keep(v):
    return (low(v), None)

def low_pass(kept, grad):
    return (grad,)

def back_keep(v):
    return (v, None)

def back_low(kept, grad):
    return (low(grad),)
low.defvjp(low_keep, low_pass)
low_back.defvjp(back_keep, back_low)
precise = lax.Precision.HIGHEST
norm_eps = 1e-05
rope_base = 10000.0
masked_score = -1e+30

def matmul(left_side, right_side):
    return jnp.dot(left_side, right_side, precision=precise, preferred_element_type=jnp.float32)

def rms_scale(values):
    return lax.rsqrt(lax.optimization_barrier(jnp.mean(values * values, axis=-1, keepdims=True)) + norm_eps)

def rope_tables(length, head_dim):
    half_dim = head_dim // 2
    inverse = rope_base ** (-(2.0 * jnp.arange(half_dim, dtype=jnp.float32)) / head_dim)
    angles = jnp.arange(length, dtype=jnp.float32)[:, None] * inverse[None, :]
    return (jnp.cos(angles), jnp.sin(angles))

def rotate(values, cosine, sine_table):
    half_dim = values.shape[-1] // 2
    front_half = values[..., :half_dim]
    back_half = values[..., half_dim:]
    cos_wide = cosine[:, None, :]
    sin_wide = sine_table[:, None, :]
    return jnp.concatenate([front_half * cos_wide - back_half * sin_wide, back_half * cos_wide + front_half * sin_wide], axis=-1)

def attend_sequence(packed):
    query_seq, key_seq, value_seq, seq_length = packed
    raw_scores = jnp.einsum('qhd,khd->hqk', query_seq, key_seq, precision=precise) * HD ** (-0.5)
    raw_scores = low_back(raw_scores)
    positions = jnp.arange(LMAX, dtype=jnp.int32)
    allowed = (positions[None, :] <= positions[:, None]) & (positions[None, :] < seq_length)
    masked = jnp.where(allowed[None], raw_scores, masked_score)
    weights = low(jax.nn.softmax(masked, axis=-1))
    return jnp.einsum('hqk,khd->qhd', weights, value_seq, precision=precise)

def expert_apply(packed):
    rows_in, gate_weight, up_weight, down_weight = packed
    gate_linear = low_back(matmul(rows_in, gate_weight))
    up_linear = low_back(matmul(rows_in, up_weight))
    inner_rows = low(jax.nn.silu(gate_linear) * up_linear)
    return low(low_back(matmul(inner_rows, down_weight)))

def slot_tables(routes):
    block_rows = SEQ_DEV * LMAX
    blocks = NSEQ // SEQ_DEV
    flat_routes = routes.reshape(blocks, 2 * block_rows)
    matches = (flat_routes[:, :, None] == jnp.arange(NFFN, dtype=jnp.int32)[None, None, :]).astype(jnp.int32)
    position = lax.optimization_barrier(jnp.sum((jnp.cumsum(matches, axis=1) - 1) * matches, axis=-1))
    is_expert = flat_routes < NFFN
    block_ids = jnp.arange(blocks, dtype=jnp.int32)[:, None]
    target = jnp.where(is_expert, (flat_routes * blocks + block_ids) * CAP + position, NFFN * blocks * CAP)
    route_ids = jnp.arange(2 * blocks * block_rows, dtype=jnp.int32)
    slot_route = jnp.full((NFFN * blocks * CAP,), -1, jnp.int32).at[target.reshape(-1)].set(route_ids, mode='drop')
    route_slot = jnp.where(is_expert, target, -1).reshape(-1)
    return (slot_route, route_slot)

def forward(float_args, seq_lengths, routes, slot_route, route_slot):
    hidden_in, prev_logits, w_query, w_key, w_value, w_output, gain_attn, gain_moe, w_router, w_gating, w_const, v_const, w_gate, w_up, w_down = float_args
    token_count = NSEQ * LMAX
    hidden = hidden_in.reshape(token_count, D)
    normed_one = low(hidden * rms_scale(hidden) * gain_attn)
    query_linear = low_back(matmul(normed_one, w_query))
    key_linear = low_back(matmul(normed_one, w_key))
    value_rows = low(low_back(matmul(normed_one, w_value)))
    cosine, sine_table = rope_tables(LMAX, HD)
    heads_shape = (NSEQ, LMAX, HEADS, HD)
    query_rot = low(rotate(query_linear.reshape(heads_shape), cosine, sine_table))
    key_rot = low(rotate(key_linear.reshape(heads_shape), cosine, sine_table))
    attended = lax.map(jax.checkpoint(attend_sequence), (query_rot, key_rot, value_rows.reshape(heads_shape), seq_lengths))
    attended = low(low_back(attended.reshape(token_count, D)))
    residual = hidden + low_back(matmul(attended, w_output))
    normed_two = residual * rms_scale(residual) * gain_moe
    logits = matmul(normed_two, w_router) + matmul(prev_logits.reshape(token_count, NE), w_gating)
    router_probs = jax.nn.softmax(logits, axis=-1)
    route_pairs = routes.reshape(token_count, 2)
    gate_values = jnp.take_along_axis(router_probs, route_pairs, axis=1)
    const_weights = jax.nn.softmax(matmul(normed_two, w_const).reshape(token_count, 2, 2), axis=-1)
    const_rows = const_weights[:, :, 0:1] * normed_two[:, None, :] + const_weights[:, :, 1:2] * v_const[None, :, :]
    sent_rows = low(normed_two)
    route_inputs = low_back(jnp.broadcast_to(sent_rows[:, None, :], (token_count, 2, D))).reshape(2 * token_count, D)
    slot_rows = slot_route.reshape(NFFN, -1)
    expert_inputs = jnp.where(slot_rows[:, :, None] >= 0, route_inputs[jnp.maximum(slot_rows, 0)], 0.0)
    expert_rows = lax.map(jax.checkpoint(expert_apply), (expert_inputs, w_gate, w_up, w_down)).reshape(-1, D)
    expert_part = jnp.where(route_slot[:, None] >= 0, expert_rows[jnp.maximum(route_slot, 0)], 0.0).reshape(token_count, 2, D)
    picked = route_pairs[:, :, None]
    route_out = expert_part + jnp.where(picked == NFFN + 1, normed_two[:, None, :], 0.0)
    route_out = route_out + jnp.where(picked == NFFN + 2, const_rows[:, 0:1, :], 0.0)
    route_out = route_out + jnp.where(picked == NFFN + 3, const_rows[:, 1:2, :], 0.0)
    mixed_out = residual + lax.optimization_barrier(jnp.sum(gate_values[:, :, None] * route_out, axis=1))
    return mixed_out.reshape(NSEQ, LMAX, D)

def reference(hidden_in, prev_logits, seq_lengths, seq_order, routes, w_query, w_key, w_value, w_output, gain_attn, gain_moe, w_router, w_gating, w_const, v_const, w_gate, w_up, w_down, out_grad):
    slot_route, route_slot = slot_tables(routes)
    inverse = jnp.zeros((NSEQ,), jnp.int32).at[seq_order].set(jnp.arange(NSEQ, dtype=jnp.int32))
    dealt_lengths = seq_lengths[seq_order]
    float_args = tuple((argument.astype(jnp.float32) for argument in (hidden_in[seq_order], prev_logits[seq_order], w_query, w_key, w_value, w_output, gain_attn, gain_moe, w_router, w_gating, w_const, v_const, w_gate, w_up, w_down)))

    def apply_layer(*arguments):
        return forward(arguments, dealt_lengths, routes, slot_route, route_slot)
    mixed_out, pullback = jax.vjp(apply_layer, *float_args)
    gradients = pullback(out_grad[seq_order].astype(jnp.float32))
    return (mixed_out.astype(jnp.bfloat16)[inverse], gradients[0][inverse], gradients[1][inverse], gradients[2], gradients[3], gradients[4], gradients[5], gradients[6], gradients[7], gradients[8], gradients[9], gradients[10], gradients[11], gradients[12], gradients[13], gradients[14])
```

```python
import jax
import jax.numpy as jnp
from jax import lax
from jax.experimental import pallas as pl
from jax.experimental.pallas import tpu as pltpu
from jax.sharding import PartitionSpec as P

HD = 64
CAP = 256
TB = 256
PAIR = 2 * HD
norm_eps = 1e-05
rope_base = 10000.0
masked_score = -1e30
f32 = jnp.float32
bf16 = jnp.bfloat16
i32 = jnp.int32


def nn(a, b):
    return lax.dot_general(a, b, (((1,), (0,)), ((), ())), preferred_element_type=f32)


def nt(a, b):
    return lax.dot_general(a, b, (((1,), (1,)), ((), ())), preferred_element_type=f32)


def tn(a, b):
    return lax.dot_general(a, b, (((0,), (0,)), ((), ())), preferred_element_type=f32)


def split2(x):
    high = x.astype(bf16)
    return high, (x - high.astype(f32)).astype(bf16)


def split3(x):
    high = x.astype(bf16)
    rest = x - high.astype(f32)
    mid = rest.astype(bf16)
    return high, mid, (rest - mid.astype(f32)).astype(bf16)


def call(kernel, grid, ins, outs, args, scratch=(), flops=0, nbytes=0, exps=0, vmem=48 << 20):
    return pl.pallas_call(
        kernel,
        grid=grid,
        in_specs=ins,
        out_specs=[o[2] for o in outs],
        out_shape=[jax.ShapeDtypeStruct(o[0], o[1]) for o in outs],
        scratch_shapes=list(scratch),
        compiler_params=pltpu.CompilerParams(
            dimension_semantics=("arbitrary",) * len(grid), vmem_limit_bytes=vmem
        ),
        cost_estimate=pl.CostEstimate(flops=flops, bytes_accessed=nbytes, transcendentals=exps),
    )(*args)


def whole(shape):
    zeros = (0,) * len(shape)
    return pl.BlockSpec(shape, lambda *_: zeros)


def lanes_of(shape):
    return lax.broadcasted_iota(i32, shape, len(shape) - 1)


def turn(values, cos_wide, sin_wide):
    first = lanes_of((1, PAIR)) % HD < HD // 2
    partner = jnp.where(first, pltpu.roll(values, PAIR - HD // 2, 1), pltpu.roll(values, HD // 2, 1))
    return values * cos_wide + partner * sin_wide


def qkv_kernel(hid_ref, gain_ref, w_ref, cos_ref, sin_ref, q_ref, k_ref, v_ref, n_ref):
    width = hid_ref.shape[1]
    hidden = hid_ref[...].astype(f32)
    scale = lax.rsqrt(jnp.mean(hidden * hidden, axis=-1, keepdims=True) + norm_eps)
    normed = (hidden * scale * gain_ref[...]).astype(bf16)
    n_ref[...] = normed
    cos_wide, sin_wide = cos_ref[...], sin_ref[...]
    for part, (out, factor) in enumerate(((q_ref, HD**-0.5), (k_ref, 1.0))):
        for at in range(0, width, PAIR):
            lin = nt(normed, w_ref[part, at : at + PAIR])
            out[:, at : at + PAIR] = (turn(lin, cos_wide, sin_wide) * factor).astype(bf16)
    v_ref[...] = nt(normed, w_ref[2]).astype(bf16)


def qkv_call(hidden, gain, weights, cos_wide, sin_wide):
    rows, width = hidden.shape
    row = pl.BlockSpec((TB, width), lambda i: (i, 0))
    tab = pl.BlockSpec((TB, PAIR), lambda i: (i, 0))
    return call(
        qkv_kernel,
        (rows // TB,),
        [row, whole((1, width)), whole(weights.shape), tab, tab],
        [((rows, width), bf16, row)] * 4,
        (hidden, gain, weights, cos_wide, sin_wide),
        flops=6 * rows * width * width,
        nbytes=10 * rows * width + 6 * width * width,
    )


def attend_kernel(len_ref, q_ref, k_ref, v_ref, o_ref, r_ref, e_ref):
    rows = q_ref.shape[0]
    live = len_ref[0]
    low_lanes = lanes_of((1, PAIR)) < HD
    keys = k_ref[...]
    nil = jnp.zeros_like(keys)
    key_heads = (jnp.where(low_lanes, keys, nil), jnp.where(low_lanes, nil, keys))
    value_t = v_ref[...].T
    zeros = jnp.zeros((HD, rows), bf16)
    ones = jnp.ones((HD, rows), bf16)
    value_heads = (
        jnp.concatenate([value_t[:HD], zeros, ones, zeros], axis=0),
        jnp.concatenate([zeros, value_t[HD:], zeros, ones], axis=0),
    )
    key_at = lax.broadcasted_iota(i32, (TB, TB), 0)
    causal = key_at <= lax.broadcasted_iota(i32, (TB, TB), 1)
    for i in range(rows // TB):
        query = q_ref[i * TB : (i + 1) * TB, :]
        total = jnp.zeros((2 * PAIR, TB), f32)
        for head in range(2):
            blocks = []
            for j in range(i + 1):
                score = nt(key_heads[head][j * TB : (j + 1) * TB], query)
                keep = None
                if j > 0:
                    keep = key_at < live - j * TB
                if j == i:
                    keep = causal if keep is None else keep & causal
                if keep is not None:
                    score = jnp.where(keep, score, masked_score)
                blocks.append(score)
            top = jnp.max(blocks[0], axis=0, keepdims=True)
            for block in blocks[1:]:
                top = jnp.maximum(top, jnp.max(block, axis=0, keepdims=True))
            for j, block in enumerate(blocks):
                expo = jnp.exp(block - top).astype(bf16)
                e_ref[0, head, i * (i + 1) // 2 + j] = expo
                total = total + nn(value_heads[head][:, j * TB : (j + 1) * TB], expo)
        recip = 1.0 / total[PAIR:]
        o_ref[i * TB : (i + 1) * TB, :] = (total[:PAIR] * recip).T.astype(bf16)
        r_ref[i * TB : (i + 1) * TB, :] = recip.T


def attend_call(live, query, key, value):
    rows, width = query.shape
    pairs = width // PAIR
    steps = rows // TB
    tiles = steps * (steps + 1) // 2
    col = pl.BlockSpec((rows, PAIR), lambda p: (0, p))
    expo = (1, 2, tiles, TB, TB)
    return call(
        attend_kernel,
        (pairs,),
        [pl.BlockSpec(memory_space=pltpu.SMEM), col, col, col],
        [
            ((rows, width), bf16, col),
            ((rows, width), f32, col),
            ((pairs,) + expo[1:], bf16, pl.BlockSpec(expo, lambda p: (p, 0, 0, 0, 0))),
        ],
        (live, query, key, value),
        flops=pairs * 2 * tiles * TB * TB * 4 * PAIR,
        nbytes=pairs * 2 * tiles * TB * TB * 2 + 12 * rows * width,
        exps=pairs * 2 * tiles * TB * TB,
    )


def attend_back_kernel(
    q_ref, k_ref, v_ref, e_ref, do_ref, att_ref, r_ref, cos_ref, sin_ref, dq_ref, dk_ref, dv_ref, dqt_ref
):
    rows = q_ref.shape[0]
    steps = rows // TB
    low_lanes = lanes_of((1, PAIR)) < HD

    def halves(x):
        nil = jnp.zeros_like(x)
        return jnp.where(low_lanes, x, nil), jnp.where(low_lanes, nil, x)

    scaled = do_ref[...].astype(f32) * r_ref[...]
    product_t = (scaled * att_ref[...].astype(f32)).T
    deltas = (
        jnp.sum(product_t[:HD], axis=0, keepdims=True),
        jnp.sum(product_t[HD:], axis=0, keepdims=True),
    )
    grad = scaled.astype(bf16)
    grad_heads = halves(grad)
    query_heads = halves(q_ref[...])
    value_heads = halves(v_ref[...])
    key_t = k_ref[...].T
    zeros = jnp.zeros((HD, rows), bf16)
    key_heads = (
        jnp.concatenate([key_t[:HD], zeros], axis=0),
        jnp.concatenate([zeros, key_t[HD:]], axis=0),
    )
    for j in range(steps):
        js = slice(j * TB, (j + 1) * TB)
        value_grad = jnp.zeros((TB, PAIR), f32)
        key_grad = jnp.zeros((TB, PAIR), f32)
        keys_t = jnp.concatenate([key_heads[0][:, js], key_heads[1][:, js]], axis=1)
        for i in range(j, steps):
            rs = slice(i * TB, (i + 1) * TB)
            tile = i * (i + 1) // 2 + j
            expos, scores = [], []
            for head in range(2):
                grad_prob = nt(value_heads[head][js], grad[rs])
                expo = e_ref[0, head, tile]
                expos.append(expo)
                scores.append(
                    (expo.astype(f32) * (grad_prob - deltas[head][:, rs])).astype(bf16)
                )
            value_grad = value_grad + nn(
                jnp.concatenate(expos, axis=1),
                jnp.concatenate([grad_heads[0][rs], grad_heads[1][rs]], axis=0),
            )
            key_grad = key_grad + nn(
                jnp.concatenate(scores, axis=1),
                jnp.concatenate([query_heads[0][rs], query_heads[1][rs]], axis=0),
            )
            add = nn(keys_t, jnp.concatenate(scores, axis=0))
            if j == 0:
                dqt_ref[:, rs] = add
            else:
                dqt_ref[:, rs] += add
        dv_ref[js, :] = value_grad.astype(bf16)
        dk_ref[js, :] = turn(key_grad, cos_ref[js, :], -sin_ref[js, :]).astype(bf16)
    query_grad = dqt_ref[...].T * (HD**-0.5)
    dq_ref[...] = turn(query_grad, cos_ref[...], -sin_ref[...]).astype(bf16)


def attend_back_call(query, key, value, expo, grad, attended, recip, cos_wide, sin_wide):
    rows, width = query.shape
    pairs, _, tiles = expo.shape[:3]
    col = pl.BlockSpec((rows, PAIR), lambda p: (0, p))
    tab = whole((rows, PAIR))
    e_spec = pl.BlockSpec((1,) + expo.shape[1:], lambda p: (p, 0, 0, 0, 0))
    return call(
        attend_back_kernel,
        (pairs,),
        [col, col, col, e_spec, col, col, col, tab, tab],
        [((rows, width), bf16, col)] * 3,
        (query, key, value, expo, grad, attended, recip, cos_wide, sin_wide),
        scratch=[pltpu.VMEM((PAIR, rows), f32)],
        flops=pairs * 2 * tiles * TB * TB * 8 * PAIR,
        nbytes=pairs * 2 * tiles * TB * TB * 2 + 22 * rows * width,
    )


def route_kernel(
    att_ref, hid_ref, grad_ref, wo_ref, gain_ref, sw_ref, prev_ref, gating_ref, rcol_ref, prow_ref,
    res_ref, info_ref, send_ref, nlow_ref, rg_ref,
):
    step = pl.program_id(0)
    rows = nlow_ref.shape[0]
    blocks = rows // TB
    choices = prev_ref.shape[1]

    @pl.when(step < blocks)
    def _():
        residual = hid_ref[...].astype(f32) + nn(att_ref[...], wo_ref[...])
        res_ref[...] = residual
        scale = lax.rsqrt(jnp.mean(residual * residual, axis=-1, keepdims=True) + norm_eps)
        normed = residual * scale * gain_ref[...]
        high, mid, low = split3(normed)
        small_weights = sw_ref[...]
        small = nn(high, small_weights) + nn(mid, small_weights) + nn(low, small_weights)
        logits = small + nn(prev_ref[...], gating_ref[...])
        lane = lanes_of(logits.shape)
        is_choice = lane < choices
        masked = jnp.where(is_choice, logits, masked_score)
        expo = jnp.exp(masked - jnp.max(masked, axis=-1, keepdims=True))
        probs = expo / jnp.sum(expo, axis=-1, keepdims=True)
        wide = small.shape[1]
        partner = jnp.where(lane % 2 == 0, pltpu.roll(small, wide - 1, 1), pltpu.roll(small, 1, 1))
        top = jnp.maximum(small, partner)
        own = jnp.exp(small - top)
        alpha = own / (own + jnp.exp(partner - top))
        gates = [
            jnp.sum(jnp.where(lane == rcol_ref[:, j : j + 1], probs, 0.0), axis=-1, keepdims=True)
            for j in range(2)
        ]
        info = jnp.where(is_choice, probs, alpha)
        for at, column in enumerate((gates[0], gates[1], scale)):
            info = jnp.where(lane == choices + 4 + at, column, info)
        info_ref[...] = info
        here = pl.ds(pl.multiple_of(step * TB, TB), TB)
        nlow_ref[here, :] = high
        grad = grad_ref[...].astype(f32)
        rg_ref[0, here, :] = (gates[0] * grad).astype(bf16)
        rg_ref[1, here, :] = (gates[1] * grad).astype(bf16)

    @pl.when(step >= blocks)
    def _():
        slot = (step - blocks) * CAP + lax.broadcasted_iota(i32, (CAP, rows), 0)
        hot = [jnp.where(prow_ref[j : j + 1, :] == slot, 1.0, 0.0).astype(bf16) for j in range(2)]
        send_ref[0, :CAP, :] = nn(hot[0] + hot[1], nlow_ref[...]).astype(bf16)
        send_ref[0, CAP:, :] = (nn(hot[0], rg_ref[0]) + nn(hot[1], rg_ref[1])).astype(bf16)


def route_call(attended, hidden, grad, w_out, gain, small_weights, prev, gating, rcols, prows, experts):
    rows, width = attended.shape
    blocks = rows // TB
    wide = small_weights.shape[1]

    def block(cols):
        return pl.BlockSpec((TB, cols), lambda i: (jnp.minimum(i, blocks - 1), 0))

    return call(
        route_kernel,
        (blocks + experts,),
        [
            block(width), block(width), block(width), whole(w_out.shape), whole(gain.shape),
            whole(small_weights.shape), block(prev.shape[1]), whole(gating.shape), block(2), whole(prows.shape),
        ],
        [
            ((rows, width), f32, block(width)),
            ((rows, wide), f32, block(wide)),
            (
                (experts, 2 * CAP, width),
                bf16,
                pl.BlockSpec((1, 2 * CAP, width), lambda i: (jnp.maximum(i - blocks, 0), 0, 0)),
            ),
        ],
        (attended, hidden, grad, w_out, gain, small_weights, prev, gating, rcols, prows),
        scratch=[pltpu.VMEM((rows, width), bf16), pltpu.VMEM((2, rows, width), bf16)],
        flops=2 * rows * width * width + 6 * experts * CAP * rows * width,
        nbytes=10 * rows * width + 2 * width * width + 4 * experts * CAP * width,
    )


def expert_kernel(x_ref, w_ref, y_ref, inner_ref, fa_ref, fb_ref, acc_ref):
    step = pl.program_id(0)
    rows = acc_ref.shape[0]
    rows_in = x_ref[...].reshape(rows, x_ref.shape[2])
    gate = nt(rows_in, w_ref[0, 0])
    up = nt(rows_in, w_ref[0, 1])
    sig = 1.0 / (1.0 + jnp.exp(-gate))
    act = gate * sig
    inner = (act * up).astype(bf16)
    inner_ref[0] = inner
    fa_ref[0] = (up * sig * (1.0 + gate * (1.0 - sig))).astype(bf16)
    fb_ref[0] = act.astype(bf16)
    out = nn(inner, w_ref[0, 2])

    @pl.when(step == 0)
    def _():
        acc_ref[...] = out

    @pl.when(step > 0)
    def _():
        acc_ref[...] += out

    @pl.when(step == pl.num_programs(0) - 1)
    def _():
        y_ref[...] = acc_ref[...].astype(bf16).reshape(y_ref.shape)


def expert_back_kernel(g_ref, w_ref, fa_ref, fb_ref, dx_ref, dgu_ref, acc_ref):
    step = pl.program_id(0)
    rows = acc_ref.shape[0]
    grad_in = g_ref[...].reshape(rows, g_ref.shape[2])
    grad_inner = nt(grad_in, w_ref[0, 2])
    grad_gate = (grad_inner * fa_ref[0].astype(f32)).astype(bf16)
    grad_up = (grad_inner * fb_ref[0].astype(f32)).astype(bf16)
    dgu_ref[0, 0] = grad_gate
    dgu_ref[0, 1] = grad_up
    out = nn(grad_gate, w_ref[0, 0]) + nn(grad_up, w_ref[0, 1])

    @pl.when(step == 0)
    def _():
        acc_ref[...] = out

    @pl.when(step > 0)
    def _():
        acc_ref[...] += out

    @pl.when(step == pl.num_programs(0) - 1)
    def _():
        dx_ref[...] = acc_ref[...].astype(bf16).reshape(dx_ref.shape)


def expert_weights_kernel(x_ref, g_ref, inner_ref, dgu_ref, dw_ref):
    rows = inner_ref.shape[1]
    rows_in = x_ref[...].reshape(rows, x_ref.shape[2])
    grad_in = g_ref[...].reshape(rows, g_ref.shape[2])
    dw_ref[0, 0] = tn(dgu_ref[0, 0], rows_in).astype(bf16)
    dw_ref[0, 1] = tn(dgu_ref[0, 1], rows_in).astype(bf16)
    dw_ref[0, 2] = tn(inner_ref[0], grad_in).astype(bf16)


def expert_specs(sent, weights):
    experts, _, width = sent.shape
    chunks, _, units, _ = weights.shape
    rows = experts * CAP
    return dict(
        rows=rows,
        x=pl.BlockSpec((experts, CAP, width), lambda c: (0, 0, 0)),
        g=pl.BlockSpec((experts, CAP, width), lambda c: (0, 1, 0)),
        w=pl.BlockSpec((1, 3, units, width), lambda c: (c, 0, 0, 0)),
        unit=pl.BlockSpec((1, rows, units), lambda c: (c, 0, 0)),
        pair=pl.BlockSpec((1, 2, rows, units), lambda c: (c, 0, 0, 0)),
        flops=6 * rows * width * chunks * units,
        nbytes=6 * chunks * units * (rows + width) + 4 * rows * width,
    )


def expert_call(sent, weights):
    s = expert_specs(sent, weights)
    chunks, _, units, width = weights.shape
    rows = s["rows"]
    hidden = ((chunks, rows, units), bf16, s["unit"])
    return call(
        expert_kernel,
        (chunks,),
        [s["x"], s["w"]],
        [((sent.shape[0], CAP, width), bf16, s["x"]), hidden, hidden, hidden],
        (sent, weights),
        scratch=[pltpu.VMEM((rows, width), f32)],
        flops=s["flops"],
        nbytes=s["nbytes"],
        exps=rows * chunks * units,
    )


def expert_back_call(sent, weights, factor_a, factor_b):
    s = expert_specs(sent, weights)
    chunks, _, units, width = weights.shape
    rows = s["rows"]
    return call(
        expert_back_kernel,
        (chunks,),
        [s["g"], s["w"], s["unit"], s["unit"]],
        [
            ((sent.shape[0], CAP, width), bf16, s["x"]),
            ((chunks, 2, rows, units), bf16, s["pair"]),
        ],
        (sent, weights, factor_a, factor_b),
        scratch=[pltpu.VMEM((rows, width), f32)],
        flops=s["flops"],
        nbytes=s["nbytes"],
    )


def expert_weights_call(sent, inner, dgu, weights_shape):
    chunks, _, units, width = weights_shape
    s = expert_specs(sent, jax.ShapeDtypeStruct(weights_shape, bf16))
    return call(
        expert_weights_kernel,
        (chunks,),
        [s["x"], s["g"], s["unit"], s["pair"]],
        [(weights_shape, bf16, s["w"])],
        (sent, sent, inner, dgu),
        flops=s["flops"],
        nbytes=s["nbytes"],
    )[0]


def combine_kernel(
    y_ref, res_ref, info_ref, rcol_ref, pcol_ref, grad_ref, gain_ref, vec_ref, sw_ref, prev_ref, gt_ref,
    out_ref, part_ref, gprev_ref, gsw_ref, gvec_ref, ggat_ref,
):
    step = pl.program_id(0)
    choices = prev_ref.shape[1]
    experts = y_ref.shape[0]
    slots = experts * CAP
    rows_out = y_ref[...].reshape(slots, y_ref.shape[2])
    residual = res_ref[...]
    info = info_ref[...]
    lane = lanes_of(info.shape)

    def column(at):
        return info[:, at : at + 1]

    gates = (column(choices + 4), column(choices + 5))
    normed = residual * column(choices + 6) * gain_ref[...]
    grad = grad_ref[...].astype(f32)
    vectors = (vec_ref[0:1, :], vec_ref[1:2, :])
    alphas = ((column(choices), column(choices + 1)), (column(choices + 2), column(choices + 3)))
    dot_normed = jnp.sum(grad * normed, axis=-1, keepdims=True)
    dot_vectors = [jnp.sum(grad * v, axis=-1, keepdims=True) for v in vectors]
    mixed = residual
    weight_normed = jnp.zeros_like(dot_normed)
    weight_copy = jnp.zeros_like(dot_normed)
    weight_const = [jnp.zeros_like(dot_normed), jnp.zeros_like(dot_normed)]
    grad_probs = jnp.zeros_like(info)
    slot = lanes_of((TB, slots))
    for j in range(2):
        route = rcol_ref[:, j : j + 1]
        hot = jnp.where(pcol_ref[:, j : j + 1] == slot, 1.0, 0.0).astype(bf16)
        rows_j = nn(hot, rows_out)
        is_copy = jnp.where(route == experts + 1, 1.0, 0.0)
        is_const = [jnp.where(route == experts + 2 + c, 1.0, 0.0) for c in range(2)]
        on_normed = is_copy + is_const[0] * alphas[0][0] + is_const[1] * alphas[1][0]
        grad_gate = jnp.sum(grad * rows_j, axis=-1, keepdims=True) + on_normed * dot_normed
        for c in range(2):
            grad_gate = grad_gate + is_const[c] * alphas[c][1] * dot_vectors[c]
            weight_const[c] = weight_const[c] + gates[j] * is_const[c]
        grad_probs = grad_probs + jnp.where(lane == route, grad_gate, 0.0)
        mixed = mixed + gates[j] * rows_j
        weight_normed = weight_normed + gates[j] * on_normed
        weight_copy = weight_copy + gates[j] * is_copy
    mixed = mixed + weight_normed * normed
    for c in range(2):
        mixed = mixed + weight_const[c] * alphas[c][1] * vectors[c]
    out_ref[...] = mixed.astype(bf16)
    is_choice = lane < choices
    probs = jnp.where(is_choice, info, 0.0)
    grad_small = probs * (grad_probs - jnp.sum(probs * grad_probs, axis=-1, keepdims=True))
    direct = weight_copy
    coefs = jnp.zeros_like(info)
    for c in range(2):
        grad_alpha = (weight_const[c] * dot_normed, weight_const[c] * dot_vectors[c])
        mean = alphas[c][0] * grad_alpha[0] + alphas[c][1] * grad_alpha[1]
        for k in range(2):
            grad_small = jnp.where(
                lane == choices + 2 * c + k, alphas[c][k] * (grad_alpha[k] - mean), grad_small
            )
        direct = direct + alphas[c][0] * weight_const[c]
        coefs = jnp.where(lane == c, alphas[c][1] * weight_const[c], coefs)
    high, mid, low = split3(grad_small)
    small_weights = sw_ref[...]
    part_ref[...] = direct * grad + (
        nt(high, small_weights) + nt(mid, small_weights) + nt(low, small_weights)
    )
    gating_t = gt_ref[...]
    logits_high, logits_mid, logits_low = split3(jnp.where(is_choice, grad_small, 0.0))
    grad_prev = nn(logits_high, gating_t) + nn(logits_mid, gating_t) + nn(logits_low, gating_t)
    gprev_ref[...] = grad_prev[:, :choices]
    normed_high, normed_mid = split2(normed)
    grad_sw = tn(high, normed_high) + tn(mid, normed_high) + tn(high, normed_mid)
    coef_high, coef_mid = split2(coefs)
    grad_vec = tn(coef_high, grad_ref[...]) + tn(coef_mid, grad_ref[...])
    prev = prev_ref[...]
    grad_gating = tn(prev, high) + tn(prev, mid) + tn(prev, low)

    @pl.when(step == 0)
    def _():
        gsw_ref[...] = grad_sw
        gvec_ref[...] = grad_vec
        ggat_ref[...] = grad_gating

    @pl.when(step > 0)
    def _():
        gsw_ref[...] += grad_sw
        gvec_ref[...] += grad_vec
        ggat_ref[...] += grad_gating


def combine_call(back, residual, info, rcols, pcols, grad, gain, vectors, small_weights, prev, gating_t):
    rows, width = residual.shape
    wide = info.shape[1]
    choices = prev.shape[1]
    slots = back.shape[0] * CAP

    def block(cols):
        return pl.BlockSpec((TB, cols), lambda i: (i, 0))

    return call(
        combine_kernel,
        (rows // TB,),
        [
            whole(back.shape), block(width), block(wide), block(2), block(2), block(width), whole(gain.shape),
            whole(vectors.shape), whole(small_weights.shape), block(choices), whole(gating_t.shape),
        ],
        [
            ((rows, width), bf16, block(width)),
            ((rows, width), f32, block(width)),
            ((rows, choices), f32, block(choices)),
            ((wide, width), f32, whole((wide, width))),
            ((wide, width), f32, whole((wide, width))),
            ((choices, wide), f32, whole((choices, wide))),
        ],
        (back, residual, info, rcols, pcols, grad, gain, vectors, small_weights, prev, gating_t),
        flops=4 * slots * rows * width,
        nbytes=14 * rows * width + 2 * slots * width,
    )


def residual_kernel(
    dx_ref, part_ref, res_ref, info_ref, pcol_ref, grad_ref, gain_ref, wo_ref, att_ref,
    gres_ref, gatt_ref, gwo_ref, ggain_ref, acc_ref,
):
    step = pl.program_id(0)
    experts = dx_ref.shape[0]
    slots = experts * CAP
    scale_at = info_ref.shape[1]
    del scale_at
    slot = lanes_of((TB, slots))
    hot = jnp.where(
        (pcol_ref[:, 0:1] == slot) | (pcol_ref[:, 1:2] == slot), 1.0, 0.0
    ).astype(bf16)
    grad_normed = part_ref[...] + nn(hot, dx_ref[...].reshape(slots, dx_ref.shape[2]))
    residual = res_ref[...]
    scale = lax.rsqrt(jnp.mean(residual * residual, axis=-1, keepdims=True) + norm_eps)
    unit = residual * scale
    grad_gain = jnp.sum(grad_normed * unit, axis=0, keepdims=True)
    scaled = grad_normed * gain_ref[...]
    grad_residual = grad_ref[...].astype(f32) + scale * (
        scaled - unit * jnp.mean(scaled * unit, axis=-1, keepdims=True)
    )
    gres_ref[...] = grad_residual
    low = grad_residual.astype(bf16)
    gatt_ref[...] = nt(low, wo_ref[...]).astype(bf16)
    grad_out = tn(att_ref[...], low)

    @pl.when(step == 0)
    def _():
        acc_ref[...] = grad_out
        ggain_ref[...] = grad_gain

    @pl.when(step > 0)
    def _():
        acc_ref[...] += grad_out
        ggain_ref[...] += grad_gain

    @pl.when(step == pl.num_programs(0) - 1)
    def _():
        gwo_ref[...] = acc_ref[...].astype(bf16)


def residual_call(dx, part, residual, info, pcols, grad, gain, w_out, attended):
    rows, width = residual.shape
    wide = info.shape[1]
    slots = dx.shape[0] * CAP

    def block(cols):
        return pl.BlockSpec((TB, cols), lambda i: (i, 0))

    return call(
        residual_kernel,
        (rows // TB,),
        [
            whole(dx.shape), block(width), block(width), block(wide), block(2), block(width), whole(gain.shape),
            whole(w_out.shape), block(width),
        ],
        [
            ((rows, width), f32, block(width)),
            ((rows, width), bf16, block(width)),
            ((width, width), bf16, whole((width, width))),
            ((1, width), f32, whole((1, width))),
        ],
        (dx, part, residual, info, pcols, grad, gain, w_out, attended),
        scratch=[pltpu.VMEM((width, width), f32)],
        flops=2 * slots * rows * width + 4 * rows * width * width,
        nbytes=18 * rows * width + 2 * slots * width,
    )


def qkv_weights_kernel(dq_ref, dk_ref, dv_ref, n_ref, out_ref):
    normed = n_ref[...]
    for part, ref in enumerate((dq_ref, dk_ref, dv_ref)):
        out_ref[part] = tn(ref[...], normed).astype(bf16)


def qkv_weights_call(dq, dk, dv, normed):
    rows, width = normed.shape
    col = pl.BlockSpec((rows, 256), lambda c: (0, c))
    return call(
        qkv_weights_kernel,
        (width // 256,),
        [col, col, col, whole((rows, width))],
        [((3, width, width), bf16, pl.BlockSpec((3, 256, width), lambda c: (0, c, 0)))],
        (dq, dk, dv, normed),
        flops=6 * rows * width * width,
        nbytes=8 * rows * width + 6 * width * width,
    )[0]


def hidden_kernel(dq_ref, dk_ref, dv_ref, w_ref, hid_ref, gain_ref, gres_ref, out_ref, ggain_ref):
    step = pl.program_id(0)
    grad_normed = nn(dq_ref[...], w_ref[0]) + nn(dk_ref[...], w_ref[1]) + nn(dv_ref[...], w_ref[2])
    hidden = hid_ref[...].astype(f32)
    scale = lax.rsqrt(jnp.mean(hidden * hidden, axis=-1, keepdims=True) + norm_eps)
    unit = hidden * scale
    grad_gain = jnp.sum(grad_normed * unit, axis=0, keepdims=True)
    scaled = grad_normed * gain_ref[...]
    out_ref[...] = gres_ref[...] + scale * (
        scaled - unit * jnp.mean(scaled * unit, axis=-1, keepdims=True)
    )

    @pl.when(step == 0)
    def _():
        ggain_ref[...] = grad_gain

    @pl.when(step > 0)
    def _():
        ggain_ref[...] += grad_gain


def hidden_call(dq, dk, dv, weights, hidden, gain, grad_residual):
    rows, width = hidden.shape
    row = pl.BlockSpec((TB, width), lambda i: (i, 0))
    return call(
        hidden_kernel,
        (rows // TB,),
        [row, row, row, whole(weights.shape), row, whole(gain.shape), row],
        [((rows, width), f32, row), ((1, width), f32, whole((1, width)))],
        (dq, dk, dv, weights, hidden, gain, grad_residual),
        flops=6 * rows * width * width,
        nbytes=16 * rows * width + 6 * width * width,
    )


def rope_wide(length):
    inverse = rope_base ** (-(2.0 * jnp.arange(HD // 2, dtype=f32)) / HD)
    angles = jnp.arange(length, dtype=f32)[:, None] * inverse[None, :]
    cosine, sine = jnp.cos(angles), jnp.sin(angles)
    return (
        jnp.concatenate([cosine] * 4, axis=1),
        jnp.concatenate([-sine, sine, -sine, sine], axis=1),
    )


def to_rows(flat, width):
    count = -(-flat.shape[1] // width)
    return jnp.pad(flat, ((0, 0), (0, count * width - flat.shape[1]))).reshape(
        flat.shape[0], count, width
    )


def per_device(
    hidden_in,
    prev_logits,
    seq_lengths,
    seq_order,
    routes,
    w_query,
    w_key,
    w_value,
    w_output,
    gain_attn,
    gain_moe,
    w_router,
    w_gating,
    w_const,
    v_const,
    w_gate,
    w_up,
    w_down,
    out_grad,
):
    rows, width = hidden_in.shape[1:]
    experts = lax.axis_size("expert")
    shards = lax.axis_size("fsdp")
    choices = w_router.shape[1]
    part = width // shards
    hidden = hidden_in.reshape(rows, width)
    grad = out_grad.reshape(rows, width)
    prev = prev_logits.reshape(rows, choices)

    fsdp_here = lax.axis_index("fsdp")
    own = lax.axis_index("expert") * shards + fsdp_here
    live = lax.dynamic_slice(seq_lengths, (own,), (1,))
    dealt = lax.all_gather(routes.reshape(rows, 2).T, "expert", axis=0, tiled=False)
    peers = jnp.arange(experts, dtype=i32) * shards + fsdp_here
    mine = seq_order[peers] == own
    route_rows = jnp.sum(jnp.where(mine[:, None, None], dealt, 0), axis=0)
    ids = jnp.arange(experts, dtype=i32)
    named = (route_rows[0][None, :] == ids[:, None]) | (route_rows[1][None, :] == ids[:, None])
    at = jnp.arange(rows, dtype=i32)
    earlier = (at[:, None] < at[None, :]).astype(bf16)
    counts = nn(named.astype(bf16), earlier).astype(i32)
    place_rows = jnp.stack(
        [
            jnp.where(
                r < experts,
                r * CAP + jnp.sum(jnp.where(r[None, :] == ids[:, None], counts, 0), axis=0),
                -1,
            )
            for r in (route_rows[0], route_rows[1])
        ]
    )
    route_cols = route_rows.T
    place_cols = place_rows.T
    cos_wide, sin_wide = rope_wide(rows)

    small_parts = jnp.concatenate(
        [gain_attn[:, None], gain_moe[:, None], w_router, w_const, v_const.T], axis=1
    )
    small_count = small_parts.shape[1]
    small_rows = to_rows(small_parts.T.reshape(1, -1), width)[0]
    first_pack = jnp.concatenate([w_query.T, w_key.T, w_value.T, small_rows], axis=0)
    first = lax.all_gather(first_pack, "fsdp", axis=0, tiled=False)
    w_out = lax.all_gather(w_output, "fsdp", axis=0, tiled=True)
    expert_pack = jnp.stack([w_gate[0].T, w_up[0].T, w_down[0]])
    expert_weights = lax.all_gather(expert_pack, "fsdp", axis=0, tiled=False)

    qkv_weights = (
        first[:, : 3 * part].reshape(shards, 3, part, width).transpose(1, 0, 2, 3).reshape(3, width, width)
    )
    small = (
        first[:, 3 * part :]
        .reshape(shards, -1)[:, : small_count * part]
        .reshape(shards, small_count, part)
        .transpose(1, 0, 2)
        .reshape(small_count, width)
    )
    gain_one = small[0:1].astype(f32)
    gain_two = small[1:2].astype(f32)
    small_weights = jnp.pad(small[2 : choices + 6].T, ((0, 0), (0, 128 - choices - 4)))
    vectors = small[choices + 6 :].astype(f32)
    gating_wide = jnp.pad(w_gating, ((0, 0), (0, 128 - choices)))
    gating_t = jnp.pad(w_gating.T, ((0, 128 - choices), (0, 128 - choices)))

    query, key, value, normed_one = qkv_call(hidden, gain_one, qkv_weights, cos_wide, sin_wide)
    attended, recip, expo = attend_call(live, query, key, value)
    residual, info, send = route_call(
        attended, hidden, grad, w_out, gain_two, small_weights, prev, gating_wide, route_cols, place_rows, experts
    )
    sent = lax.all_to_all(send, "expert", split_axis=0, concat_axis=0, tiled=True)
    expert_out, inner, factor_a, factor_b = expert_call(sent, expert_weights)
    returned = lax.all_to_all(expert_out, "expert", split_axis=0, concat_axis=0, tiled=True)
    expert_dx, dgu = expert_back_call(sent, expert_weights, factor_a, factor_b)
    returned_dx = lax.all_to_all(expert_dx, "expert", split_axis=0, concat_axis=0, tiled=True)
    expert_dw = expert_weights_call(sent, inner, dgu, expert_weights.shape)
    expert_sum = lax.psum_scatter(expert_dw, "fsdp", scatter_dimension=0, tiled=False)

    hidden_out, part_grad, grad_prev, grad_sw, grad_vec, grad_gating = combine_call(
        returned, residual, info, route_cols, place_cols, grad, gain_two, vectors, small_weights, prev, gating_t
    )
    grad_residual, grad_attended, grad_wo, grad_gain_two = residual_call(
        returned_dx, part_grad, residual, info, place_cols, grad, gain_two, w_out, attended
    )
    dq, dk, dv = attend_back_call(
        query, key, value, expo, grad_attended, attended, recip, cos_wide, sin_wide
    )
    grad_qkv = qkv_weights_call(dq, dk, dv, normed_one)
    grad_hidden, grad_gain_one = hidden_call(
        dq, dk, dv, qkv_weights, hidden, gain_one, grad_residual
    )

    small_grads = jnp.concatenate(
        [grad_gain_one, grad_gain_two, grad_sw[: choices + 4], grad_vec[:2]], axis=0
    )
    small_flat = small_grads.reshape(small_count, shards, part).transpose(1, 0, 2).reshape(shards, -1)
    gating_flat = grad_gating[:, :choices].reshape(1, -1)
    gating_high = gating_flat.astype(bf16)
    gating_low = (gating_flat - gating_high.astype(f32)).astype(bf16)
    gating_both = jnp.concatenate([gating_high, gating_low], axis=1)
    flat = jnp.concatenate(
        [small_flat.astype(bf16), jnp.broadcast_to(gating_both, (shards, gating_both.shape[1]))], axis=1
    )
    shared = jnp.concatenate(
        [
            grad_qkv.reshape(3, shards, part, width).transpose(1, 0, 2, 3).reshape(shards, 3 * part, width),
            grad_wo.reshape(shards, part, width),
            to_rows(flat, width),
        ],
        axis=1,
    )
    scattered = lax.psum_scatter(shared, "fsdp", scatter_dimension=0, tiled=False)
    total = lax.psum(scattered, "expert").astype(f32)
    flat_total = total[4 * part :].reshape(-1)
    small_total = flat_total[: small_count * part].reshape(small_count, part)
    gating_at = small_count * part
    pair_total = flat_total[gating_at : gating_at + 2 * choices * choices].reshape(2, choices, choices)
    expert_total = expert_sum.astype(f32)
    return (
        hidden_out[None],
        grad_hidden[None],
        grad_prev[None],
        total[:part].T,
        total[part : 2 * part].T,
        total[2 * part : 3 * part].T,
        total[3 * part : 4 * part],
        small_total[0],
        small_total[1],
        small_total[2 : choices + 2].T,
        pair_total[0] + pair_total[1],
        small_total[choices + 2 : choices + 6].T,
        small_total[choices + 6 :],
        expert_total[0].T[None],
        expert_total[1].T[None],
        expert_total[2][None],
    )


def solution(mesh):
    rows = P(("expert", "fsdp"), None, None)
    ins = (
        rows, rows, P(), P(), rows,
        P(None, "fsdp"), P(None, "fsdp"), P(None, "fsdp"), P("fsdp", None),
        P("fsdp"), P("fsdp"), P("fsdp", None), P(), P("fsdp", None), P(None, "fsdp"),
        P("expert", None, "fsdp"), P("expert", None, "fsdp"), P("expert", "fsdp", None), rows,
    )
    outs = (
        rows, rows, rows,
        P(None, "fsdp"), P(None, "fsdp"), P(None, "fsdp"), P("fsdp", None),
        P("fsdp"), P("fsdp"), P("fsdp", None), P(), P("fsdp", None), P(None, "fsdp"),
        P("expert", None, "fsdp"), P("expert", None, "fsdp"), P("expert", "fsdp", None),
    )
    return jax.shard_map(per_device, mesh=mesh, in_specs=ins, out_specs=outs, check_vma=False)
```

```python
import functools

import jax
import jax.numpy as jnp
from jax import lax
from jax.experimental import pallas as pl
from jax.experimental.pallas import tpu as pltpu
from jax.sharding import PartitionSpec as P

HD = 64
CAP = 256
TB = 256
PAIR = 2 * HD
WIDE = 128
norm_eps = 1e-05
rope_base = 10000.0
masked_score = -1e30
f32 = jnp.float32
bf16 = jnp.bfloat16
i32 = jnp.int32


def nn(a, b):
    return lax.dot_general(a, b, (((1,), (0,)), ((), ())), preferred_element_type=f32)


def nt(a, b):
    return lax.dot_general(a, b, (((1,), (1,)), ((), ())), preferred_element_type=f32)


def tn(a, b):
    return lax.dot_general(a, b, (((0,), (0,)), ((), ())), preferred_element_type=f32)


def split2(x):
    high = x.astype(bf16)
    return high, (x - high.astype(f32)).astype(bf16)


def split3(x):
    high = x.astype(bf16)
    rest = x - high.astype(f32)
    mid = rest.astype(bf16)
    return high, mid, (rest - mid.astype(f32)).astype(bf16)


def call(kernel, grid, ins, outs, args, scratch=(), flops=0, nbytes=0, exps=0, vmem=48 << 20):
    return pl.pallas_call(
        kernel,
        grid=grid,
        in_specs=ins,
        out_specs=[o[2] for o in outs],
        out_shape=[jax.ShapeDtypeStruct(o[0], o[1]) for o in outs],
        scratch_shapes=list(scratch),
        compiler_params=pltpu.CompilerParams(
            dimension_semantics=("arbitrary",) * len(grid), vmem_limit_bytes=vmem
        ),
        cost_estimate=pl.CostEstimate(flops=flops, bytes_accessed=nbytes, transcendentals=exps),
    )(*args)


def whole(shape):
    zeros = (0,) * len(shape)
    return pl.BlockSpec(shape, lambda *_: zeros)


def lanes_of(shape):
    return lax.broadcasted_iota(i32, shape, len(shape) - 1)


def turn(values, cos_wide, sin_wide):
    first = lanes_of((1, PAIR)) % HD < HD // 2
    partner = jnp.where(first, pltpu.roll(values, PAIR - HD // 2, 1), pltpu.roll(values, HD // 2, 1))
    return values * cos_wide + partner * sin_wide


def qkv_rows(hid_ref, gain, w_ref, cos_ref, sin_ref, q_ref, k_ref, v_ref, n_ref):
    width = hid_ref.shape[1]
    hidden = hid_ref[...].astype(f32)
    scale = lax.rsqrt(jnp.mean(hidden * hidden, axis=-1, keepdims=True) + norm_eps)
    normed = (hidden * scale * gain).astype(bf16)
    n_ref[...] = normed
    cos_wide, sin_wide = cos_ref[...], sin_ref[...]
    for part, (out, factor) in enumerate(((q_ref, HD**-0.5), (k_ref, 1.0))):
        for at in range(0, width, PAIR):
            lin = nt(normed, w_ref[part, at : at + PAIR])
            out[:, at : at + PAIR] = (turn(lin, cos_wide, sin_wide) * factor).astype(bf16)
    v_ref[...] = nt(normed, w_ref[2]).astype(bf16)


def qkv_kernel(gain_at, hid_ref, small_ref, w_ref, *refs):
    gain = small_ref[gain_at : gain_at + 1, :].astype(f32)
    qkv_rows(hid_ref, gain, w_ref, *refs)


def qkv_pieces_kernel(gain_at, part, where_ref, hid_ref, cos_ref, sin_ref, *refs):
    pieces, (q_ref, k_ref, v_ref, n_ref, w_ref, small_ref, vec_ref) = refs[:-7], refs[-7:]
    count = len(pieces) // 2
    half = part // 2
    vectors = pieces[0].shape[0] - 3 * half

    @pl.when(pl.program_id(0) == 0)
    def _():
        vec_ref[...] = jnp.zeros_like(vec_ref)
        core = where_ref[count]
        for own in range(2):
            side = core if own == 0 else 1 - core
            total = None
            for r in range(count):
                ref = pieces[own * count + r]
                shard = where_ref[r]
                for at in range(3):
                    row = pl.multiple_of(shard * part + side * half, 16)
                    w_ref[at, pl.ds(row, half), :] = ref[at * half : (at + 1) * half, :]
                moved = pltpu.roll(ref[3 * half :, :].astype(f32), shard * part, 1)
                total = moved if total is None else total + moved
            vec_ref[pl.ds(pl.multiple_of(side * vectors, 8), vectors), :] = total
        small_ref[...] = vec_ref[...].astype(bf16)

    gain = small_ref[gain_at : gain_at + 1, :].astype(f32)
    qkv_rows(hid_ref, gain, w_ref, cos_ref, sin_ref, q_ref, k_ref, v_ref, n_ref)


def qkv_specs(hidden):
    rows, width = hidden.shape
    row = pl.BlockSpec((TB, width), lambda i: (i, 0))
    return dict(
        row=row,
        tab=pl.BlockSpec((TB, PAIR), lambda i: (i, 0)),
        outs=[((rows, width), bf16, row)] * 4,
        flops=6 * rows * width * width,
        nbytes=10 * rows * width + 6 * width * width,
    )


def qkv_call(hidden, small, gain_at, weights, cos_wide, sin_wide):
    s = qkv_specs(hidden)
    return call(
        functools.partial(qkv_kernel, gain_at),
        (hidden.shape[0] // TB,),
        [s["row"], whole(small.shape), whole(weights.shape), s["tab"], s["tab"]],
        s["outs"],
        (hidden, small, weights, cos_wide, sin_wide),
        flops=s["flops"],
        nbytes=s["nbytes"],
    )


def qkv_pieces_call(hidden, where, own, other, gain_at, part, cos_wide, sin_wide):
    s = qkv_specs(hidden)
    width = hidden.shape[1]
    pieces = list(own) + list(other)
    return call(
        functools.partial(qkv_pieces_kernel, gain_at, part),
        (hidden.shape[0] // TB,),
        [pl.BlockSpec(memory_space=pltpu.SMEM), s["row"], s["tab"], s["tab"]]
        + [whole(piece.shape) for piece in pieces],
        s["outs"]
        + [
            ((3, width, width), bf16, whole((3, width, width))),
            ((WIDE, width), bf16, whole((WIDE, width))),
        ],
        (where, hidden, cos_wide, sin_wide, *pieces),
        scratch=[pltpu.VMEM((WIDE, width), f32)],
        flops=s["flops"],
        nbytes=s["nbytes"],
    )


def attend_kernel(len_ref, q_ref, k_ref, v_ref, o_ref, r_ref, e_ref):
    rows = q_ref.shape[0]
    live = len_ref[0]
    low_lanes = lanes_of((1, PAIR)) < HD
    keys = k_ref[...]
    nil = jnp.zeros_like(keys)
    key_heads = (jnp.where(low_lanes, keys, nil), jnp.where(low_lanes, nil, keys))
    value_t = v_ref[...].T
    zeros = jnp.zeros((HD, rows), bf16)
    ones = jnp.ones((HD, rows), bf16)
    value_heads = (
        jnp.concatenate([value_t[:HD], zeros, ones, zeros], axis=0),
        jnp.concatenate([zeros, value_t[HD:], zeros, ones], axis=0),
    )
    key_at = lax.broadcasted_iota(i32, (TB, TB), 0)
    causal = key_at <= lax.broadcasted_iota(i32, (TB, TB), 1)
    for i in range(rows // TB):
        query = q_ref[i * TB : (i + 1) * TB, :]
        total = jnp.zeros((2 * PAIR, TB), f32)
        for head in range(2):
            blocks = []
            for j in range(i + 1):
                score = nt(key_heads[head][j * TB : (j + 1) * TB], query)
                keep = None
                if j > 0:
                    keep = key_at < live - j * TB
                if j == i:
                    keep = causal if keep is None else keep & causal
                if keep is not None:
                    score = jnp.where(keep, score, masked_score)
                blocks.append(score)
            top = jnp.max(blocks[0], axis=0, keepdims=True)
            for block in blocks[1:]:
                top = jnp.maximum(top, jnp.max(block, axis=0, keepdims=True))
            for j, block in enumerate(blocks):
                expo = jnp.exp(block - top).astype(bf16)
                e_ref[0, head, i * (i + 1) // 2 + j] = expo
                total = total + nn(value_heads[head][:, j * TB : (j + 1) * TB], expo)
        recip = 1.0 / total[PAIR:]
        o_ref[i * TB : (i + 1) * TB, :] = (total[:PAIR] * recip).T.astype(bf16)
        r_ref[i * TB : (i + 1) * TB, :] = recip.T


def attend_call(live, query, key, value):
    rows, width = query.shape
    pairs = width // PAIR
    steps = rows // TB
    tiles = steps * (steps + 1) // 2
    col = pl.BlockSpec((rows, PAIR), lambda p: (0, p))
    expo = (1, 2, tiles, TB, TB)
    return call(
        attend_kernel,
        (pairs,),
        [pl.BlockSpec(memory_space=pltpu.SMEM), col, col, col],
        [
            ((rows, width), bf16, col),
            ((rows, width), f32, col),
            ((pairs,) + expo[1:], bf16, pl.BlockSpec(expo, lambda p: (p, 0, 0, 0, 0))),
        ],
        (live, query, key, value),
        flops=pairs * 2 * tiles * TB * TB * 4 * PAIR,
        nbytes=pairs * 2 * tiles * TB * TB * 2 + 12 * rows * width,
        exps=pairs * 2 * tiles * TB * TB,
    )


def attend_back_kernel(
    q_ref, k_ref, v_ref, e_ref, do_ref, att_ref, r_ref, cos_ref, sin_ref, dq_ref, dk_ref, dv_ref, dqt_ref
):
    rows = q_ref.shape[0]
    steps = rows // TB
    low_lanes = lanes_of((1, PAIR)) < HD

    def halves(x):
        nil = jnp.zeros_like(x)
        return jnp.where(low_lanes, x, nil), jnp.where(low_lanes, nil, x)

    scaled = do_ref[...].astype(f32) * r_ref[...]
    product_t = (scaled * att_ref[...].astype(f32)).T
    deltas = (
        jnp.sum(product_t[:HD], axis=0, keepdims=True),
        jnp.sum(product_t[HD:], axis=0, keepdims=True),
    )
    grad = scaled.astype(bf16)
    grad_heads = halves(grad)
    query_heads = halves(q_ref[...])
    value_heads = halves(v_ref[...])
    key_t = k_ref[...].T
    zeros = jnp.zeros((HD, rows), bf16)
    key_heads = (
        jnp.concatenate([key_t[:HD], zeros], axis=0),
        jnp.concatenate([zeros, key_t[HD:]], axis=0),
    )
    for j in range(steps):
        js = slice(j * TB, (j + 1) * TB)
        value_grad = jnp.zeros((TB, PAIR), f32)
        key_grad = jnp.zeros((TB, PAIR), f32)
        keys_t = jnp.concatenate([key_heads[0][:, js], key_heads[1][:, js]], axis=1)
        for i in range(j, steps):
            rs = slice(i * TB, (i + 1) * TB)
            tile = i * (i + 1) // 2 + j
            expos, scores = [], []
            for head in range(2):
                grad_prob = nt(value_heads[head][js], grad[rs])
                expo = e_ref[0, head, tile]
                expos.append(expo)
                scores.append(
                    (expo.astype(f32) * (grad_prob - deltas[head][:, rs])).astype(bf16)
                )
            value_grad = value_grad + nn(
                jnp.concatenate(expos, axis=1),
                jnp.concatenate([grad_heads[0][rs], grad_heads[1][rs]], axis=0),
            )
            key_grad = key_grad + nn(
                jnp.concatenate(scores, axis=1),
                jnp.concatenate([query_heads[0][rs], query_heads[1][rs]], axis=0),
            )
            add = nn(keys_t, jnp.concatenate(scores, axis=0))
            if j == 0:
                dqt_ref[:, rs] = add
            else:
                dqt_ref[:, rs] += add
        dv_ref[js, :] = value_grad.astype(bf16)
        dk_ref[js, :] = turn(key_grad, cos_ref[js, :], -sin_ref[js, :]).astype(bf16)
    query_grad = dqt_ref[...].T * (HD**-0.5)
    dq_ref[...] = turn(query_grad, cos_ref[...], -sin_ref[...]).astype(bf16)


def attend_back_call(query, key, value, expo, grad, attended, recip, cos_wide, sin_wide):
    rows, width = query.shape
    pairs, _, tiles = expo.shape[:3]
    col = pl.BlockSpec((rows, PAIR), lambda p: (0, p))
    tab = whole((rows, PAIR))
    e_spec = pl.BlockSpec((1,) + expo.shape[1:], lambda p: (p, 0, 0, 0, 0))
    return call(
        attend_back_kernel,
        (pairs,),
        [col, col, col, e_spec, col, col, col, tab, tab],
        [((rows, width), bf16, col)] * 3,
        (query, key, value, expo, grad, attended, recip, cos_wide, sin_wide),
        scratch=[pltpu.VMEM((PAIR, rows), f32)],
        flops=pairs * 2 * tiles * TB * TB * 8 * PAIR,
        nbytes=pairs * 2 * tiles * TB * TB * 2 + 22 * rows * width,
    )


def route_kernel(
    att_ref, hid_ref, grad_ref, wo_ref, sw_ref, prev_ref, gating_ref, rcol_ref, prow_ref,
    res_ref, info_ref, send_ref, nlow_ref, rg_ref,
):
    step = pl.program_id(0)
    rows = nlow_ref.shape[0]
    blocks = rows // TB
    choices = prev_ref.shape[1]

    @pl.when(step < blocks)
    def _():
        residual = hid_ref[...].astype(f32) + nn(att_ref[...], wo_ref[...])
        res_ref[...] = residual
        scale = lax.rsqrt(jnp.mean(residual * residual, axis=-1, keepdims=True) + norm_eps)
        gain = sw_ref[choices + 5 : choices + 6, :].astype(f32)
        normed = residual * scale * gain
        high, mid, low = split3(normed)
        small_weights = sw_ref[...]
        small = nt(high, small_weights) + nt(mid, small_weights) + nt(low, small_weights)
        logits = small + nn(prev_ref[...], gating_ref[...])
        lane = lanes_of(logits.shape)
        is_choice = lane < choices
        masked = jnp.where(is_choice, logits, masked_score)
        expo = jnp.exp(masked - jnp.max(masked, axis=-1, keepdims=True))
        probs = expo / jnp.sum(expo, axis=-1, keepdims=True)
        wide = small.shape[1]
        partner = jnp.where(lane % 2 == 0, pltpu.roll(small, wide - 1, 1), pltpu.roll(small, 1, 1))
        top = jnp.maximum(small, partner)
        own = jnp.exp(small - top)
        alpha = own / (own + jnp.exp(partner - top))
        gates = [
            jnp.sum(jnp.where(lane == rcol_ref[:, j : j + 1], probs, 0.0), axis=-1, keepdims=True)
            for j in range(2)
        ]
        info = jnp.where(is_choice, probs, alpha)
        for at, column in enumerate((gates[0], gates[1], scale)):
            info = jnp.where(lane == choices + 4 + at, column, info)
        info_ref[...] = info
        here = pl.ds(pl.multiple_of(step * TB, TB), TB)
        nlow_ref[here, :] = high
        grad = grad_ref[...].astype(f32)
        rg_ref[0, here, :] = (gates[0] * grad).astype(bf16)
        rg_ref[1, here, :] = (gates[1] * grad).astype(bf16)

    @pl.when(step >= blocks)
    def _():
        slot = (step - blocks) * CAP + lax.broadcasted_iota(i32, (CAP, rows), 0)
        hot = [jnp.where(prow_ref[j : j + 1, :] == slot, 1.0, 0.0).astype(bf16) for j in range(2)]
        send_ref[0, :CAP, :] = nn(hot[0] + hot[1], nlow_ref[...]).astype(bf16)
        send_ref[0, CAP:, :] = (nn(hot[0], rg_ref[0]) + nn(hot[1], rg_ref[1])).astype(bf16)


def route_call(attended, hidden, grad, w_out, small_weights, prev, gating, rcols, prows, experts):
    rows, width = attended.shape
    blocks = rows // TB
    wide = WIDE

    def block(cols):
        return pl.BlockSpec((TB, cols), lambda i: (jnp.minimum(i, blocks - 1), 0))

    return call(
        route_kernel,
        (blocks + experts,),
        [
            block(width), block(width), block(width), whole(w_out.shape),
            whole(small_weights.shape), block(prev.shape[1]), whole(gating.shape), block(2), whole(prows.shape),
        ],
        [
            ((rows, width), f32, block(width)),
            ((rows, wide), f32, block(wide)),
            (
                (experts, 2 * CAP, width),
                bf16,
                pl.BlockSpec((1, 2 * CAP, width), lambda i: (jnp.maximum(i - blocks, 0), 0, 0)),
            ),
        ],
        (attended, hidden, grad, w_out, small_weights, prev, gating, rcols, prows),
        scratch=[pltpu.VMEM((rows, width), bf16), pltpu.VMEM((2, rows, width), bf16)],
        flops=2 * rows * width * width + 6 * experts * CAP * rows * width,
        nbytes=10 * rows * width + 2 * width * width + 4 * experts * CAP * width,
    )


def ring_order(count):
    wide = 1 << ((count.bit_length() - 1) // 2)
    tall = count // wide
    if wide < 2 or wide * tall != count or tall % 2:
        return list(range(count))
    order = [z * wide for z in range(tall)]
    for turn_at in range(tall):
        z = tall - 1 - turn_at
        across = range(1, wide) if turn_at % 2 == 0 else range(wide - 1, 0, -1)
        order.extend(z * wide + y for y in across)
    return order


def ring_send(x, order, step):
    count = len(order)
    pairs = [(order[i], order[(i + step) % count]) for i in range(count)]
    return lax.ppermute(x, "fsdp", pairs)


def swap(x, experts, bit):
    return lax.ppermute(x, "expert", [(e, e ^ bit) for e in range(experts)])


def cut(x, axis):
    size = x.shape[axis]
    half = -(-size // 32) * 16
    return lax.slice_in_dim(x, 0, half, axis=axis), lax.slice_in_dim(x, half, size, axis=axis)


def ring_gather(x, order, axis):
    count = len(order)
    half = count // 2
    pieces = [None] * count
    pieces[0] = x
    ahead, back = x, x
    for k in range(1, half):
        ahead = ring_send(ahead, order, 1)
        back = ring_send(back, order, -1)
        pieces[count - k] = ahead
        pieces[k] = back
    first = ring_send(cut(ahead, axis)[0], order, 1)
    second = ring_send(cut(back, axis)[1], order, -1)
    pieces[half] = jnp.concatenate([first, second], axis=axis)
    return pieces


def plus(a, b):
    return (a.astype(f32) + b.astype(f32)).astype(bf16)


class RingReduce:
    def __init__(self, parts, order, axis):
        self.parts, self.order, self.axis = parts, order, axis
        self.left = len(order) // 2 - 1
        self.flight = None

    def start(self):
        first, second = cut(self.parts[len(self.order) // 2], self.axis)
        self.flight = (ring_send(first, self.order, 1), ring_send(second, self.order, -1))

    def turn(self):
        k, axis = self.left, self.axis
        ahead, back = self.flight
        mine, other = self.parts[k], self.parts[len(self.order) - k]
        if k == len(self.order) // 2 - 1:
            low, high = cut(mine, axis)
            mine = jnp.concatenate([plus(low, ahead), high], axis=axis)
            low, high = cut(other, axis)
            other = jnp.concatenate([low, plus(high, back)], axis=axis)
        else:
            mine, other = plus(mine, ahead), plus(other, back)
        self.flight = (ring_send(mine, self.order, 1), ring_send(other, self.order, -1))
        self.left = k - 1

    def result(self):
        return self.parts[0].astype(f32) + self.flight[0].astype(f32) + self.flight[1].astype(f32)


def ring_reduce(parts, order, axis):
    sums = RingReduce(parts, order, axis)
    sums.start()
    while sums.left:
        sums.turn()
    return sums.result()


def fetch_chunk(w_refs, buf, sems, turn_of):
    step = pl.program_id(0)
    count = len(w_refs)

    def copy(at, slot):
        return pltpu.make_async_copy(w_refs[turn_of[at]], buf.at[slot], sems.at[slot])

    @pl.when(step == 0)
    def _():
        copy(0, 0).start()

    for at in range(count):

        @pl.when(step == at)
        def _():
            if at + 1 < count:
                copy(at + 1, (at + 1) % 2).start()
            copy(at, at % 2).wait()

    return buf.at[lax.rem(step, 2)]


def accumulate(acc_ref, out, final):
    step = pl.program_id(0)

    @pl.when(step == 0)
    def _():
        acc_ref[...] = out

    @pl.when(step > 0)
    def _():
        acc_ref[...] += out

    @pl.when(step == pl.num_programs(0) - 1)
    def _():
        final[...] = acc_ref[...].astype(bf16).reshape(final.shape)


def expert_kernel(x_ref, *refs):
    w_refs, (y_ref, inner_ref, fa_ref, fb_ref, acc_ref, buf, sems) = refs[:-7], refs[-7:]
    weights = fetch_chunk(w_refs, buf, sems, list(range(len(w_refs))))
    rows_in = x_ref[...].reshape(acc_ref.shape[0], x_ref.shape[2])
    gate = nt(rows_in, weights[0])
    up = nt(rows_in, weights[1])
    sig = 1.0 / (1.0 + jnp.exp(-gate))
    act = gate * sig
    inner = (act * up).astype(bf16)
    inner_ref[0] = inner
    fa_ref[0] = (up * sig * (1.0 + gate * (1.0 - sig))).astype(bf16)
    fb_ref[0] = act.astype(bf16)
    accumulate(acc_ref, nn(inner, weights[2]), y_ref)


def expert_back_kernel(g_ref, fa_ref, fb_ref, *refs):
    w_refs, (dx_ref, dgu_ref, acc_ref, buf, sems) = refs[:-5], refs[-5:]
    weights = fetch_chunk(w_refs, buf, sems, list(range(len(w_refs))))
    grad_in = g_ref[...].reshape(acc_ref.shape[0], g_ref.shape[2])
    grad_inner = nt(grad_in, weights[2])
    grad_gate = (grad_inner * fa_ref[0].astype(f32)).astype(bf16)
    grad_up = (grad_inner * fb_ref[0].astype(f32)).astype(bf16)
    dgu_ref[0, 0] = grad_gate
    dgu_ref[0, 1] = grad_up
    accumulate(acc_ref, nn(grad_gate, weights[0]) + nn(grad_up, weights[1]), dx_ref)


def expert_weights_kernel(x_ref, g_ref, inner_ref, dgu_ref, *dw_refs):
    step = pl.program_id(0)
    rows = inner_ref.shape[1]
    rows_in = x_ref[...].reshape(rows, x_ref.shape[2])
    grad_in = g_ref[...].reshape(rows, g_ref.shape[2])
    terms = (tn(dgu_ref[0, 0], rows_in), tn(dgu_ref[0, 1], rows_in), tn(inner_ref[0], grad_in))
    for at, ref in enumerate(dw_refs):

        @pl.when(step == at)
        def _():
            for part, term in enumerate(terms):
                ref[part] = term.astype(bf16)


def expert_specs(sent, chunks, weight):
    experts, _, width = sent.shape
    _, units, _ = weight.shape
    rows = experts * CAP
    return dict(
        rows=rows,
        chunks=chunks,
        units=units,
        width=width,
        x=pl.BlockSpec((experts, CAP, width), lambda c: (0, 0, 0)),
        g=pl.BlockSpec((experts, CAP, width), lambda c: (0, 1, 0)),
        unit=pl.BlockSpec((1, rows, units), lambda c: (c, 0, 0)),
        pair=pl.BlockSpec((1, 2, rows, units), lambda c: (c, 0, 0, 0)),
        flops=6 * rows * width * chunks * units,
        nbytes=6 * chunks * units * (rows + width) + 4 * rows * width,
        scratch=[
            pltpu.VMEM((rows, width), f32),
            pltpu.VMEM((2,) + weight.shape, bf16),
            pltpu.SemaphoreType.DMA((2,)),
        ],
    )


def expert_call(sent, weights):
    chunks = len(weights)
    s = expert_specs(sent, chunks, weights[0])
    hidden = ((chunks, s["rows"], s["units"]), bf16, s["unit"])
    return call(
        expert_kernel,
        (chunks,),
        [s["x"]] + [pl.BlockSpec(memory_space=pl.ANY)] * chunks,
        [((sent.shape[0], CAP, s["width"]), bf16, s["x"]), hidden, hidden, hidden],
        (sent, *weights),
        scratch=s["scratch"],
        flops=s["flops"],
        nbytes=s["nbytes"],
        exps=s["rows"] * chunks * s["units"],
    )


def expert_back_call(sent, weights, factor_a, factor_b):
    chunks = len(weights)
    s = expert_specs(sent, chunks, weights[0])
    return call(
        expert_back_kernel,
        (chunks,),
        [s["g"], s["unit"], s["unit"]] + [pl.BlockSpec(memory_space=pl.ANY)] * chunks,
        [
            ((sent.shape[0], CAP, s["width"]), bf16, s["x"]),
            ((chunks, 2, s["rows"], s["units"]), bf16, s["pair"]),
        ],
        (sent, factor_a, factor_b, *weights),
        scratch=s["scratch"],
        flops=s["flops"],
        nbytes=s["nbytes"],
    )


def expert_weights_call(sent, inner, dgu, weight, chosen):
    s = expert_specs(sent, len(chosen), weight)
    start = chosen[0]
    unit = pl.BlockSpec((1, s["rows"], s["units"]), lambda c: (start + c, 0, 0))
    pair = pl.BlockSpec((1, 2, s["rows"], s["units"]), lambda c: (start + c, 0, 0, 0))
    return call(
        expert_weights_kernel,
        (len(chosen),),
        [s["x"], s["g"], unit, pair],
        [(weight.shape, bf16, whole(weight.shape))] * len(chosen),
        (sent, sent, inner, dgu),
        flops=s["flops"],
        nbytes=s["nbytes"],
    )


def combine_kernel(
    y_ref, res_ref, info_ref, rcol_ref, pcol_ref, grad_ref, sw_ref, prev_ref, gt_ref,
    out_ref, part_ref, gprev_ref, gsw_ref, gvec_ref, ggat_ref,
):
    step = pl.program_id(0)
    choices = prev_ref.shape[1]
    experts = y_ref.shape[0]
    slots = experts * CAP
    rows_out = y_ref[...].reshape(slots, y_ref.shape[2])
    residual = res_ref[...]
    info = info_ref[...]
    lane = lanes_of(info.shape)

    def column(at):
        return info[:, at : at + 1]

    gates = (column(choices + 4), column(choices + 5))
    small_weights = sw_ref[...]
    gain = small_weights[choices + 5 : choices + 6].astype(f32)
    normed = residual * column(choices + 6) * gain
    grad = grad_ref[...].astype(f32)
    vectors = [small_weights[choices + 6 + c : choices + 7 + c].astype(f32) for c in range(2)]
    alphas = ((column(choices), column(choices + 1)), (column(choices + 2), column(choices + 3)))
    dot_normed = jnp.sum(grad * normed, axis=-1, keepdims=True)
    dot_vectors = [jnp.sum(grad * v, axis=-1, keepdims=True) for v in vectors]
    mixed = residual
    weight_normed = jnp.zeros_like(dot_normed)
    weight_copy = jnp.zeros_like(dot_normed)
    weight_const = [jnp.zeros_like(dot_normed), jnp.zeros_like(dot_normed)]
    grad_probs = jnp.zeros_like(info)
    slot = lanes_of((TB, slots))
    for j in range(2):
        route = rcol_ref[:, j : j + 1]
        hot = jnp.where(pcol_ref[:, j : j + 1] == slot, 1.0, 0.0).astype(bf16)
        rows_j = nn(hot, rows_out)
        is_copy = jnp.where(route == experts + 1, 1.0, 0.0)
        is_const = [jnp.where(route == experts + 2 + c, 1.0, 0.0) for c in range(2)]
        on_normed = is_copy + is_const[0] * alphas[0][0] + is_const[1] * alphas[1][0]
        grad_gate = jnp.sum(grad * rows_j, axis=-1, keepdims=True) + on_normed * dot_normed
        for c in range(2):
            grad_gate = grad_gate + is_const[c] * alphas[c][1] * dot_vectors[c]
            weight_const[c] = weight_const[c] + gates[j] * is_const[c]
        grad_probs = grad_probs + jnp.where(lane == route, grad_gate, 0.0)
        mixed = mixed + gates[j] * rows_j
        weight_normed = weight_normed + gates[j] * on_normed
        weight_copy = weight_copy + gates[j] * is_copy
    mixed = mixed + weight_normed * normed
    for c in range(2):
        mixed = mixed + weight_const[c] * alphas[c][1] * vectors[c]
    out_ref[...] = mixed.astype(bf16)
    is_choice = lane < choices
    probs = jnp.where(is_choice, info, 0.0)
    grad_small = probs * (grad_probs - jnp.sum(probs * grad_probs, axis=-1, keepdims=True))
    direct = weight_copy
    coefs = jnp.zeros_like(info)
    for c in range(2):
        grad_alpha = (weight_const[c] * dot_normed, weight_const[c] * dot_vectors[c])
        mean = alphas[c][0] * grad_alpha[0] + alphas[c][1] * grad_alpha[1]
        for k in range(2):
            grad_small = jnp.where(
                lane == choices + 2 * c + k, alphas[c][k] * (grad_alpha[k] - mean), grad_small
            )
        direct = direct + alphas[c][0] * weight_const[c]
        coefs = jnp.where(lane == c, alphas[c][1] * weight_const[c], coefs)
    high, mid, low = split3(grad_small)
    part_ref[...] = direct * grad + (
        nn(high, small_weights) + nn(mid, small_weights) + nn(low, small_weights)
    )
    gating_t = gt_ref[...]
    logits_high, logits_mid, logits_low = split3(jnp.where(is_choice, grad_small, 0.0))
    grad_prev = nn(logits_high, gating_t) + nn(logits_mid, gating_t) + nn(logits_low, gating_t)
    gprev_ref[...] = grad_prev[:, :choices]
    normed_high, normed_mid = split2(normed)
    grad_sw = tn(high, normed_high) + tn(mid, normed_high) + tn(high, normed_mid)
    coef_high, coef_mid = split2(coefs)
    grad_vec = tn(coef_high, grad_ref[...]) + tn(coef_mid, grad_ref[...])
    prev = prev_ref[...]
    grad_gating = tn(prev, high) + tn(prev, mid) + tn(prev, low)

    @pl.when(step == 0)
    def _():
        gsw_ref[...] = grad_sw
        gvec_ref[...] = grad_vec
        ggat_ref[...] = grad_gating

    @pl.when(step > 0)
    def _():
        gsw_ref[...] += grad_sw
        gvec_ref[...] += grad_vec
        ggat_ref[...] += grad_gating


def combine_call(back, residual, info, rcols, pcols, grad, small_weights, prev, gating_t):
    rows, width = residual.shape
    wide = info.shape[1]
    choices = prev.shape[1]
    slots = back.shape[0] * CAP

    def block(cols):
        return pl.BlockSpec((TB, cols), lambda i: (i, 0))

    return call(
        combine_kernel,
        (rows // TB,),
        [
            whole(back.shape), block(width), block(wide), block(2), block(2), block(width),
            whole(small_weights.shape), block(choices), whole(gating_t.shape),
        ],
        [
            ((rows, width), bf16, block(width)),
            ((rows, width), f32, block(width)),
            ((rows, choices), f32, block(choices)),
            ((wide, width), f32, whole((wide, width))),
            ((wide, width), f32, whole((wide, width))),
            ((choices, wide), f32, whole((choices, wide))),
        ],
        (back, residual, info, rcols, pcols, grad, small_weights, prev, gating_t),
        flops=4 * slots * rows * width,
        nbytes=14 * rows * width + 2 * slots * width,
    )


def residual_kernel(
    gain_at, dx_ref, part_ref, res_ref, pcol_ref, grad_ref, sw_ref, wo_ref, att_ref,
    gres_ref, gatt_ref, gwo_ref, ggain_ref, acc_ref,
):
    step = pl.program_id(0)
    experts = dx_ref.shape[0]
    slots = experts * CAP
    slot = lanes_of((TB, slots))
    hot = jnp.where(
        (pcol_ref[:, 0:1] == slot) | (pcol_ref[:, 1:2] == slot), 1.0, 0.0
    ).astype(bf16)
    grad_normed = part_ref[...] + nn(hot, dx_ref[...].reshape(slots, dx_ref.shape[2]))
    residual = res_ref[...]
    scale = lax.rsqrt(jnp.mean(residual * residual, axis=-1, keepdims=True) + norm_eps)
    unit = residual * scale
    grad_gain = jnp.sum(grad_normed * unit, axis=0, keepdims=True)
    scaled = grad_normed * sw_ref[gain_at : gain_at + 1, :].astype(f32)
    grad_residual = grad_ref[...].astype(f32) + scale * (
        scaled - unit * jnp.mean(scaled * unit, axis=-1, keepdims=True)
    )
    gres_ref[...] = grad_residual
    low = grad_residual.astype(bf16)
    gatt_ref[...] = nt(low, wo_ref[...]).astype(bf16)
    grad_out = tn(att_ref[...], low)

    @pl.when(step == 0)
    def _():
        acc_ref[...] = grad_out
        ggain_ref[...] = grad_gain

    @pl.when(step > 0)
    def _():
        acc_ref[...] += grad_out
        ggain_ref[...] += grad_gain

    @pl.when(step == pl.num_programs(0) - 1)
    def _():
        gwo_ref[...] = acc_ref[...].astype(bf16)


def residual_call(dx, part, residual, pcols, grad, small_weights, gain_at, w_out, attended):
    rows, width = residual.shape
    slots = dx.shape[0] * CAP

    def block(cols):
        return pl.BlockSpec((TB, cols), lambda i: (i, 0))

    return call(
        functools.partial(residual_kernel, gain_at),
        (rows // TB,),
        [
            whole(dx.shape), block(width), block(width), block(2), block(width), whole(small_weights.shape),
            whole(w_out.shape), block(width),
        ],
        [
            ((rows, width), f32, block(width)),
            ((rows, width), bf16, block(width)),
            ((width, width), bf16, whole((width, width))),
            ((1, width), f32, whole((1, width))),
        ],
        (dx, part, residual, pcols, grad, small_weights, w_out, attended),
        scratch=[pltpu.VMEM((width, width), f32)],
        flops=2 * slots * rows * width + 4 * rows * width * width,
        nbytes=18 * rows * width + 2 * slots * width,
    )


def qkv_weights_kernel(
    gain_at, where_ref, dq_ref, dk_ref, dv_ref, n_ref, w_ref, small_ref, gwo_ref, ggain_ref, gsw_ref, gvec_ref,
    ggat_ref, own_ref, other_ref, acc_ref,
):
    step = pl.program_id(0)
    count, _, width = own_ref.shape
    part = width // count
    half = part // 2
    shards = dq_ref.shape[1] // part
    normed = n_ref[...]
    core = where_ref[count]
    gain_grad = jnp.zeros((1, width), f32)

    def put(side, shard, at, value):
        rel = where_ref[count + 1 + shard]

        @pl.when(core == side)
        def _():
            own_ref[rel, at : at + value.shape[0], :] = value

        @pl.when(core != side)
        def _():
            other_ref[rel, at : at + value.shape[0], :] = value

    for at, ref in enumerate((dq_ref, dk_ref, dv_ref, None)):
        if ref is None:
            term = gwo_ref[...]
        else:
            full = tn(ref[...], normed)
            gain_grad = gain_grad + jnp.sum(full * w_ref[at].astype(f32), axis=0, keepdims=True)
            term = full.astype(bf16)
        for m in range(shards):
            for side in range(2):
                row = m * part + side * half
                put(side, step * shards + m, at * half, term[row : row + half])

    @pl.when(step == 0)
    def _():
        acc_ref[...] = gain_grad

    @pl.when(step > 0)
    def _():
        acc_ref[...] += gain_grad

    @pl.when(step == pl.num_programs(0) - 1)
    def _():
        gain_one = acc_ref[...] / small_ref[gain_at : gain_at + 1, :].astype(f32)
        vectors = jnp.concatenate(
            [gsw_ref[:gain_at, :], gain_one, ggain_ref[...], gvec_ref[:2, :]], axis=0
        )
        gating_high = ggat_ref[...].astype(bf16).astype(f32)
        gating = (gating_high, ggat_ref[...] - gating_high)
        lanes = lanes_of((1, width)) < part
        split = vectors.shape[0] // 2
        spare = jnp.zeros((16 - split - 1, width), f32)
        for m in range(count):
            here = vectors if m == 0 else pltpu.roll(vectors, width - m * part, 1)
            here = jnp.where(lanes, here, 0.0)
            for side in range(2):
                block = jnp.concatenate(
                    [here[side * split : (side + 1) * split], gating[side], spare], axis=0
                )
                put(side, m, 4 * half, block.astype(bf16))


def qkv_weights_call(where, dq, dk, dv, normed, weights, small, gain_at, gwo, ggain, gsw, gvec, ggat, count):
    rows, width = normed.shape
    steps = 2
    cols = width // steps
    col = pl.BlockSpec((rows, cols), lambda c: (0, c))
    part = width // count
    shape = (count, 2 * part + 16, width)
    return call(
        functools.partial(qkv_weights_kernel, gain_at),
        (steps,),
        [
            pl.BlockSpec(memory_space=pltpu.SMEM), col, col, col, whole(normed.shape),
            pl.BlockSpec((3, cols, width), lambda c: (0, c, 0)), whole(small.shape),
            pl.BlockSpec((cols, width), lambda c: (c, 0)), whole(ggain.shape), whole(gsw.shape), whole(gvec.shape),
            whole(ggat.shape),
        ],
        [(shape, bf16, whole(shape))] * 2,
        (where, dq, dk, dv, normed, weights, small, gwo, ggain, gsw, gvec, ggat),
        scratch=[pltpu.VMEM((1, width), f32)],
        flops=6 * rows * width * width,
        nbytes=8 * rows * width + 18 * width * width,
    )


def finish_kernel(choices, where_ref, mine_ref, theirs_ref, gq_ref, gk_ref, gv_ref, gwo_ref, small_ref, gat_ref):
    part = gwo_ref.shape[0]
    half = part // 2
    core = where_ref[where_ref.shape[0] // 2]
    width = gwo_ref.shape[1]

    def side(which, at, size):
        first = mine_ref[at : at + size, :].astype(f32)
        second = theirs_ref[at : at + size, :].astype(f32)
        return jnp.where(core == which, first, second)

    for at, ref in enumerate((gq_ref, gk_ref, gv_ref, gwo_ref)):
        both = jnp.concatenate([side(0, at * half, half), side(1, at * half, half)], axis=0)
        if at == 3:
            ref[...] = both
        else:
            ref[...] = both.T[:, :part]
    split = (choices + 8) // 2
    low, high = side(0, 4 * half, 16), side(1, 4 * half, 16)
    small_ref[...] = jnp.concatenate([low[:split, :WIDE], high[:split, :WIDE]], axis=0)
    gat_ref[...] = (low + high)[split : split + 1, :]


def finish_call(where, mine, theirs, part, choices):
    width = mine.shape[1]
    thin = (width, part)
    return call(
        functools.partial(finish_kernel, choices),
        (1,),
        [pl.BlockSpec(memory_space=pltpu.SMEM), whole(mine.shape), whole(mine.shape)],
        [
            (thin, f32, whole(thin)),
            (thin, f32, whole(thin)),
            (thin, f32, whole(thin)),
            ((part, width), f32, whole((part, width))),
            ((choices + 8, WIDE), f32, whole((choices + 8, WIDE))),
            ((1, width), f32, whole((1, width))),
        ],
        (where, mine, theirs),
        flops=10,
        nbytes=20 * part * width,
    )


def plain_weights_kernel(dq_ref, dk_ref, dv_ref, n_ref, out_ref):
    normed = n_ref[...]
    for part, ref in enumerate((dq_ref, dk_ref, dv_ref)):
        out_ref[part] = tn(ref[...], normed)


def plain_weights_call(dq, dk, dv, normed):
    rows, width = normed.shape
    col = pl.BlockSpec((rows, 256), lambda c: (0, c))
    return call(
        plain_weights_kernel,
        (width // 256,),
        [col, col, col, whole((rows, width))],
        [((3, width, width), f32, pl.BlockSpec((3, 256, width), lambda c: (0, c, 0)))],
        (dq, dk, dv, normed),
        flops=6 * rows * width * width,
        nbytes=8 * rows * width + 12 * width * width,
    )[0]


def hidden_kernel(gain_at, dq_ref, dk_ref, dv_ref, w_ref, hid_ref, small_ref, gres_ref, out_ref):
    grad_normed = nn(dq_ref[...], w_ref[0]) + nn(dk_ref[...], w_ref[1]) + nn(dv_ref[...], w_ref[2])
    hidden = hid_ref[...].astype(f32)
    scale = lax.rsqrt(jnp.mean(hidden * hidden, axis=-1, keepdims=True) + norm_eps)
    unit = hidden * scale
    scaled = grad_normed * small_ref[gain_at : gain_at + 1, :].astype(f32)
    out_ref[...] = gres_ref[...] + scale * (
        scaled - unit * jnp.mean(scaled * unit, axis=-1, keepdims=True)
    )


def hidden_call(dq, dk, dv, weights, hidden, small, gain_at, grad_residual):
    rows, width = hidden.shape
    row = pl.BlockSpec((TB, width), lambda i: (i, 0))
    return call(
        functools.partial(hidden_kernel, gain_at),
        (rows // TB,),
        [row, row, row, whole(weights.shape), row, whole(small.shape), row],
        [((rows, width), f32, row)],
        (dq, dk, dv, weights, hidden, small, grad_residual),
        flops=6 * rows * width * width,
        nbytes=16 * rows * width + 6 * width * width,
    )[0]


def rope_wide(length):
    inverse = rope_base ** (-(2.0 * jnp.arange(HD // 2, dtype=f32)) / HD)
    angles = jnp.arange(length, dtype=f32)[:, None] * inverse[None, :]
    cosine, sine = jnp.cos(angles), jnp.sin(angles)
    return (
        jnp.concatenate([cosine] * 4, axis=1),
        jnp.concatenate([-sine, sine, -sine, sine], axis=1),
    )


def to_rows(flat, width):
    count = -(-flat.shape[1] // width)
    return jnp.pad(flat, ((0, 0), (0, count * width - flat.shape[1]))).reshape(
        flat.shape[0], count, width
    )


def per_device(
    hidden_in,
    prev_logits,
    seq_lengths,
    seq_order,
    routes,
    w_query,
    w_key,
    w_value,
    w_output,
    gain_attn,
    gain_moe,
    w_router,
    w_gating,
    w_const,
    v_const,
    w_gate,
    w_up,
    w_down,
    out_grad,
):
    rows, width = hidden_in.shape[1:]
    experts = lax.axis_size("expert")
    shards = lax.axis_size("fsdp")
    choices = w_router.shape[1]
    part = width // shards
    hidden = hidden_in.reshape(rows, width)
    grad = out_grad.reshape(rows, width)
    prev = prev_logits.reshape(rows, choices)

    fsdp_here = lax.axis_index("fsdp")
    own = lax.axis_index("expert") * shards + fsdp_here
    live = lax.dynamic_slice(seq_lengths, (own,), (1,))
    dealt = lax.all_gather(routes.reshape(rows, 2).T, "expert", axis=0, tiled=False)
    peers = jnp.arange(experts, dtype=i32) * shards + fsdp_here
    mine = seq_order[peers] == own
    route_rows = jnp.sum(jnp.where(mine[:, None, None], dealt, 0), axis=0)
    ids = jnp.arange(experts, dtype=i32)
    named = (route_rows[0][None, :] == ids[:, None]) | (route_rows[1][None, :] == ids[:, None])
    at = jnp.arange(rows, dtype=i32)
    earlier = (at[:, None] < at[None, :]).astype(bf16)
    counts = nn(named.astype(bf16), earlier).astype(i32)
    place_rows = jnp.stack(
        [
            jnp.where(
                r < experts,
                r * CAP + jnp.sum(jnp.where(r[None, :] == ids[:, None], counts, 0), axis=0),
                -1,
            )
            for r in (route_rows[0], route_rows[1])
        ]
    )
    route_cols = route_rows.T
    place_cols = place_rows.T
    cos_wide, sin_wide = rope_wide(rows)

    gain_at = choices + 4
    small_parts = jnp.concatenate(
        [w_router.T, w_const.T, gain_attn[None], gain_moe[None], v_const], axis=0
    )
    small_count = choices + 8
    order = ring_order(shards)
    place = jnp.asarray([order.index(m) for m in range(shards)], dtype=i32)
    spot = place[fsdp_here]
    core = lax.rem(lax.axis_index("expert"), 2)
    paired = part % 32 == 0 and small_count == 16 and shards % 2 == 0 and experts & (experts - 1) == 0
    ring = jnp.asarray(order, dtype=i32)
    where = jnp.concatenate(
        [ring[(spot + jnp.arange(shards, dtype=i32)) % shards], core[None], (place - spot) % shards]
    )
    expert_pack = jnp.stack([w_gate[0].T, w_up[0].T, w_down[0]])
    w_out = lax.all_gather(w_output, "fsdp", axis=0, tiled=True)
    if paired:
        half = part // 2
        small_wide = jnp.pad(small_parts, ((0, 0), (0, width - part)))
        thin = (w_query.T, w_key.T, w_value.T)
        pack = jnp.concatenate(
            [
                x
                for side in range(2)
                for x in [w[side * half : (side + 1) * half] for w in thin]
                + [small_wide[side * 8 : (side + 1) * 8]]
            ],
            axis=0,
        )
        tall = 3 * half + 8
        own = ring_gather(lax.dynamic_slice_in_dim(pack, core * tall, tall), order, 0)
        other = [lax.dynamic_slice_in_dim(pack, (1 - core) * tall, tall)]
        other += [swap(piece, experts, 1) for piece in own[1:]]
        expert_pack, _ = lax.optimization_barrier((expert_pack, own[shards // 2]))
        query, key, value, normed_one, qkv_weights, small = qkv_pieces_call(
            hidden, where, own, other, gain_at, part, cos_wide, sin_wide
        )
    else:
        first_pack = jnp.concatenate(
            [w_query.T, w_key.T, w_value.T, to_rows(small_parts.reshape(1, -1), width)[0]], axis=0
        )
        first = lax.all_gather(first_pack, "fsdp", axis=0, tiled=False)
        qkv_weights = (
            first[:, : 3 * part]
            .reshape(shards, 3, part, width)
            .transpose(1, 0, 2, 3)
            .reshape(3, width, width)
        )
        small = (
            first[:, 3 * part :]
            .reshape(shards, -1)[:, : small_count * part]
            .reshape(shards, small_count, part)
            .transpose(1, 0, 2)
            .reshape(small_count, width)
        )
        small = jnp.pad(small, ((0, WIDE - small_count), (0, 0)))
        query, key, value, normed_one = qkv_call(
            hidden, small, gain_at, qkv_weights, cos_wide, sin_wide
        )
    expert_weights = ring_gather(expert_pack, order, 1)
    farthest = shards // 2
    turns = [farthest] + [r for k in range(farthest - 1, 0, -1) for r in (k, shards - k)] + [0]
    expert_weights = [expert_weights[r] for r in turns]

    gating_wide = jnp.pad(w_gating, ((0, 0), (0, WIDE - choices)))
    gating_t = jnp.pad(w_gating.T, ((0, WIDE - choices), (0, WIDE - choices)))

    attended, recip, expo = attend_call(live, query, key, value)
    residual, info, send = route_call(
        attended, hidden, grad, w_out, small, prev, gating_wide, route_cols, place_rows, experts
    )
    sent = lax.all_to_all(send, "expert", split_axis=0, concat_axis=0, tiled=True)
    expert_out, inner, factor_a, factor_b = expert_call(sent, expert_weights)
    returned = lax.all_to_all(expert_out, "expert", split_axis=0, concat_axis=0, tiled=True)
    expert_dx, dgu = expert_back_call(sent, expert_weights, factor_a, factor_b)
    returned_dx = lax.all_to_all(expert_dx, "expert", split_axis=0, concat_axis=0, tiled=True)
    lead = min(3, shards)
    groups = [list(range(lead)), list(range(lead, shards))]
    expert_dw = [None] * shards
    for chosen in groups:
        terms = expert_weights_call(sent, inner, dgu, expert_pack, chosen)
        for at, term in zip(chosen, terms):
            expert_dw[turns[at]] = term
    sums = RingReduce(expert_dw, order, 1)
    sums.start()
    returned, _ = lax.optimization_barrier((returned, (expert_dw, sums.flight)))
    sums.turn()

    hidden_out, part_grad, grad_prev, grad_sw, grad_vec, grad_gating = combine_call(
        returned, residual, info, route_cols, place_cols, grad, small, prev, gating_t
    )
    grad_residual, grad_attended, grad_wo, grad_gain_two = residual_call(
        returned_dx, part_grad, residual, place_cols, grad, small, gain_at + 1, w_out, attended
    )
    if sums.left:
        grad_attended, _ = lax.optimization_barrier((grad_attended, sums.flight))
        sums.turn()
    dq, dk, dv = attend_back_call(
        query, key, value, expo, grad_attended, attended, recip, cos_wide, sin_wide
    )
    if sums.left:
        dq, _ = lax.optimization_barrier((dq, sums.flight))
        sums.turn()
    grad_hidden = hidden_call(dq, dk, dv, qkv_weights, hidden, small, gain_at, grad_residual)
    if paired:
        own, other = qkv_weights_call(
            where, dq, dk, dv, normed_one, qkv_weights, small, gain_at, grad_wo, grad_gain_two, grad_sw, grad_vec,
            jnp.pad(grad_gating[:, :choices].reshape(1, -1), ((0, 0), (0, width - choices * choices))), shards,
        )
        got = swap(other, experts, 1)
        mine = ring_reduce([plus(own[r], got[r]) for r in range(shards)], order, 0).astype(bf16)
        bit = 2
        while bit < experts:
            mine = plus(mine, swap(mine, experts, bit))
            bit *= 2
        theirs = swap(mine, experts, 1)
        total_q, total_k, total_v, total_o, small_total, gating_row = finish_call(
            where, mine, theirs, part, choices
        )
        small_total = small_total[:, :part]
        gating_total = gating_row[0, : choices * choices].reshape(choices, choices)
    else:
        grad_qkv = plain_weights_call(dq, dk, dv, normed_one)
        grad_gain_one = jnp.sum(grad_qkv * qkv_weights.astype(f32), axis=(0, 1))[None] / small[
            gain_at : gain_at + 1
        ].astype(f32)
        small_grads = jnp.concatenate(
            [grad_sw[:gain_at], grad_gain_one, grad_gain_two, grad_vec[:2]], axis=0
        )
        small_flat = (
            small_grads.reshape(small_count, shards, part).transpose(1, 0, 2).reshape(shards, -1)
        )
        gating_flat = grad_gating[:, :choices].reshape(1, -1)
        gating_both = jnp.concatenate(split2(gating_flat), axis=1)
        flat = jnp.concatenate(
            [small_flat.astype(bf16), jnp.broadcast_to(gating_both, (shards, gating_both.shape[1]))], axis=1
        )
        shared = jnp.concatenate(
            [
                grad_qkv.astype(bf16)
                .reshape(3, shards, part, width)
                .transpose(1, 0, 2, 3)
                .reshape(shards, 3 * part, width),
                grad_wo.reshape(shards, part, width),
                to_rows(flat, width),
            ],
            axis=1,
        )
        scattered = lax.psum_scatter(shared, "fsdp", scatter_dimension=0, tiled=False)
        total = lax.psum(scattered, "expert").astype(f32)
        total_q, total_k, total_v = [total[at * part : (at + 1) * part].T for at in range(3)]
        total_o = total[3 * part : 4 * part]
        flat_total = total[4 * part :].reshape(-1)
        small_total = flat_total[: small_count * part].reshape(small_count, part)
        gating_at = small_count * part
        gating_total = jnp.sum(
            flat_total[gating_at : gating_at + 2 * choices * choices].reshape(2, choices, choices), axis=0
        )
    while sums.left:
        sums.turn()
    expert_total = sums.result()
    return (
        hidden_out[None],
        grad_hidden[None],
        grad_prev[None],
        total_q,
        total_k,
        total_v,
        total_o,
        small_total[gain_at],
        small_total[gain_at + 1],
        small_total[:choices].T,
        gating_total,
        small_total[choices:gain_at].T,
        small_total[gain_at + 2 :],
        expert_total[0].T[None],
        expert_total[1].T[None],
        expert_total[2][None],
    )


def solution(mesh):
    rows = P(("expert", "fsdp"), None, None)
    ins = (
        rows, rows, P(), P(), rows,
        P(None, "fsdp"), P(None, "fsdp"), P(None, "fsdp"), P("fsdp", None),
        P("fsdp"), P("fsdp"), P("fsdp", None), P(), P("fsdp", None), P(None, "fsdp"),
        P("expert", None, "fsdp"), P("expert", None, "fsdp"), P("expert", "fsdp", None), rows,
    )
    outs = (
        rows, rows, rows,
        P(None, "fsdp"), P(None, "fsdp"), P(None, "fsdp"), P("fsdp", None),
        P("fsdp"), P("fsdp"), P("fsdp", None), P(), P("fsdp", None), P(None, "fsdp"),
        P("expert", None, "fsdp"), P("expert", None, "fsdp"), P("expert", "fsdp", None),
    )
    return jax.shard_map(per_device, mesh=mesh, in_specs=ins, out_specs=outs, check_vma=False)
```

```python
import functools

import jax
import jax.numpy as jnp
from jax import lax
from jax.experimental import pallas as pl
from jax.experimental.pallas import tpu as pltpu
from jax.sharding import PartitionSpec as P

HD = 64
CAP = 256
TB = 256
PAIR = 2 * HD
WIDE = 128
SLOW = 3.0
norm_eps = 1e-05
rope_base = 10000.0
masked_score = -1e30
f32 = jnp.float32
bf16 = jnp.bfloat16
i32 = jnp.int32


def nn(a, b):
    return lax.dot_general(a, b, (((1,), (0,)), ((), ())), preferred_element_type=f32)


def nt(a, b):
    return lax.dot_general(a, b, (((1,), (1,)), ((), ())), preferred_element_type=f32)


def tn(a, b):
    return lax.dot_general(a, b, (((0,), (0,)), ((), ())), preferred_element_type=f32)


def split2(x):
    high = x.astype(bf16)
    return high, (x - high.astype(f32)).astype(bf16)


def split3(x):
    high = x.astype(bf16)
    rest = x - high.astype(f32)
    mid = rest.astype(bf16)
    return high, mid, (rest - mid.astype(f32)).astype(bf16)


def call(kernel, grid, ins, outs, args, scratch=(), flops=0, nbytes=0, vmem=60 << 20, aliases=None):
    body = kernel.func if isinstance(kernel, functools.partial) else kernel
    return pl.pallas_call(
        kernel,
        name=body.__name__,
        grid=grid,
        in_specs=ins,
        out_specs=[o[2] for o in outs],
        out_shape=[jax.ShapeDtypeStruct(o[0], o[1]) for o in outs],
        scratch_shapes=list(scratch),
        input_output_aliases=aliases or {},
        compiler_params=pltpu.CompilerParams(
            dimension_semantics=("arbitrary",) * len(grid), vmem_limit_bytes=vmem
        ),
        cost_estimate=pl.CostEstimate(
            flops=int(flops * SLOW), bytes_accessed=nbytes, transcendentals=0
        ),
    )(*args)


def whole(shape):
    zeros = (0,) * len(shape)
    return pl.BlockSpec(shape, lambda *_: zeros)


def lanes_of(shape):
    return lax.broadcasted_iota(i32, shape, len(shape) - 1)


def turn(values, cos_wide, sin_wide):
    first = lanes_of((1, PAIR)) % HD < HD // 2
    partner = jnp.where(first, pltpu.roll(values, PAIR - HD // 2, 1), pltpu.roll(values, HD // 2, 1))
    return values * cos_wide + partner * sin_wide


def eye(size):
    at = (lax.broadcasted_iota(i32, (size, size), 0), lax.broadcasted_iota(i32, (size, size), 1))
    return jnp.where(at[0] == at[1], 1.0, 0.0).astype(bf16)


def pack_kernel(
    core_ref, wq_ref, wk_ref, wv_ref, wo_ref, router_ref, const_ref, g1_ref, g2_ref, vec_ref, own_ref, other_ref
):
    part, width = wq_ref.shape
    half = part // 2
    core = core_ref[0]
    small = jnp.concatenate(
        [ref[...].astype(f32) for ref in (router_ref, const_ref, g1_ref, g2_ref, vec_ref)], axis=0
    )
    small = jnp.concatenate([small, jnp.zeros((small.shape[0], width - part), f32)], axis=1).astype(bf16)
    split = small.shape[0] // 2
    for side in range(2):
        rows = [ref[side * half : (side + 1) * half, :] for ref in (wq_ref, wk_ref, wv_ref, wo_ref)]
        rows.append(small[side * split : (side + 1) * split])

        def put(ref):
            at = 0
            for piece in rows:
                ref[at : at + piece.shape[0], :] = piece
                at += piece.shape[0]

        @pl.when(core == side)
        def _():
            put(own_ref)

        @pl.when(core != side)
        def _():
            put(other_ref)


def pack_call(core, *weights):
    part, width = weights[0].shape
    count = sum(w.shape[0] for w in weights[4:])
    shape = (4 * (part // 2) + count // 2, width)
    return call(
        pack_kernel,
        (1,),
        [pl.BlockSpec(memory_space=pltpu.SMEM)] + [whole(w.shape) for w in weights],
        [(shape, bf16, whole(shape))] * 2,
        (core, *weights),
        flops=1 << 20,
        nbytes=12 * width * part,
    )


def deal_kernel(experts, mine_ref, dealt_ref, out_ref):
    count, _, rows = dealt_ref.shape
    routes = jnp.zeros((2, rows), i32)
    for e in range(count):
        routes = routes + dealt_ref[e] * mine_ref[e]
    at = lax.broadcasted_iota(i32, (experts, rows), 0)
    named = [routes[j : j + 1] == at for j in range(2)]
    hits = jnp.where(named[0] | named[1], 1.0, 0.0).astype(bf16)
    before = lax.broadcasted_iota(i32, (rows, rows), 0) < lax.broadcasted_iota(i32, (rows, rows), 1)
    counts = nn(hits, jnp.where(before, 1.0, 0.0).astype(bf16)) + (at * CAP).astype(f32)
    out_ref[...] = jnp.zeros(out_ref.shape, f32)
    out_ref[0:2, :] = routes.astype(f32)
    for j in range(2):
        slot = jnp.sum(jnp.where(named[j], counts, 0.0), axis=0, keepdims=True)
        out_ref[2 + j : 3 + j, :] = jnp.where(routes[j : j + 1] < experts, slot, -1.0)


def deal_call(mine, dealt):
    experts, _, rows = dealt.shape
    return call(
        functools.partial(deal_kernel, experts),
        (1,),
        [pl.BlockSpec(memory_space=pltpu.SMEM), whole(dealt.shape)],
        [((8, rows), f32, whole((8, rows)))],
        (mine, dealt),
        flops=2 * 128 * rows * rows,
        nbytes=64 * rows,
    )[0]


def columns_of(table_ref):
    return table_ref[...].T.astype(i32)


def pack_experts_kernel(gate_ref, up_ref, down_ref, out_ref):
    one = eye(gate_ref.shape[2])
    out_ref[0] = nt(one, gate_ref[0]).astype(bf16)
    out_ref[1] = nt(one, up_ref[0]).astype(bf16)
    out_ref[2] = down_ref[0]


def pack_experts_call(gate, up, down):
    _, width, units = gate.shape
    shape = (3, units, width)
    return call(
        pack_experts_kernel,
        (1,),
        [whole(gate.shape)] * 2 + [whole(down.shape)],
        [(shape, bf16, whole(shape))],
        (gate, up, down),
        flops=1 << 20,
        nbytes=12 * width * units,
    )[0]


def finish_experts_kernel(own_ref, ahead_ref, back_ref, gate_ref, up_ref):
    for at, ref in enumerate((gate_ref, up_ref)):
        total = own_ref[at].astype(f32) + ahead_ref[at].astype(f32) + back_ref[at].astype(f32)
        ref[0] = total.T


def finish_experts_call(own, ahead, back):
    _, units, width = own.shape
    outs = [(1, width, units)] * 2
    return call(
        finish_experts_kernel,
        (1,),
        [whole(own.shape)] * 3,
        [(shape, f32, whole(shape)) for shape in outs],
        (own, ahead, back),
        flops=1 << 20,
        nbytes=30 * units * width,
    )


def qkv_rows(hid_ref, gain, w_ref, cos_ref, sin_ref, q_ref, k_ref, v_ref, n_ref):
    width = hid_ref.shape[1]
    hidden = hid_ref[...].astype(f32)
    scale = lax.rsqrt(jnp.mean(hidden * hidden, axis=-1, keepdims=True) + norm_eps)
    normed = (hidden * scale * gain).astype(bf16)
    n_ref[...] = normed
    cos_wide, sin_wide = cos_ref[...], sin_ref[...]
    for part, (out, factor) in enumerate(((q_ref, HD**-0.5), (k_ref, 1.0))):
        full = nt(normed, w_ref[part])
        for at in range(0, width, PAIR):
            lin = full[:, at : at + PAIR]
            out[:, at : at + PAIR] = (turn(lin, cos_wide, sin_wide) * factor).astype(bf16)
    v_ref[...] = nt(normed, w_ref[2]).astype(bf16)


def qkv_kernel(gain_at, hid_ref, small_ref, w_ref, *refs):
    gain = small_ref[gain_at : gain_at + 1, :].astype(f32)
    qkv_rows(hid_ref, gain, w_ref, *refs)


def qkv_pieces_kernel(gain_at, part, where_ref, hid_ref, cos_ref, sin_ref, *refs):
    pieces, (q_ref, k_ref, v_ref, n_ref, w_ref, wo_ref, small_ref, vec_ref) = refs[:-8], refs[-8:]
    count = len(pieces) // 2
    half = part // 2
    vectors = pieces[0].shape[0] - 4 * half

    @pl.when(pl.program_id(0) == 0)
    def _():
        vec_ref[...] = jnp.zeros_like(vec_ref)
        core = where_ref[count]
        for own in range(2):
            side = core if own == 0 else 1 - core
            total = None
            for r in range(count):
                ref = pieces[own * count + r]
                shard = where_ref[r]
                row = pl.multiple_of(shard * part + side * half, 16)
                for at in range(3):
                    w_ref[at, pl.ds(row, half), :] = ref[at * half : (at + 1) * half, :]
                wo_ref[pl.ds(row, half), :] = ref[3 * half : 4 * half, :]
                moved = pltpu.roll(ref[4 * half :, :].astype(f32), shard * part, 1)
                total = moved if total is None else total + moved
            vec_ref[pl.ds(pl.multiple_of(side * vectors, 8), vectors), :] = total
        small_ref[...] = vec_ref[...].astype(bf16)

    gain = small_ref[gain_at : gain_at + 1, :].astype(f32)
    qkv_rows(hid_ref, gain, w_ref, cos_ref, sin_ref, q_ref, k_ref, v_ref, n_ref)


def qkv_specs(hidden):
    rows, width = hidden.shape
    row = pl.BlockSpec((TB, width), lambda i: (i, 0))
    return dict(
        row=row,
        tab=pl.BlockSpec((TB, PAIR), lambda i: (i, 0)),
        outs=[((rows, width), bf16, row)] * 4,
        flops=6 * rows * width * width,
        nbytes=10 * rows * width + 6 * width * width,
    )


def qkv_call(hidden, small, gain_at, weights, cos_wide, sin_wide):
    s = qkv_specs(hidden)
    return call(
        functools.partial(qkv_kernel, gain_at),
        (hidden.shape[0] // TB,),
        [s["row"], whole(small.shape), whole(weights.shape), s["tab"], s["tab"]],
        s["outs"],
        (hidden, small, weights, cos_wide, sin_wide),
        flops=s["flops"],
        nbytes=s["nbytes"],
    )


def qkv_pieces_call(hidden, where, own, other, gain_at, part, cos_wide, sin_wide):
    s = qkv_specs(hidden)
    width = hidden.shape[1]
    pieces = list(own) + list(other)
    return call(
        functools.partial(qkv_pieces_kernel, gain_at, part),
        (hidden.shape[0] // TB,),
        [pl.BlockSpec(memory_space=pltpu.SMEM), s["row"], s["tab"], s["tab"]]
        + [whole(piece.shape) for piece in pieces],
        s["outs"]
        + [
            ((3, width, width), bf16, whole((3, width, width))),
            ((width, width), bf16, whole((width, width))),
            ((WIDE, width), bf16, whole((WIDE, width))),
        ],
        (where, hidden, cos_wide, sin_wide, *pieces),
        scratch=[pltpu.VMEM((WIDE, width), f32)],
        flops=s["flops"],
        nbytes=s["nbytes"],
    )


def attend_kernel(len_ref, q_ref, k_ref, v_ref, *refs):
    o_ref, r_ref, e_ref = refs[-3:]
    rows = q_ref.shape[0]
    live = len_ref[0]
    low_lanes = lanes_of((1, PAIR)) < HD
    keys = k_ref[...]
    nil = jnp.zeros_like(keys)
    key_heads = (jnp.where(low_lanes, keys, nil), jnp.where(low_lanes, nil, keys))
    value_t = v_ref[...].T
    zeros = jnp.zeros((HD, rows), bf16)
    ones = jnp.ones((HD, rows), bf16)
    value_heads = (
        jnp.concatenate([value_t[:HD], zeros, ones, zeros], axis=0),
        jnp.concatenate([zeros, value_t[HD:], zeros, ones], axis=0),
    )
    key_at = lax.broadcasted_iota(i32, (TB, TB), 0)
    causal = key_at <= lax.broadcasted_iota(i32, (TB, TB), 1)
    for i in range(rows // TB):
        query = q_ref[i * TB : (i + 1) * TB, :]
        total = jnp.zeros((2 * PAIR, TB), f32)
        for head in range(2):
            blocks = []
            for j in range(i + 1):
                score = nt(key_heads[head][j * TB : (j + 1) * TB], query)
                keep = None
                if j > 0:
                    keep = key_at < live - j * TB
                if j == i:
                    keep = causal if keep is None else keep & causal
                if keep is not None:
                    score = jnp.where(keep, score, masked_score)
                blocks.append(score)
            top = jnp.max(blocks[0], axis=0, keepdims=True)
            for block in blocks[1:]:
                top = jnp.maximum(top, jnp.max(block, axis=0, keepdims=True))
            for j, block in enumerate(blocks):
                expo = jnp.exp(block - top).astype(bf16)
                e_ref[0, head, i * (i + 1) // 2 + j] = expo
                total = total + nn(value_heads[head][:, j * TB : (j + 1) * TB], expo)
        recip = 1.0 / total[PAIR:]
        o_ref[i * TB : (i + 1) * TB, :] = (total[:PAIR] * recip).T.astype(bf16)
        r_ref[i * TB : (i + 1) * TB, :] = recip.T


def attend_call(live, query, key, value, first, count, earlier=()):
    rows, width = query.shape
    pairs = width // PAIR
    steps = rows // TB
    tiles = steps * (steps + 1) // 2
    col = pl.BlockSpec((rows, PAIR), lambda p: (0, p + first))
    expo = (1, 2, tiles, TB, TB)
    return call(
        attend_kernel,
        (count,),
        [pl.BlockSpec(memory_space=pltpu.SMEM), col, col, col]
        + [pl.BlockSpec(memory_space=pl.ANY)] * len(earlier),
        [
            ((rows, width), bf16, col),
            ((rows, width), f32, col),
            ((pairs,) + expo[1:], bf16, pl.BlockSpec(expo, lambda p: (p + first, 0, 0, 0, 0))),
        ],
        (live, query, key, value, *earlier),
        flops=count * 2 * tiles * TB * TB * 8 * PAIR,
        nbytes=count * (2 * tiles * TB * TB * 2 + 12 * rows * PAIR),
        aliases={4 + at: at for at in range(len(earlier))},
    )


def attend_back_kernel(
    q_ref, k_ref, v_ref, e_ref, do_ref, att_ref, r_ref, cos_ref, sin_ref, dq_ref, dk_ref, dv_ref, dqt_ref
):
    rows = q_ref.shape[0]
    steps = rows // TB
    low_lanes = lanes_of((1, PAIR)) < HD

    def halves(x):
        nil = jnp.zeros_like(x)
        return jnp.where(low_lanes, x, nil), jnp.where(low_lanes, nil, x)

    scaled = do_ref[...].astype(f32) * r_ref[...]
    product_t = (scaled * att_ref[...].astype(f32)).T
    deltas = (
        jnp.sum(product_t[:HD], axis=0, keepdims=True),
        jnp.sum(product_t[HD:], axis=0, keepdims=True),
    )
    grad = scaled.astype(bf16)
    grad_heads = halves(grad)
    query_heads = halves(q_ref[...])
    value_heads = halves(v_ref[...])
    key_t = k_ref[...].T
    zeros = jnp.zeros((HD, rows), bf16)
    key_heads = (
        jnp.concatenate([key_t[:HD], zeros], axis=0),
        jnp.concatenate([zeros, key_t[HD:]], axis=0),
    )
    for j in range(steps):
        js = slice(j * TB, (j + 1) * TB)
        value_grad = jnp.zeros((TB, PAIR), f32)
        key_grad = jnp.zeros((TB, PAIR), f32)
        keys_t = jnp.concatenate([key_heads[0][:, js], key_heads[1][:, js]], axis=1)
        for i in range(j, steps):
            rs = slice(i * TB, (i + 1) * TB)
            tile = i * (i + 1) // 2 + j
            expos, scores = [], []
            for head in range(2):
                grad_prob = nt(value_heads[head][js], grad[rs])
                expo = e_ref[0, head, tile]
                expos.append(expo)
                scores.append(
                    (expo.astype(f32) * (grad_prob - deltas[head][:, rs])).astype(bf16)
                )
            value_grad = value_grad + nn(
                jnp.concatenate(expos, axis=1),
                jnp.concatenate([grad_heads[0][rs], grad_heads[1][rs]], axis=0),
            )
            key_grad = key_grad + nn(
                jnp.concatenate(scores, axis=1),
                jnp.concatenate([query_heads[0][rs], query_heads[1][rs]], axis=0),
            )
            add = nn(keys_t, jnp.concatenate(scores, axis=0))
            if j == 0:
                dqt_ref[:, rs] = add
            else:
                dqt_ref[:, rs] += add
        dv_ref[js, :] = value_grad.astype(bf16)
        dk_ref[js, :] = turn(key_grad, cos_ref[js, :], -sin_ref[js, :]).astype(bf16)
    query_grad = dqt_ref[...].T * (HD**-0.5)
    dq_ref[...] = turn(query_grad, cos_ref[...], -sin_ref[...]).astype(bf16)


def attend_back_call(query, key, value, expo, grad, attended, recip, cos_wide, sin_wide):
    rows, width = query.shape
    pairs, _, tiles = expo.shape[:3]
    col = pl.BlockSpec((rows, PAIR), lambda p: (0, p))
    tab = whole((rows, PAIR))
    e_spec = pl.BlockSpec((1,) + expo.shape[1:], lambda p: (p, 0, 0, 0, 0))
    return call(
        attend_back_kernel,
        (pairs,),
        [col, col, col, e_spec, col, col, col, tab, tab],
        [((rows, width), bf16, col)] * 3,
        (query, key, value, expo, grad, attended, recip, cos_wide, sin_wide),
        scratch=[pltpu.VMEM((PAIR, rows), f32)],
        flops=pairs * 2 * tiles * TB * TB * 8 * PAIR,
        nbytes=pairs * 2 * tiles * TB * TB * 2 + 22 * rows * width,
    )


def route_kernel(
    att_ref, hid_ref, grad_ref, wo_ref, sw_ref, prev_ref, gating_ref, table_ref, all_ref,
    res_ref, info_ref, rows_ref, grads_ref, nlow_ref, rg_ref,
):
    step = pl.program_id(0)
    rows = nlow_ref.shape[0]
    blocks = rows // TB
    choices = prev_ref.shape[0]

    @pl.when(step < blocks)
    def _():
        residual = hid_ref[...].astype(f32) + nn(att_ref[...], wo_ref[...])
        res_ref[...] = residual
        scale = lax.rsqrt(jnp.mean(residual * residual, axis=-1, keepdims=True) + norm_eps)
        gain = sw_ref[choices + 5 : choices + 6, :].astype(f32)
        normed = residual * scale * gain
        high, mid, low = split3(normed)
        small_weights = sw_ref[...]
        small = nt(high, small_weights) + nt(mid, small_weights) + nt(low, small_weights)
        logits = small + tn(prev_ref[...], gating_ref[...])
        cols = columns_of(table_ref)
        lane = lanes_of(logits.shape)
        is_choice = lane < choices
        masked = jnp.where(is_choice, logits, masked_score)
        expo = jnp.exp(masked - jnp.max(masked, axis=-1, keepdims=True))
        probs = expo / jnp.sum(expo, axis=-1, keepdims=True)
        wide = small.shape[1]
        partner = jnp.where(lane % 2 == 0, pltpu.roll(small, wide - 1, 1), pltpu.roll(small, 1, 1))
        top = jnp.maximum(small, partner)
        own = jnp.exp(small - top)
        alpha = own / (own + jnp.exp(partner - top))
        gates = [
            jnp.sum(jnp.where(lane == cols[:, j : j + 1], probs, 0.0), axis=-1, keepdims=True)
            for j in range(2)
        ]
        info = jnp.where(is_choice, probs, alpha)
        for at, column in enumerate((gates[0], gates[1], scale)):
            info = jnp.where(lane == choices + 4 + at, column, info)
        info_ref[...] = info
        here = pl.ds(pl.multiple_of(step * TB, TB), TB)
        nlow_ref[here, :] = high
        grad = grad_ref[...].astype(f32)
        rg_ref[0, here, :] = (gates[0] * grad).astype(bf16)
        rg_ref[1, here, :] = (gates[1] * grad).astype(bf16)

    @pl.when(step >= blocks)
    def _():
        slot = (step - blocks) * CAP + lax.broadcasted_iota(i32, (CAP, rows), 0)
        places = all_ref[...].astype(i32)
        hot = [jnp.where(places[2 + j : 3 + j] == slot, 1.0, 0.0).astype(bf16) for j in range(2)]
        rows_ref[0] = nn(hot[0] + hot[1], nlow_ref[...]).astype(bf16)
        grads_ref[0] = (nn(hot[0], rg_ref[0]) + nn(hot[1], rg_ref[1])).astype(bf16)


def route_call(attended, hidden, grad, w_out, small_weights, prev, gating, table, experts):
    rows, width = attended.shape
    blocks = rows // TB
    wide = WIDE

    def block(cols):
        return pl.BlockSpec((TB, cols), lambda i: (jnp.minimum(i, blocks - 1), 0))

    def across(count):
        return pl.BlockSpec((count, TB), lambda i: (0, jnp.minimum(i, blocks - 1)))

    return call(
        route_kernel,
        (blocks + experts,),
        [
            block(width), block(width), block(width), whole(w_out.shape),
            whole(small_weights.shape), across(prev.shape[0]), whole(gating.shape), across(8), whole(table.shape),
        ],
        [
            ((rows, width), f32, block(width)),
            ((rows, wide), f32, block(wide)),
        ]
        + [
            (
                (experts, CAP, width),
                bf16,
                pl.BlockSpec((1, CAP, width), lambda i: (jnp.maximum(i - blocks, 0), 0, 0)),
            )
        ]
        * 2,
        (attended, hidden, grad, w_out, small_weights, prev, gating, table, table),
        scratch=[pltpu.VMEM((rows, width), bf16), pltpu.VMEM((2, rows, width), bf16)],
        flops=2 * rows * width * width + 6 * experts * CAP * rows * width,
        nbytes=10 * rows * width + 2 * width * width + 4 * experts * CAP * width,
    )


def ring_order(count):
    wide = 1 << ((count.bit_length() - 1) // 2)
    tall = count // wide
    if wide < 2 or wide * tall != count or tall % 2:
        return list(range(count))
    order = [z * wide for z in range(tall)]
    for turn_at in range(tall):
        z = tall - 1 - turn_at
        across = range(1, wide) if turn_at % 2 == 0 else range(wide - 1, 0, -1)
        order.extend(z * wide + y for y in across)
    return order


def ring_send(x, order, step):
    count = len(order)
    pairs = [(order[i], order[(i + step) % count]) for i in range(count)]
    return lax.ppermute(x, "fsdp", pairs)


def swap(x, experts, bit):
    return lax.ppermute(x, "expert", [(e, e ^ bit) for e in range(experts)])


def cut(x, axis):
    size = x.shape[axis]
    half = -(-size // 32) * 16
    return lax.slice_in_dim(x, 0, half, axis=axis), lax.slice_in_dim(x, half, size, axis=axis)


def ring_gather(x, order, axis, ahead_of=()):
    count = len(order)
    half = count // 2
    pieces = [None] * count
    pieces[0] = x
    ahead, back = x, x
    for k in range(half):
        if k < len(ahead_of) and ahead_of[k]:
            ahead, back, _ = lax.optimization_barrier((ahead, back, ahead_of[k]))
        if k < half - 1:
            ahead = ring_send(ahead, order, 1)
            back = ring_send(back, order, -1)
            pieces[count - k - 1] = ahead
            pieces[k + 1] = back
    first = ring_send(cut(ahead, axis)[0], order, 1)
    second = ring_send(cut(back, axis)[1], order, -1)
    pieces[half] = jnp.concatenate([first, second], axis=axis)
    return pieces


def plus(a, b):
    return (a.astype(f32) + b.astype(f32)).astype(bf16)


class RingReduce:
    def __init__(self, parts, order, axis):
        self.parts, self.order, self.axis = parts, order, axis
        self.left = len(order) // 2 - 1
        self.flight = None

    def start(self):
        first, second = cut(self.parts[len(self.order) // 2], self.axis)
        self.flight = (ring_send(first, self.order, 1), ring_send(second, self.order, -1))

    def add(self):
        k, axis = self.left, self.axis
        ahead, back = self.flight
        mine, other = self.parts[k], self.parts[len(self.order) - k]
        if k == len(self.order) // 2 - 1:
            low, high = cut(mine, axis)
            mine = jnp.concatenate([plus(low, ahead), high], axis=axis)
            low, high = cut(other, axis)
            other = jnp.concatenate([low, plus(high, back)], axis=axis)
        else:
            mine, other = plus(mine, ahead), plus(other, back)
        self.ready = (mine, other)
        self.left = k - 1

    def send(self):
        mine, other = self.ready
        self.flight = (ring_send(mine, self.order, 1), ring_send(other, self.order, -1))

    def turn(self):
        self.add()
        self.send()

    def finish(self):
        return finish_experts_call(self.parts[0], *self.flight)

    def result(self):
        return self.parts[0].astype(f32) + self.flight[0].astype(f32) + self.flight[1].astype(f32)


def fetch_chunks(pieces, buf, sems):
    step = pl.program_id(0)
    units = pieces[0].shape[1]
    steps = len(pieces) // 2

    def copies(at, slot):
        return [
            pltpu.make_async_copy(
                pieces[2 * at + side], buf.at[slot, :, pl.ds(side * units, units), :], sems.at[side, slot]
            )
            for side in range(2)
        ]

    @pl.when(step == 0)
    def _():
        for copy in copies(0, 0):
            copy.start()

    for at in range(steps):

        @pl.when(step == at)
        def _():
            if at + 1 < steps:
                for copy in copies(at + 1, (at + 1) % 2):
                    copy.start()
            for copy in copies(at, at % 2):
                copy.wait()

    return buf.at[lax.rem(step, 2)]


def accumulate(acc_ref, out, final):
    step = pl.program_id(0)

    @pl.when(step == 0)
    def _():
        acc_ref[...] = out

    @pl.when(step > 0)
    def _():
        acc_ref[...] += out

    @pl.when(step == pl.num_programs(0) - 1)
    def _():
        final[...] = acc_ref[...].astype(bf16).reshape(final.shape)


def expert_kernel(x_ref, *refs):
    pieces, (y_ref, inner_ref, fa_ref, fb_ref, acc_ref, buf, sems) = refs[:-7], refs[-7:]
    weights = fetch_chunks(pieces, buf, sems)
    rows_in = x_ref[...].reshape(acc_ref.shape[0], x_ref.shape[2])
    gate = nt(rows_in, weights[0])
    up = nt(rows_in, weights[1])
    sig = 0.5 * jnp.tanh(0.5 * gate) + 0.5
    act = gate * sig
    inner = (act * up).astype(bf16)
    inner_ref[0] = inner
    fa_ref[0] = (up * (sig + act * (1.0 - sig))).astype(bf16)
    fb_ref[0] = act.astype(bf16)
    accumulate(acc_ref, nn(inner, weights[2]), y_ref)


def expert_back_kernel(g_ref, fa_ref, fb_ref, *refs):
    pieces, (dx_ref, dgu_ref, acc_ref, buf, sems) = refs[:-5], refs[-5:]
    weights = fetch_chunks(pieces, buf, sems)
    grad_in = g_ref[...].reshape(acc_ref.shape[0], g_ref.shape[2])
    grad_inner = nt(grad_in, weights[2])
    grads = jnp.concatenate(
        [(grad_inner * ref[0].astype(f32)).astype(bf16) for ref in (fa_ref, fb_ref)], axis=1
    )
    dgu_ref[0] = grads
    both = weights[0:2].reshape(grads.shape[1], grad_in.shape[1])
    accumulate(acc_ref, nn(grads, both), dx_ref)


def expert_weights_kernel(x_ref, dgu_ref, *dw_refs):
    step = pl.program_id(0)
    rows_in = x_ref[...].reshape(dgu_ref.shape[1], x_ref.shape[2])
    units = dw_refs[0].shape[1]
    term = tn(dgu_ref[0], rows_in).astype(bf16)
    for at in range(len(dw_refs) // 2):

        @pl.when(step == at)
        def _():
            for side in range(2):
                for part in range(2):
                    row = (2 * part + side) * units
                    dw_refs[2 * at + side][part] = term[row : row + units]


def expert_down_kernel(order_ref, g_ref, inner_ref, dw_ref, term_ref):
    del order_ref
    step = pl.program_id(0)
    units = dw_ref.shape[1]

    @pl.when(step % 2 == 0)
    def _():
        grad_in = g_ref[...].reshape(inner_ref.shape[1], g_ref.shape[2])
        term_ref[...] = tn(inner_ref[0], grad_in).astype(bf16)
        dw_ref[0] = term_ref[:units, :]

    @pl.when(step % 2 == 1)
    def _():
        dw_ref[0] = term_ref[units:, :]


def expert_specs(sent, pieces):
    experts, _, width = sent.shape
    chunks = len(pieces)
    units = pieces[0].shape[1]
    rows = experts * CAP
    return dict(
        rows=rows,
        chunks=chunks,
        steps=chunks // 2,
        units=units,
        width=width,
        any=[pl.BlockSpec(memory_space=pl.ANY)] * chunks,
        x=pl.BlockSpec((experts, CAP, width), lambda c: (0, 0, 0)),
        unit=pl.BlockSpec((1, rows, 2 * units), lambda c: (c, 0, 0)),
        pair=pl.BlockSpec((1, rows, 4 * units), lambda c: (c, 0, 0)),
        flops=6 * rows * width * chunks * units,
        nbytes=6 * chunks * units * (rows + width) + 4 * rows * width,
        scratch=[
            pltpu.VMEM((rows, width), f32),
            pltpu.VMEM((2, 3, 2 * units, width), bf16),
            pltpu.SemaphoreType.DMA((2, 2)),
        ],
    )


def expert_call(sent, pieces):
    s = expert_specs(sent, pieces)
    hidden = ((s["steps"], s["rows"], 2 * s["units"]), bf16, s["unit"])
    return call(
        expert_kernel,
        (s["steps"],),
        [s["x"], *s["any"]],
        [(sent.shape, bf16, s["x"]), hidden, hidden, hidden],
        (sent, *pieces),
        scratch=s["scratch"],
        flops=s["flops"],
        nbytes=s["nbytes"],
    )


def expert_back_call(sent, pieces, factor_a, factor_b):
    s = expert_specs(sent, pieces)
    return call(
        expert_back_kernel,
        (s["steps"],),
        [s["x"], s["unit"], s["unit"], *s["any"]],
        [
            (sent.shape, bf16, s["x"]),
            ((s["steps"], s["rows"], 4 * s["units"]), bf16, s["pair"]),
        ],
        (sent, factor_a, factor_b, *pieces),
        scratch=s["scratch"],
        flops=s["flops"],
        nbytes=s["nbytes"],
    )


def expert_weights_call(sent, dgu, pieces, first, count):
    s = expert_specs(sent, pieces)
    shape = (2,) + pieces[0].shape[1:]
    return call(
        expert_weights_kernel,
        (count,),
        [s["x"], pl.BlockSpec((1, s["rows"], 4 * s["units"]), lambda c: (first + c, 0, 0))],
        [(shape, bf16, whole(shape))] * (2 * count),
        (sent, dgu),
        flops=8 * s["rows"] * s["width"] * count * s["units"],
        nbytes=s["nbytes"] // 2,
    )


def expert_down_call(chunk_order, sent_grads, inner, pieces):
    s = expert_specs(sent_grads, pieces)
    shape = (s["chunks"], s["units"], s["width"])
    return pl.pallas_call(
        expert_down_kernel,
        name="expert_down_kernel",
        grid_spec=pltpu.PrefetchScalarGridSpec(
            num_scalar_prefetch=1,
            grid=(s["chunks"],),
            in_specs=[
                pl.BlockSpec(sent_grads.shape, lambda c, o: (0, 0, 0)),
                pl.BlockSpec((1, s["rows"], 2 * s["units"]), lambda c, o: (c // 2, 0, 0)),
            ],
            out_specs=pl.BlockSpec((1,) + shape[1:], lambda c, o: (o[c], 0, 0)),
            scratch_shapes=[pltpu.VMEM((2 * s["units"], s["width"]), bf16)],
        ),
        out_shape=jax.ShapeDtypeStruct(shape, bf16),
        compiler_params=pltpu.CompilerParams(
            dimension_semantics=("arbitrary",), vmem_limit_bytes=60 << 20
        ),
        cost_estimate=pl.CostEstimate(
            flops=int(2 * s["rows"] * s["width"] * s["chunks"] * s["units"] * SLOW),
            bytes_accessed=s["nbytes"] // 2,
            transcendentals=0,
        ),
    )(chunk_order, sent_grads, inner)


def combine_kernel(
    y_ref, res_ref, info_ref, table_ref, grad_ref, sw_ref, prev_ref, gating_ref,
    out_ref, part_ref, gprev_ref, gsw_ref, gvec_ref, ggat_ref,
):
    step = pl.program_id(0)
    choices = prev_ref.shape[0]
    experts = y_ref.shape[0]
    cols = columns_of(table_ref)
    slots = experts * CAP
    rows_out = y_ref[...].reshape(slots, y_ref.shape[2])
    residual = res_ref[...]
    info = info_ref[...]
    lane = lanes_of(info.shape)

    def column(at):
        return info[:, at : at + 1]

    gates = (column(choices + 4), column(choices + 5))
    small_weights = sw_ref[...]
    gain = small_weights[choices + 5 : choices + 6].astype(f32)
    normed = residual * column(choices + 6) * gain
    grad = grad_ref[...].astype(f32)
    vectors = [small_weights[choices + 6 + c : choices + 7 + c].astype(f32) for c in range(2)]
    dots = nt(grad_ref[...], small_weights)
    alphas = ((column(choices), column(choices + 1)), (column(choices + 2), column(choices + 3)))
    dot_normed = jnp.sum(grad * normed, axis=-1, keepdims=True)
    dot_vectors = [dots[:, choices + 6 + c : choices + 7 + c] for c in range(2)]
    mixed = residual
    weight_normed = jnp.zeros_like(dot_normed)
    weight_copy = jnp.zeros_like(dot_normed)
    weight_const = [jnp.zeros_like(dot_normed), jnp.zeros_like(dot_normed)]
    grad_probs = jnp.zeros_like(info)
    slot = lanes_of((TB, slots))
    for j in range(2):
        route = cols[:, j : j + 1]
        hot = jnp.where(cols[:, 2 + j : 3 + j] == slot, 1.0, 0.0).astype(bf16)
        rows_j = nn(hot, rows_out)
        is_copy = jnp.where(route == experts + 1, 1.0, 0.0)
        is_const = [jnp.where(route == experts + 2 + c, 1.0, 0.0) for c in range(2)]
        on_normed = is_copy + is_const[0] * alphas[0][0] + is_const[1] * alphas[1][0]
        grad_gate = jnp.sum(grad * rows_j, axis=-1, keepdims=True) + on_normed * dot_normed
        for c in range(2):
            grad_gate = grad_gate + is_const[c] * alphas[c][1] * dot_vectors[c]
            weight_const[c] = weight_const[c] + gates[j] * is_const[c]
        grad_probs = grad_probs + jnp.where(lane == route, grad_gate, 0.0)
        mixed = mixed + gates[j] * rows_j
        weight_normed = weight_normed + gates[j] * on_normed
        weight_copy = weight_copy + gates[j] * is_copy
    mixed = mixed + weight_normed * normed
    for c in range(2):
        mixed = mixed + weight_const[c] * alphas[c][1] * vectors[c]
    out_ref[...] = mixed.astype(bf16)
    is_choice = lane < choices
    probs = jnp.where(is_choice, info, 0.0)
    grad_small = probs * (grad_probs - jnp.sum(probs * grad_probs, axis=-1, keepdims=True))
    direct = weight_copy
    coefs = jnp.zeros_like(info)
    for c in range(2):
        grad_alpha = (weight_const[c] * dot_normed, weight_const[c] * dot_vectors[c])
        mean = alphas[c][0] * grad_alpha[0] + alphas[c][1] * grad_alpha[1]
        for k in range(2):
            grad_small = jnp.where(
                lane == choices + 2 * c + k, alphas[c][k] * (grad_alpha[k] - mean), grad_small
            )
        direct = direct + alphas[c][0] * weight_const[c]
        coefs = jnp.where(lane == c, alphas[c][1] * weight_const[c], coefs)
    high, mid, low = split3(grad_small)
    part_ref[...] = direct * grad + (
        nn(high, small_weights) + nn(mid, small_weights) + nn(low, small_weights)
    )
    gating = gating_ref[...]
    gprev_ref[...] = nt(gating, high) + nt(gating, mid) + nt(gating, low)
    normed_high, normed_mid = split2(normed)
    grad_sw = tn(high, normed_high) + tn(mid, normed_high) + tn(high, normed_mid)
    coef_high, coef_mid = split2(coefs)
    grad_vec = tn(coef_high, grad_ref[...]) + tn(coef_mid, grad_ref[...])
    prev = prev_ref[...]
    grad_gating = nn(prev, high) + nn(prev, mid) + nn(prev, low)

    @pl.when(step == 0)
    def _():
        gsw_ref[...] = grad_sw
        gvec_ref[...] = grad_vec
        ggat_ref[...] = grad_gating

    @pl.when(step > 0)
    def _():
        gsw_ref[...] += grad_sw
        gvec_ref[...] += grad_vec
        ggat_ref[...] += grad_gating


def combine_call(back, residual, info, table, grad, small_weights, prev, gating):
    rows, width = residual.shape
    wide = info.shape[1]
    choices = prev.shape[0]
    slots = back.shape[0] * CAP

    def block(cols):
        return pl.BlockSpec((TB, cols), lambda i: (i, 0))

    def across(count):
        return pl.BlockSpec((count, TB), lambda i: (0, i))

    return call(
        combine_kernel,
        (rows // TB,),
        [
            whole(back.shape), block(width), block(wide), across(8), block(width),
            whole(small_weights.shape), across(choices), whole(gating.shape),
        ],
        [
            ((rows, width), bf16, block(width)),
            ((rows, width), f32, block(width)),
            ((choices, rows), f32, across(choices)),
            ((wide, width), f32, whole((wide, width))),
            ((wide, width), f32, whole((wide, width))),
            ((choices, wide), f32, whole((choices, wide))),
        ],
        (back, residual, info, table, grad, small_weights, prev, gating),
        flops=4 * slots * rows * width,
        nbytes=14 * rows * width + 2 * slots * width,
    )


def residual_kernel(
    gain_at, dx_ref, part_ref, res_ref, table_ref, grad_ref, sw_ref, wo_ref, att_ref,
    gres_ref, gatt_ref, gwo_ref, ggain_ref, acc_ref,
):
    step = pl.program_id(0)
    experts = dx_ref.shape[0]
    slots = experts * CAP
    slot = lanes_of((TB, slots))
    cols = columns_of(table_ref)
    hot = jnp.where((cols[:, 2:3] == slot) | (cols[:, 3:4] == slot), 1.0, 0.0).astype(bf16)
    grad_normed = part_ref[...] + nn(hot, dx_ref[...].reshape(slots, dx_ref.shape[2]))
    residual = res_ref[...]
    scale = lax.rsqrt(jnp.mean(residual * residual, axis=-1, keepdims=True) + norm_eps)
    unit = residual * scale
    grad_gain = jnp.sum(grad_normed * unit, axis=0, keepdims=True)
    scaled = grad_normed * sw_ref[gain_at : gain_at + 1, :].astype(f32)
    grad_residual = grad_ref[...].astype(f32) + scale * (
        scaled - unit * jnp.mean(scaled * unit, axis=-1, keepdims=True)
    )
    gres_ref[...] = grad_residual
    low = grad_residual.astype(bf16)
    gatt_ref[...] = nt(low, wo_ref[...]).astype(bf16)
    grad_out = tn(att_ref[...], low)

    @pl.when(step == 0)
    def _():
        acc_ref[...] = grad_out
        ggain_ref[...] = grad_gain

    @pl.when(step > 0)
    def _():
        acc_ref[...] += grad_out
        ggain_ref[...] += grad_gain

    @pl.when(step == pl.num_programs(0) - 1)
    def _():
        gwo_ref[...] = acc_ref[...].astype(bf16)


def residual_call(dx, part, residual, table, grad, small_weights, gain_at, w_out, attended):
    rows, width = residual.shape
    slots = dx.shape[0] * CAP

    def block(cols):
        return pl.BlockSpec((TB, cols), lambda i: (i, 0))

    return call(
        functools.partial(residual_kernel, gain_at),
        (rows // TB,),
        [
            whole(dx.shape), block(width), block(width), pl.BlockSpec((8, TB), lambda i: (0, i)), block(width),
            whole(small_weights.shape),
            whole(w_out.shape), block(width),
        ],
        [
            ((rows, width), f32, block(width)),
            ((rows, width), bf16, block(width)),
            ((width, width), bf16, whole((width, width))),
            ((1, width), f32, whole((1, width))),
        ],
        (dx, part, residual, table, grad, small_weights, w_out, attended),
        scratch=[pltpu.VMEM((width, width), f32)],
        flops=2 * slots * rows * width + 4 * rows * width * width,
        nbytes=18 * rows * width + 2 * slots * width,
    )


def qkv_weights_kernel(
    gain_at, where_ref, dq_ref, dk_ref, dv_ref, n_ref, w_ref, small_ref, gwo_ref, ggain_ref, gsw_ref, gvec_ref,
    ggat_ref, own_ref, other_ref, acc_ref,
):
    step = pl.program_id(0)
    count, _, width = own_ref.shape
    part = width // count
    half = part // 2
    shards = dq_ref.shape[1] // part
    normed = n_ref[...]
    core = where_ref[count]
    gain_grad = jnp.zeros((1, width), f32)

    def put(side, shard, at, value):
        rel = where_ref[count + 1 + shard]

        @pl.when(core == side)
        def _():
            own_ref[rel, at : at + value.shape[0], :] = value

        @pl.when(core != side)
        def _():
            other_ref[rel, at : at + value.shape[0], :] = value

    for at, ref in enumerate((dq_ref, dk_ref, dv_ref, None)):
        if ref is None:
            term = gwo_ref[...]
        else:
            full = tn(ref[...], normed)
            gain_grad = gain_grad + jnp.sum(full * w_ref[at].astype(f32), axis=0, keepdims=True)
            term = full.astype(bf16)
        for m in range(shards):
            for side in range(2):
                row = m * part + side * half
                put(side, step * shards + m, at * half, term[row : row + half])

    @pl.when(step == 0)
    def _():
        acc_ref[...] = gain_grad

    @pl.when(step > 0)
    def _():
        acc_ref[...] += gain_grad

    @pl.when(step == pl.num_programs(0) - 1)
    def _():
        gain_one = acc_ref[...] / small_ref[gain_at : gain_at + 1, :].astype(f32)
        vectors = jnp.concatenate(
            [gsw_ref[:gain_at, :], gain_one, ggain_ref[...], gvec_ref[:2, :]], axis=0
        )
        gating_high = ggat_ref[...].astype(bf16).astype(f32)
        gating = (gating_high, ggat_ref[...] - gating_high)
        lanes = lanes_of((1, width)) < part
        split = vectors.shape[0] // 2
        spare = jnp.zeros((16 - split - 1, width), f32)
        for m in range(count):
            here = vectors if m == 0 else pltpu.roll(vectors, width - m * part, 1)
            here = jnp.where(lanes, here, 0.0)
            for side in range(2):
                block = jnp.concatenate(
                    [here[side * split : (side + 1) * split], gating[side], spare], axis=0
                )
                put(side, m, 4 * half, block.astype(bf16))


def qkv_weights_call(where, dq, dk, dv, normed, weights, small, gain_at, gwo, ggain, gsw, gvec, ggat, count):
    rows, width = normed.shape
    steps = 2
    cols = width // steps
    col = pl.BlockSpec((rows, cols), lambda c: (0, c))
    part = width // count
    shape = (count, 2 * part + 16, width)
    return call(
        functools.partial(qkv_weights_kernel, gain_at),
        (steps,),
        [
            pl.BlockSpec(memory_space=pltpu.SMEM), col, col, col, whole(normed.shape),
            pl.BlockSpec((3, cols, width), lambda c: (0, c, 0)), whole(small.shape),
            pl.BlockSpec((cols, width), lambda c: (c, 0)), whole(ggain.shape), whole(gsw.shape), whole(gvec.shape),
            whole(ggat.shape),
        ],
        [(shape, bf16, whole(shape))] * 2,
        (where, dq, dk, dv, normed, weights, small, gwo, ggain, gsw, gvec, ggat),
        scratch=[pltpu.VMEM((1, width), f32)],
        flops=6 * rows * width * width,
        nbytes=8 * rows * width + 18 * width * width,
    )


def finish_kernel(
    choices, where_ref, mine_ref, theirs_ref, gq_ref, gk_ref, gv_ref, gwo_ref, g1_ref, g2_ref, router_ref, gat_ref,
    const_ref, vec_ref,
):
    part, width = gwo_ref.shape
    half = part // 2
    core = where_ref[where_ref.shape[0] // 2]

    def side(which, at, size):
        first = mine_ref[at : at + size, :].astype(f32)
        second = theirs_ref[at : at + size, :].astype(f32)
        return jnp.where(core == which, first, second)

    for at, ref in enumerate((gq_ref, gk_ref, gv_ref, gwo_ref)):
        both = jnp.concatenate([side(0, at * half, half), side(1, at * half, half)], axis=0)
        ref[...] = both
    split = (choices + 8) // 2
    low, high = side(0, 4 * half, 16), side(1, 4 * half, 16)
    small = jnp.concatenate([low[:split, :WIDE], high[:split, :WIDE]], axis=0)
    router_ref[...] = small[:choices, :part]
    const_ref[...] = small[choices : choices + 4, :part]
    g1_ref[...] = small[choices + 4 : choices + 5, :part]
    g2_ref[...] = small[choices + 5 : choices + 6, :part]
    vec_ref[...] = small[choices + 6 : choices + 8, :part]
    gating = (low + high)[split : split + 1, :]
    for at in range(choices):
        moved = gating if at == 0 else pltpu.roll(gating, width - at * choices, 1)
        gat_ref[at : at + 1, :] = moved[:, :choices]


def finish_call(where, mine, theirs, part, choices):
    width = mine.shape[1]
    outs = [(part, width)] * 4 + [
        (1, part), (1, part), (choices, part), (choices, choices), (4, part), (2, part),
    ]
    return call(
        functools.partial(finish_kernel, choices),
        (1,),
        [pl.BlockSpec(memory_space=pltpu.SMEM), whole(mine.shape), whole(mine.shape)],
        [(shape, f32, whole(shape)) for shape in outs],
        (where, mine, theirs),
        flops=1 << 20,
        nbytes=20 * part * width,
    )


def plain_weights_kernel(dq_ref, dk_ref, dv_ref, n_ref, out_ref):
    normed = n_ref[...]
    for part, ref in enumerate((dq_ref, dk_ref, dv_ref)):
        out_ref[part] = tn(ref[...], normed)


def plain_weights_call(dq, dk, dv, normed):
    rows, width = normed.shape
    col = pl.BlockSpec((rows, 256), lambda c: (0, c))
    return call(
        plain_weights_kernel,
        (width // 256,),
        [col, col, col, whole((rows, width))],
        [((3, width, width), f32, pl.BlockSpec((3, 256, width), lambda c: (0, c, 0)))],
        (dq, dk, dv, normed),
        flops=6 * rows * width * width,
        nbytes=8 * rows * width + 12 * width * width,
    )[0]


def hidden_kernel(gain_at, dq_ref, dk_ref, dv_ref, w_ref, hid_ref, small_ref, gres_ref, *refs):
    out_ref = refs[-1]
    grad_normed = nn(dq_ref[...], w_ref[0]) + nn(dk_ref[...], w_ref[1]) + nn(dv_ref[...], w_ref[2])
    hidden = hid_ref[...].astype(f32)
    scale = lax.rsqrt(jnp.mean(hidden * hidden, axis=-1, keepdims=True) + norm_eps)
    unit = hidden * scale
    scaled = grad_normed * small_ref[gain_at : gain_at + 1, :].astype(f32)
    out_ref[...] = gres_ref[...] + scale * (
        scaled - unit * jnp.mean(scaled * unit, axis=-1, keepdims=True)
    )


def hidden_call(dq, dk, dv, weights, hidden, small, gain_at, grad_residual, first, count, earlier=()):
    rows, width = hidden.shape
    row = pl.BlockSpec((TB, width), lambda i: (i + first, 0))
    return call(
        functools.partial(hidden_kernel, gain_at),
        (count,),
        [row, row, row, whole(weights.shape), row, whole(small.shape), row]
        + [pl.BlockSpec(memory_space=pl.ANY)] * len(earlier),
        [((rows, width), f32, row)],
        (dq, dk, dv, weights, hidden, small, grad_residual, *earlier),
        flops=6 * count * TB * width * width,
        nbytes=16 * count * TB * width + 6 * width * width,
        aliases={7: 0} if earlier else None,
    )


def rope_wide(length):
    inverse = rope_base ** (-(2.0 * jnp.arange(HD // 2, dtype=f32)) / HD)
    angles = jnp.arange(length, dtype=f32)[:, None] * inverse[None, :]
    cosine, sine = jnp.cos(angles), jnp.sin(angles)
    return (
        jnp.concatenate([cosine] * 4, axis=1),
        jnp.concatenate([-sine, sine, -sine, sine], axis=1),
    )


def to_rows(flat, width):
    count = -(-flat.shape[1] // width)
    return jnp.pad(flat, ((0, 0), (0, count * width - flat.shape[1]))).reshape(
        flat.shape[0], count, width
    )


def per_device(
    hidden_in,
    prev_logits,
    seq_lengths,
    seq_order,
    routes,
    w_query,
    w_key,
    w_value,
    w_output,
    gain_attn,
    gain_moe,
    w_router,
    w_gating,
    w_const,
    v_const,
    w_gate,
    w_up,
    w_down,
    out_grad,
):
    rows, width = hidden_in.shape[1:]
    experts = lax.axis_size("expert")
    shards = lax.axis_size("fsdp")
    choices = w_router.shape[1]
    part = width // shards
    hidden = hidden_in.reshape(rows, width)
    grad = out_grad.reshape(rows, width)
    prev = prev_logits.reshape(rows, choices).T

    fsdp_here = lax.axis_index("fsdp")
    own = lax.axis_index("expert") * shards + fsdp_here
    live = lax.dynamic_slice(seq_lengths, (own,), (1,))
    dealt = lax.all_gather(routes.reshape(rows, 2).T, "expert", axis=0, tiled=False)
    peers = jnp.arange(experts, dtype=i32) * shards + fsdp_here
    table = deal_call((seq_order[peers] == own).astype(i32), dealt)
    cos_wide, sin_wide = rope_wide(rows)

    gain_at = choices + 4
    small_count = choices + 8
    order = ring_order(shards)
    place = jnp.asarray([order.index(m) for m in range(shards)], dtype=i32)
    spot = place[fsdp_here]
    core = lax.rem(lax.axis_index("expert"), 2)
    paired = part % 32 == 0 and small_count == 16 and shards % 2 == 0 and experts & (experts - 1) == 0
    ring = jnp.asarray(order, dtype=i32)
    where = jnp.concatenate(
        [ring[(spot + jnp.arange(shards, dtype=i32)) % shards], core[None], (place - spot) % shards]
    )
    expert_pack = pack_experts_call(w_gate, w_up, w_down)
    if paired:
        pack, spare = pack_call(
            core[None], w_query.T, w_key.T, w_value.T, w_output, w_router.T, w_const.T, gain_attn[None], gain_moe[None], v_const
        )
        own = ring_gather(pack, order, 0, [(), (cos_wide, sin_wide), (dealt,), (expert_pack, table)])
        other = [spare] + [swap(piece, experts, 1) for piece in own[1:]]
        expert_pack, _ = lax.optimization_barrier((expert_pack, own[shards // 2]))
        query, key, value, normed_one, qkv_weights, w_out, small = qkv_pieces_call(
            hidden, where, own, other, gain_at, part, cos_wide, sin_wide
        )
    else:
        small_parts = jnp.concatenate(
            [w_router.T, w_const.T, gain_attn[None], gain_moe[None], v_const], axis=0
        )
        first_pack = jnp.concatenate(
            [w_query.T, w_key.T, w_value.T, to_rows(small_parts.reshape(1, -1), width)[0]], axis=0
        )
        first = lax.all_gather(first_pack, "fsdp", axis=0, tiled=False)
        w_out = lax.all_gather(w_output, "fsdp", axis=0, tiled=True)
        qkv_weights = (
            first[:, : 3 * part]
            .reshape(shards, 3, part, width)
            .transpose(1, 0, 2, 3)
            .reshape(3, width, width)
        )
        small = (
            first[:, 3 * part :]
            .reshape(shards, -1)[:, : small_count * part]
            .reshape(shards, small_count, part)
            .transpose(1, 0, 2)
            .reshape(small_count, width)
        )
        small = jnp.pad(small, ((0, WIDE - small_count), (0, 0)))
        query, key, value, normed_one = qkv_call(
            hidden, small, gain_at, qkv_weights, cos_wide, sin_wide
        )
    pairs = width // PAIR
    some = pairs // 2
    early = attend_call(live, query, key, value, 0, some)
    expert_weights = ring_gather(expert_pack, order, 1, [()] + [early[:1]])
    farthest = shards // 2
    turns = [farthest, 0] + [r for k in range(farthest - 1, 0, -1) for r in (k, shards - k)]
    by_turn = [expert_weights[r] for r in turns]

    def after(value, step):
        if step >= farthest:
            return value
        return lax.optimization_barrier((value, expert_weights[step], expert_weights[-step]))[0]

    gating_wide = jnp.pad(w_gating, ((0, 0), (0, WIDE - choices)))

    attended, recip, expo = attend_call(
        live, after(query, 1), key, value, some, pairs - some, early
    )
    residual, info, send_rows, send_grads = route_call(
        after(attended, 2), hidden, grad, w_out, small, prev, gating_wide, table, experts
    )
    sent = lax.all_to_all(send_rows, "expert", split_axis=0, concat_axis=0, tiled=True)
    sent_grads = lax.all_to_all(
        after(send_grads, 3), "expert", split_axis=0, concat_axis=0, tiled=True
    )
    chunk_order = where[jnp.asarray(turns, dtype=i32)]
    expert_out, inner, factor_a, factor_b = expert_call(sent, by_turn)
    returned = lax.all_to_all(expert_out, "expert", split_axis=0, concat_axis=0, tiled=True)
    expert_dx, dgu = expert_back_call(sent_grads, by_turn, factor_a, factor_b)
    returned_dx = lax.all_to_all(expert_dx, "expert", split_axis=0, concat_axis=0, tiled=True)
    lead = min(2, shards // 2)
    expert_dw = [None] * shards
    terms = expert_weights_call(sent, dgu, by_turn, 0, lead)
    for at, term in enumerate(terms):
        expert_dw[turns[at]] = term
    inner, _ = lax.optimization_barrier((inner, terms))
    grad_down = expert_down_call(chunk_order, sent_grads, inner, by_turn)
    down_total = lax.psum_scatter(grad_down, "fsdp", scatter_dimension=0, tiled=False)
    sums = RingReduce(expert_dw, order, 1)
    sums.start()
    sums.add()
    sums.ready, _ = lax.optimization_barrier((sums.ready, grad_down))
    dgu, sums.ready = lax.optimization_barrier((dgu, sums.ready))
    sums.send()
    for at, term in enumerate(expert_weights_call(sent, dgu, by_turn, lead, shards // 2 - lead)):
        expert_dw[turns[2 * lead + at]] = term

    def before(value):
        if not sums.left:
            return value
        sums.add()
        value, sums.ready = lax.optimization_barrier((value, sums.ready))
        sums.send()
        return value

    returned, _ = lax.optimization_barrier((returned, expert_dw))
    hidden_out, part_grad, grad_prev, grad_sw, grad_vec, grad_gating = combine_call(
        returned, residual, info, table, grad, small, prev, gating_wide
    )
    grad_residual, grad_attended, grad_wo, grad_gain_two = residual_call(
        returned_dx, before(part_grad), residual, table, grad, small, gain_at + 1, w_out, attended
    )
    dq, dk, dv = attend_back_call(
        query, key, value, expo, before(grad_attended), attended, recip, cos_wide, sin_wide
    )
    while sums.left:
        sums.turn()
    dq, sums.flight, down_total = lax.optimization_barrier((dq, sums.flight, down_total))
    blocks = rows // TB
    last = (qkv_weights, hidden, small, gain_at, grad_residual)
    grad_hidden = hidden_call(dq, dk, dv, *last, 0, blocks // 2)
    if paired:
        own, other = qkv_weights_call(
            where, dq, dk, dv, normed_one, qkv_weights, small, gain_at, grad_wo, grad_gain_two, grad_sw, grad_vec,
            jnp.pad(grad_gating[:, :choices].reshape(1, -1), ((0, 0), (0, width - choices * choices))), shards,
        )
        got = swap(other, experts, 1)
        shared = RingReduce([plus(own[r], got[r]) for r in range(shards)], order, 0)
        shared.start()
        shared.add()
        expert_grads = sums.finish()
        shared.ready, expert_grads, grad_hidden = lax.optimization_barrier(
            (shared.ready, expert_grads, grad_hidden)
        )
        shared.send()
        grad_hidden = hidden_call(dq, dk, dv, *last, blocks // 2, blocks - blocks // 2, grad_hidden)
        while shared.left:
            shared.add()
            shared.ready, grad_hidden = lax.optimization_barrier((shared.ready, grad_hidden))
            shared.send()
        mine = shared.result().astype(bf16)
        bit = 2
        while bit < experts:
            mine = plus(mine, swap(mine, experts, bit))
            bit *= 2
        theirs = swap(mine, experts, 1)
        shared_grads = finish_call(where, mine, theirs, part, choices)
        shared_grads = [
            g[0] if at in (4, 5) else g.T if at in (0, 1, 2, 6, 8) else g
            for at, g in enumerate(shared_grads)
        ]
    else:
        grad_qkv = plain_weights_call(dq, dk, dv, normed_one)
        grad_gain_one = jnp.sum(grad_qkv * qkv_weights.astype(f32), axis=(0, 1))[None] / small[
            gain_at : gain_at + 1
        ].astype(f32)
        small_grads = jnp.concatenate(
            [grad_sw[:gain_at], grad_gain_one, grad_gain_two, grad_vec[:2]], axis=0
        )
        small_flat = (
            small_grads.reshape(small_count, shards, part).transpose(1, 0, 2).reshape(shards, -1)
        )
        gating_flat = grad_gating[:, :choices].reshape(1, -1)
        gating_both = jnp.concatenate(split2(gating_flat), axis=1)
        flat = jnp.concatenate(
            [small_flat.astype(bf16), jnp.broadcast_to(gating_both, (shards, gating_both.shape[1]))], axis=1
        )
        shared = jnp.concatenate(
            [
                grad_qkv.astype(bf16)
                .reshape(3, shards, part, width)
                .transpose(1, 0, 2, 3)
                .reshape(shards, 3 * part, width),
                grad_wo.reshape(shards, part, width),
                to_rows(flat, width),
            ],
            axis=1,
        )
        scattered = lax.psum_scatter(shared, "fsdp", scatter_dimension=0, tiled=False)
        total = lax.psum(scattered, "expert").astype(f32)
        flat_total = total[4 * part :].reshape(-1)
        small_total = flat_total[: small_count * part].reshape(small_count, part)
        at = small_count * part
        gating_total = flat_total[at : at + 2 * choices * choices].reshape(2, choices, choices)
        shared_grads = [total[at * part : (at + 1) * part].T for at in range(3)] + [
            total[3 * part : 4 * part],
            small_total[gain_at],
            small_total[gain_at + 1],
            small_total[:choices].T,
            jnp.sum(gating_total, axis=0),
            small_total[choices:gain_at].T,
            small_total[gain_at + 2 :],
        ]
        expert_grads = sums.finish()
        grad_hidden = hidden_call(dq, dk, dv, *last, blocks // 2, blocks - blocks // 2, grad_hidden)
    down_total = down_total.astype(f32)[None]
    return (hidden_out[None], grad_hidden[0][None], grad_prev.T[None], *shared_grads, *expert_grads, down_total)


def solution(mesh):
    rows = P(("expert", "fsdp"), None, None)
    ins = (
        rows, rows, P(), P(), rows,
        P(None, "fsdp"), P(None, "fsdp"), P(None, "fsdp"), P("fsdp", None),
        P("fsdp"), P("fsdp"), P("fsdp", None), P(), P("fsdp", None), P(None, "fsdp"),
        P("expert", None, "fsdp"), P("expert", None, "fsdp"), P("expert", "fsdp", None), rows,
    )
    outs = (
        rows, rows, rows,
        P(None, "fsdp"), P(None, "fsdp"), P(None, "fsdp"), P("fsdp", None),
        P("fsdp"), P("fsdp"), P("fsdp", None), P(), P("fsdp", None), P(None, "fsdp"),
        P("expert", None, "fsdp"), P("expert", None, "fsdp"), P("expert", "fsdp", None),
    )
    return jax.shard_map(per_device, mesh=mesh, in_specs=ins, out_specs=outs, check_vma=False)
```

```python
import functools

import jax
import jax.numpy as jnp
from jax import lax
from jax.experimental import pallas as pl
from jax.experimental.pallas import tpu as pltpu
from jax.sharding import PartitionSpec as P

HD = 64
CAP = 256
TB = 256
PAIR = 2 * HD
WIDE = 128
SLOW = 3.0
norm_eps = 1e-05
rope_base = 10000.0
masked_score = -1e30
f32 = jnp.float32
bf16 = jnp.bfloat16
i32 = jnp.int32


def nn(a, b):
    return lax.dot_general(a, b, (((1,), (0,)), ((), ())), preferred_element_type=f32)


def nt(a, b):
    return lax.dot_general(a, b, (((1,), (1,)), ((), ())), preferred_element_type=f32)


def tn(a, b):
    return lax.dot_general(a, b, (((0,), (0,)), ((), ())), preferred_element_type=f32)


def split2(x):
    high = x.astype(bf16)
    return high, (x - high.astype(f32)).astype(bf16)


def split3(x):
    high = x.astype(bf16)
    rest = x - high.astype(f32)
    mid = rest.astype(bf16)
    return high, mid, (rest - mid.astype(f32)).astype(bf16)


def call(kernel, grid, ins, outs, args, scratch=(), flops=0, nbytes=0, vmem=60 << 20, aliases=None):
    body = kernel.func if isinstance(kernel, functools.partial) else kernel
    return pl.pallas_call(
        kernel,
        name=body.__name__,
        grid=grid,
        in_specs=ins,
        out_specs=[o[2] for o in outs],
        out_shape=[jax.ShapeDtypeStruct(o[0], o[1]) for o in outs],
        scratch_shapes=list(scratch),
        input_output_aliases=aliases or {},
        compiler_params=pltpu.CompilerParams(
            dimension_semantics=("arbitrary",) * len(grid), vmem_limit_bytes=vmem
        ),
        cost_estimate=pl.CostEstimate(
            flops=int(flops * SLOW), bytes_accessed=nbytes, transcendentals=0
        ),
    )(*args)


def whole(shape):
    zeros = (0,) * len(shape)
    return pl.BlockSpec(shape, lambda *_: zeros)


def lanes_of(shape):
    return lax.broadcasted_iota(i32, shape, len(shape) - 1)


def turn(values, cos_wide, sin_wide):
    first = lanes_of((1, PAIR)) % HD < HD // 2
    partner = jnp.where(first, pltpu.roll(values, PAIR - HD // 2, 1), pltpu.roll(values, HD // 2, 1))
    return values * cos_wide + partner * sin_wide


def eye(size):
    at = (lax.broadcasted_iota(i32, (size, size), 0), lax.broadcasted_iota(i32, (size, size), 1))
    return jnp.where(at[0] == at[1], 1.0, 0.0).astype(bf16)


def pack_kernel(
    core_ref, wq_ref, wk_ref, wv_ref, wo_ref, router_ref, const_ref, g1_ref, g2_ref, vec_ref, own_ref, other_ref
):
    part, width = wq_ref.shape
    half = part // 2
    core = core_ref[0]
    small = jnp.concatenate(
        [ref[...].astype(f32) for ref in (router_ref, const_ref, g1_ref, g2_ref, vec_ref)], axis=0
    )
    small = jnp.concatenate([small, jnp.zeros((small.shape[0], width - part), f32)], axis=1).astype(bf16)
    split = small.shape[0] // 2
    for side in range(2):
        rows = [ref[side * half : (side + 1) * half, :] for ref in (wq_ref, wk_ref, wv_ref, wo_ref)]
        rows.append(small[side * split : (side + 1) * split])

        def put(ref):
            at = 0
            for piece in rows:
                ref[at : at + piece.shape[0], :] = piece
                at += piece.shape[0]

        @pl.when(core == side)
        def _():
            put(own_ref)

        @pl.when(core != side)
        def _():
            put(other_ref)


def pack_call(core, *weights):
    part, width = weights[0].shape
    count = sum(w.shape[0] for w in weights[4:])
    shape = (4 * (part // 2) + count // 2, width)
    return call(
        pack_kernel,
        (1,),
        [pl.BlockSpec(memory_space=pltpu.SMEM)] + [whole(w.shape) for w in weights],
        [(shape, bf16, whole(shape))] * 2,
        (core, *weights),
        flops=1 << 20,
        nbytes=12 * width * part,
    )


def deal_kernel(experts, mine_ref, dealt_ref, out_ref):
    count, _, rows = dealt_ref.shape
    routes = jnp.zeros((2, rows), i32)
    for e in range(count):
        routes = routes + dealt_ref[e] * mine_ref[e]
    at = lax.broadcasted_iota(i32, (experts, rows), 0)
    named = [routes[j : j + 1] == at for j in range(2)]
    hits = jnp.where(named[0] | named[1], 1.0, 0.0).astype(bf16)
    before = lax.broadcasted_iota(i32, (rows, rows), 0) < lax.broadcasted_iota(i32, (rows, rows), 1)
    counts = nn(hits, jnp.where(before, 1.0, 0.0).astype(bf16)) + (at * CAP).astype(f32)
    out_ref[...] = jnp.zeros(out_ref.shape, f32)
    out_ref[0:2, :] = routes.astype(f32)
    for j in range(2):
        slot = jnp.sum(jnp.where(named[j], counts, 0.0), axis=0, keepdims=True)
        out_ref[2 + j : 3 + j, :] = jnp.where(routes[j : j + 1] < experts, slot, -1.0)


def deal_call(mine, dealt):
    experts, _, rows = dealt.shape
    return call(
        functools.partial(deal_kernel, experts),
        (1,),
        [pl.BlockSpec(memory_space=pltpu.SMEM), whole(dealt.shape)],
        [((8, rows), f32, whole((8, rows)))],
        (mine, dealt),
        flops=2 * 128 * rows * rows,
        nbytes=64 * rows,
    )[0]


def columns_of(table_ref):
    return table_ref[...].T.astype(i32)


def pack_experts_kernel(gate_ref, up_ref, down_ref, out_ref):
    one = eye(gate_ref.shape[2])
    out_ref[0] = nt(one, gate_ref[0]).astype(bf16)
    out_ref[1] = nt(one, up_ref[0]).astype(bf16)
    out_ref[2] = down_ref[0]


def pack_experts_call(gate, up, down):
    _, width, units = gate.shape
    shape = (3, units, width)
    return call(
        pack_experts_kernel,
        (1,),
        [whole(gate.shape)] * 2 + [whole(down.shape)],
        [(shape, bf16, whole(shape))],
        (gate, up, down),
        flops=1 << 20,
        nbytes=12 * width * units,
    )[0]


def finish_experts_kernel(own_ref, ahead_ref, back_ref, gate_ref, up_ref, down_ref):
    for at, ref in enumerate((gate_ref, up_ref, down_ref)):
        total = own_ref[at].astype(f32) + ahead_ref[at].astype(f32) + back_ref[at].astype(f32)
        ref[0] = total if at == 2 else total.T


def finish_experts_call(own, ahead, back):
    _, units, width = own.shape
    outs = [(1, width, units)] * 2 + [(1, units, width)]
    return call(
        finish_experts_kernel,
        (1,),
        [whole(own.shape)] * 3,
        [(shape, f32, whole(shape)) for shape in outs],
        (own, ahead, back),
        flops=10**10,
        nbytes=30 * units * width,
    )


def qkv_rows(hid_ref, gain, w_ref, cos_ref, sin_ref, q_ref, k_ref, v_ref, n_ref):
    width = hid_ref.shape[1]
    hidden = hid_ref[...].astype(f32)
    scale = lax.rsqrt(jnp.mean(hidden * hidden, axis=-1, keepdims=True) + norm_eps)
    normed = (hidden * scale * gain).astype(bf16)
    n_ref[...] = normed
    cos_wide, sin_wide = cos_ref[...], sin_ref[...]
    for part, (out, factor) in enumerate(((q_ref, HD**-0.5), (k_ref, 1.0))):
        full = nt(normed, w_ref[part])
        for at in range(0, width, PAIR):
            lin = full[:, at : at + PAIR]
            out[:, at : at + PAIR] = (turn(lin, cos_wide, sin_wide) * factor).astype(bf16)
    v_ref[...] = nt(normed, w_ref[2]).astype(bf16)


def qkv_kernel(gain_at, hid_ref, small_ref, w_ref, *refs):
    gain = small_ref[gain_at : gain_at + 1, :].astype(f32)
    qkv_rows(hid_ref, gain, w_ref, *refs)


def qkv_pieces_kernel(gain_at, part, where_ref, hid_ref, cos_ref, sin_ref, *refs):
    pieces, (q_ref, k_ref, v_ref, n_ref, w_ref, wo_ref, small_ref, vec_ref) = refs[:-8], refs[-8:]
    count = len(pieces) // 2
    half = part // 2
    vectors = pieces[0].shape[0] - 4 * half

    @pl.when(pl.program_id(0) == 0)
    def _():
        vec_ref[...] = jnp.zeros_like(vec_ref)
        core = where_ref[count]
        for own in range(2):
            side = core if own == 0 else 1 - core
            total = None
            for r in range(count):
                ref = pieces[own * count + r]
                shard = where_ref[r]
                row = pl.multiple_of(shard * part + side * half, 16)
                for at in range(3):
                    w_ref[at, pl.ds(row, half), :] = ref[at * half : (at + 1) * half, :]
                wo_ref[pl.ds(row, half), :] = ref[3 * half : 4 * half, :]
                moved = pltpu.roll(ref[4 * half :, :].astype(f32), shard * part, 1)
                total = moved if total is None else total + moved
            vec_ref[pl.ds(pl.multiple_of(side * vectors, 8), vectors), :] = total
        small_ref[...] = vec_ref[...].astype(bf16)

    gain = small_ref[gain_at : gain_at + 1, :].astype(f32)
    qkv_rows(hid_ref, gain, w_ref, cos_ref, sin_ref, q_ref, k_ref, v_ref, n_ref)


def qkv_specs(hidden):
    rows, width = hidden.shape
    row = pl.BlockSpec((TB, width), lambda i: (i, 0))
    return dict(
        row=row,
        tab=pl.BlockSpec((TB, PAIR), lambda i: (i, 0)),
        outs=[((rows, width), bf16, row)] * 4,
        flops=6 * rows * width * width,
        nbytes=10 * rows * width + 6 * width * width,
    )


def qkv_call(hidden, small, gain_at, weights, cos_wide, sin_wide):
    s = qkv_specs(hidden)
    return call(
        functools.partial(qkv_kernel, gain_at),
        (hidden.shape[0] // TB,),
        [s["row"], whole(small.shape), whole(weights.shape), s["tab"], s["tab"]],
        s["outs"],
        (hidden, small, weights, cos_wide, sin_wide),
        flops=s["flops"],
        nbytes=s["nbytes"],
    )


def qkv_pieces_call(hidden, where, own, other, gain_at, part, cos_wide, sin_wide):
    s = qkv_specs(hidden)
    width = hidden.shape[1]
    pieces = list(own) + list(other)
    return call(
        functools.partial(qkv_pieces_kernel, gain_at, part),
        (hidden.shape[0] // TB,),
        [pl.BlockSpec(memory_space=pltpu.SMEM), s["row"], s["tab"], s["tab"]]
        + [whole(piece.shape) for piece in pieces],
        s["outs"]
        + [
            ((3, width, width), bf16, whole((3, width, width))),
            ((width, width), bf16, whole((width, width))),
            ((WIDE, width), bf16, whole((WIDE, width))),
        ],
        (where, hidden, cos_wide, sin_wide, *pieces),
        scratch=[pltpu.VMEM((WIDE, width), f32)],
        flops=s["flops"],
        nbytes=s["nbytes"],
    )


def attend_kernel(len_ref, q_ref, k_ref, v_ref, *refs):
    o_ref, r_ref, e_ref = refs[-3:]
    rows = q_ref.shape[0]
    live = len_ref[0]
    low_lanes = lanes_of((1, PAIR)) < HD
    keys = k_ref[...]
    nil = jnp.zeros_like(keys)
    key_heads = (jnp.where(low_lanes, keys, nil), jnp.where(low_lanes, nil, keys))
    value_t = v_ref[...].T
    zeros = jnp.zeros((HD, rows), bf16)
    ones = jnp.ones((HD, rows), bf16)
    value_heads = (
        jnp.concatenate([value_t[:HD], zeros, ones, zeros], axis=0),
        jnp.concatenate([zeros, value_t[HD:], zeros, ones], axis=0),
    )
    key_at = lax.broadcasted_iota(i32, (TB, TB), 0)
    causal = key_at <= lax.broadcasted_iota(i32, (TB, TB), 1)
    for i in range(rows // TB):
        query = q_ref[i * TB : (i + 1) * TB, :]
        total = jnp.zeros((2 * PAIR, TB), f32)
        for head in range(2):
            blocks = []
            for j in range(i + 1):
                score = nt(key_heads[head][j * TB : (j + 1) * TB], query)
                keep = None
                if j > 0:
                    keep = key_at < live - j * TB
                if j == i:
                    keep = causal if keep is None else keep & causal
                if keep is not None:
                    score = jnp.where(keep, score, masked_score)
                blocks.append(score)
            top = jnp.max(blocks[0], axis=0, keepdims=True)
            for block in blocks[1:]:
                top = jnp.maximum(top, jnp.max(block, axis=0, keepdims=True))
            for j, block in enumerate(blocks):
                expo = jnp.exp(block - top).astype(bf16)
                e_ref[0, head, i * (i + 1) // 2 + j] = expo
                total = total + nn(value_heads[head][:, j * TB : (j + 1) * TB], expo)
        recip = 1.0 / total[PAIR:]
        o_ref[i * TB : (i + 1) * TB, :] = (total[:PAIR] * recip).T.astype(bf16)
        r_ref[i * TB : (i + 1) * TB, :] = recip.T


def attend_call(live, query, key, value, first, count, earlier=()):
    rows, width = query.shape
    pairs = width // PAIR
    steps = rows // TB
    tiles = steps * (steps + 1) // 2
    col = pl.BlockSpec((rows, PAIR), lambda p: (0, p + first))
    expo = (1, 2, tiles, TB, TB)
    return call(
        attend_kernel,
        (count,),
        [pl.BlockSpec(memory_space=pltpu.SMEM), col, col, col]
        + [pl.BlockSpec(memory_space=pl.ANY)] * len(earlier),
        [
            ((rows, width), bf16, col),
            ((rows, width), f32, col),
            ((pairs,) + expo[1:], bf16, pl.BlockSpec(expo, lambda p: (p + first, 0, 0, 0, 0))),
        ],
        (live, query, key, value, *earlier),
        flops=count * 2 * tiles * TB * TB * 8 * PAIR,
        nbytes=count * (2 * tiles * TB * TB * 2 + 12 * rows * PAIR),
        aliases={4 + at: at for at in range(len(earlier))},
    )


def attend_back_kernel(
    q_ref, k_ref, v_ref, e_ref, do_ref, att_ref, r_ref, cos_ref, sin_ref, dq_ref, dk_ref, dv_ref, dqt_ref
):
    rows = q_ref.shape[0]
    steps = rows // TB
    low_lanes = lanes_of((1, PAIR)) < HD

    def halves(x):
        nil = jnp.zeros_like(x)
        return jnp.where(low_lanes, x, nil), jnp.where(low_lanes, nil, x)

    scaled = do_ref[...].astype(f32) * r_ref[...]
    product_t = (scaled * att_ref[...].astype(f32)).T
    deltas = (
        jnp.sum(product_t[:HD], axis=0, keepdims=True),
        jnp.sum(product_t[HD:], axis=0, keepdims=True),
    )
    grad = scaled.astype(bf16)
    grad_heads = halves(grad)
    query_heads = halves(q_ref[...])
    value_heads = halves(v_ref[...])
    key_t = k_ref[...].T
    zeros = jnp.zeros((HD, rows), bf16)
    key_heads = (
        jnp.concatenate([key_t[:HD], zeros], axis=0),
        jnp.concatenate([zeros, key_t[HD:]], axis=0),
    )
    for j in range(steps):
        js = slice(j * TB, (j + 1) * TB)
        value_grad = jnp.zeros((TB, PAIR), f32)
        key_grad = jnp.zeros((TB, PAIR), f32)
        keys_t = jnp.concatenate([key_heads[0][:, js], key_heads[1][:, js]], axis=1)
        for i in range(j, steps):
            rs = slice(i * TB, (i + 1) * TB)
            tile = i * (i + 1) // 2 + j
            expos, scores = [], []
            for head in range(2):
                grad_prob = nt(value_heads[head][js], grad[rs])
                expo = e_ref[0, head, tile]
                expos.append(expo)
                scores.append(
                    (expo.astype(f32) * (grad_prob - deltas[head][:, rs])).astype(bf16)
                )
            value_grad = value_grad + nn(
                jnp.concatenate(expos, axis=1),
                jnp.concatenate([grad_heads[0][rs], grad_heads[1][rs]], axis=0),
            )
            key_grad = key_grad + nn(
                jnp.concatenate(scores, axis=1),
                jnp.concatenate([query_heads[0][rs], query_heads[1][rs]], axis=0),
            )
            add = nn(keys_t, jnp.concatenate(scores, axis=0))
            if j == 0:
                dqt_ref[:, rs] = add
            else:
                dqt_ref[:, rs] += add
        dv_ref[js, :] = value_grad.astype(bf16)
        dk_ref[js, :] = turn(key_grad, cos_ref[js, :], -sin_ref[js, :]).astype(bf16)
    query_grad = dqt_ref[...].T * (HD**-0.5)
    dq_ref[...] = turn(query_grad, cos_ref[...], -sin_ref[...]).astype(bf16)


def attend_back_call(query, key, value, expo, grad, attended, recip, cos_wide, sin_wide):
    rows, width = query.shape
    pairs, _, tiles = expo.shape[:3]
    col = pl.BlockSpec((rows, PAIR), lambda p: (0, p))
    tab = whole((rows, PAIR))
    e_spec = pl.BlockSpec((1,) + expo.shape[1:], lambda p: (p, 0, 0, 0, 0))
    return call(
        attend_back_kernel,
        (pairs,),
        [col, col, col, e_spec, col, col, col, tab, tab],
        [((rows, width), bf16, col)] * 3,
        (query, key, value, expo, grad, attended, recip, cos_wide, sin_wide),
        scratch=[pltpu.VMEM((PAIR, rows), f32)],
        flops=pairs * 2 * tiles * TB * TB * 8 * PAIR,
        nbytes=pairs * 2 * tiles * TB * TB * 2 + 22 * rows * width,
    )


def route_kernel(
    att_ref, hid_ref, grad_ref, wo_ref, sw_ref, prev_ref, gating_ref, table_ref, all_ref,
    res_ref, info_ref, rows_ref, grads_ref, nlow_ref, rg_ref,
):
    step = pl.program_id(0)
    rows = nlow_ref.shape[0]
    blocks = rows // TB
    choices = prev_ref.shape[0]

    @pl.when(step < blocks)
    def _():
        residual = hid_ref[...].astype(f32) + nn(att_ref[...], wo_ref[...])
        res_ref[...] = residual
        scale = lax.rsqrt(jnp.mean(residual * residual, axis=-1, keepdims=True) + norm_eps)
        gain = sw_ref[choices + 5 : choices + 6, :].astype(f32)
        normed = residual * scale * gain
        high, mid, low = split3(normed)
        small_weights = sw_ref[...]
        small = nt(high, small_weights) + nt(mid, small_weights) + nt(low, small_weights)
        logits = small + tn(prev_ref[...], gating_ref[...])
        cols = columns_of(table_ref)
        lane = lanes_of(logits.shape)
        is_choice = lane < choices
        masked = jnp.where(is_choice, logits, masked_score)
        expo = jnp.exp(masked - jnp.max(masked, axis=-1, keepdims=True))
        probs = expo / jnp.sum(expo, axis=-1, keepdims=True)
        wide = small.shape[1]
        partner = jnp.where(lane % 2 == 0, pltpu.roll(small, wide - 1, 1), pltpu.roll(small, 1, 1))
        top = jnp.maximum(small, partner)
        own = jnp.exp(small - top)
        alpha = own / (own + jnp.exp(partner - top))
        gates = [
            jnp.sum(jnp.where(lane == cols[:, j : j + 1], probs, 0.0), axis=-1, keepdims=True)
            for j in range(2)
        ]
        info = jnp.where(is_choice, probs, alpha)
        for at, column in enumerate((gates[0], gates[1], scale)):
            info = jnp.where(lane == choices + 4 + at, column, info)
        info_ref[...] = info
        here = pl.ds(pl.multiple_of(step * TB, TB), TB)
        nlow_ref[here, :] = high
        grad = grad_ref[...].astype(f32)
        rg_ref[0, here, :] = (gates[0] * grad).astype(bf16)
        rg_ref[1, here, :] = (gates[1] * grad).astype(bf16)

    @pl.when(step >= blocks)
    def _():
        slot = (step - blocks) * CAP + lax.broadcasted_iota(i32, (CAP, rows), 0)
        places = all_ref[...].astype(i32)
        hot = [jnp.where(places[2 + j : 3 + j] == slot, 1.0, 0.0).astype(bf16) for j in range(2)]
        rows_ref[0] = nn(hot[0] + hot[1], nlow_ref[...]).astype(bf16)
        grads_ref[0] = (nn(hot[0], rg_ref[0]) + nn(hot[1], rg_ref[1])).astype(bf16)


def route_call(attended, hidden, grad, w_out, small_weights, prev, gating, table, experts):
    rows, width = attended.shape
    blocks = rows // TB
    wide = WIDE

    def block(cols):
        return pl.BlockSpec((TB, cols), lambda i: (jnp.minimum(i, blocks - 1), 0))

    def across(count):
        return pl.BlockSpec((count, TB), lambda i: (0, jnp.minimum(i, blocks - 1)))

    return call(
        route_kernel,
        (blocks + experts,),
        [
            block(width), block(width), block(width), whole(w_out.shape),
            whole(small_weights.shape), across(prev.shape[0]), whole(gating.shape), across(8), whole(table.shape),
        ],
        [
            ((rows, width), f32, block(width)),
            ((rows, wide), f32, block(wide)),
        ]
        + [
            (
                (experts, CAP, width),
                bf16,
                pl.BlockSpec((1, CAP, width), lambda i: (jnp.maximum(i - blocks, 0), 0, 0)),
            )
        ]
        * 2,
        (attended, hidden, grad, w_out, small_weights, prev, gating, table, table),
        scratch=[pltpu.VMEM((rows, width), bf16), pltpu.VMEM((2, rows, width), bf16)],
        flops=2 * rows * width * width + 6 * experts * CAP * rows * width,
        nbytes=10 * rows * width + 2 * width * width + 4 * experts * CAP * width,
    )


def ring_order(count):
    wide = 1 << ((count.bit_length() - 1) // 2)
    tall = count // wide
    if wide < 2 or wide * tall != count or tall % 2:
        return list(range(count))
    order = [z * wide for z in range(tall)]
    for turn_at in range(tall):
        z = tall - 1 - turn_at
        across = range(1, wide) if turn_at % 2 == 0 else range(wide - 1, 0, -1)
        order.extend(z * wide + y for y in across)
    return order


def ring_send(x, order, step):
    count = len(order)
    pairs = [(order[i], order[(i + step) % count]) for i in range(count)]
    return lax.ppermute(x, "fsdp", pairs)


def swap(x, experts, bit):
    return lax.ppermute(x, "expert", [(e, e ^ bit) for e in range(experts)])


def cut(x, axis):
    size = x.shape[axis]
    half = -(-size // 32) * 16
    return lax.slice_in_dim(x, 0, half, axis=axis), lax.slice_in_dim(x, half, size, axis=axis)


def ring_gather(x, order, axis, ahead_of=()):
    count = len(order)
    half = count // 2
    pieces = [None] * count
    pieces[0] = x
    ahead, back = x, x
    for k in range(half):
        if k < len(ahead_of) and ahead_of[k]:
            ahead, back, _ = lax.optimization_barrier((ahead, back, ahead_of[k]))
        if k < half - 1:
            ahead = ring_send(ahead, order, 1)
            back = ring_send(back, order, -1)
            pieces[count - k - 1] = ahead
            pieces[k + 1] = back
    first = ring_send(cut(ahead, axis)[0], order, 1)
    second = ring_send(cut(back, axis)[1], order, -1)
    pieces[half] = jnp.concatenate([first, second], axis=axis)
    return pieces


def plus(a, b):
    return (a.astype(f32) + b.astype(f32)).astype(bf16)


class RingReduce:
    def __init__(self, parts, order, axis):
        self.parts, self.order, self.axis = parts, order, axis
        self.left = len(order) // 2 - 1
        self.flight = None

    def start(self):
        first, second = cut(self.parts[len(self.order) // 2], self.axis)
        self.flight = (ring_send(first, self.order, 1), ring_send(second, self.order, -1))

    def add(self):
        k, axis = self.left, self.axis
        ahead, back = self.flight
        mine, other = self.parts[k], self.parts[len(self.order) - k]
        if k == len(self.order) // 2 - 1:
            low, high = cut(mine, axis)
            mine = jnp.concatenate([plus(low, ahead), high], axis=axis)
            low, high = cut(other, axis)
            other = jnp.concatenate([low, plus(high, back)], axis=axis)
        else:
            mine, other = plus(mine, ahead), plus(other, back)
        self.ready = (mine, other)
        self.left = k - 1

    def send(self):
        mine, other = self.ready
        self.flight = (ring_send(mine, self.order, 1), ring_send(other, self.order, -1))

    def turn(self):
        self.add()
        self.send()

    def finish(self):
        return finish_experts_call(self.parts[0], *self.flight)

    def result(self):
        return self.parts[0].astype(f32) + self.flight[0].astype(f32) + self.flight[1].astype(f32)


class Copies:
    def __init__(self, sems):
        self.sems, self.count = sems, 0

    def make(self, src, dst):
        self.count += 1
        return pltpu.make_async_copy(src, dst, self.sems.at[self.count - 1])


def expert_kernel(steps, x_ref, *refs):
    pieces, refs = refs[: 2 * steps], refs[2 * steps :]
    y_ref, inner_ref, fa_ref, fb_ref, acc_ref, buf, sems = refs
    step = pl.program_id(0)
    units = pieces[0].shape[1]
    copies = Copies(sems)
    loads = [
        [
            copies.make(pieces[2 * at + side], buf.at[at % 2, :, pl.ds(side * units, units), :])
            for side in range(2)
        ]
        for at in range(steps)
    ]
    for at in range(steps):

        @pl.when(step == at)
        def _():
            for ahead in (at, at + 1) if at == 0 else (at + 1,):
                if ahead < steps:
                    for copy in loads[ahead]:
                        copy.start()
            for copy in loads[at]:
                copy.wait()

    weights = buf.at[lax.rem(step, 2)]
    rows_in = x_ref[...].reshape(acc_ref.shape[0], x_ref.shape[2])
    gate = nt(rows_in, weights[0])
    up = nt(rows_in, weights[1])
    sig = 0.5 * jnp.tanh(0.5 * gate) + 0.5
    act = gate * sig
    inner = (act * up).astype(bf16)
    inner_ref[0] = inner
    fa_ref[0] = (up * (sig + act * (1.0 - sig))).astype(bf16)
    fb_ref[0] = act.astype(bf16)
    out = nn(inner, weights[2])

    @pl.when(step == 0)
    def _():
        acc_ref[...] = out

    @pl.when((step > 0) & (step < steps - 1))
    def _():
        acc_ref[...] += out

    @pl.when(step == steps - 1)
    def _():
        y_ref[...] = (acc_ref[...] + out).astype(bf16).reshape(y_ref.shape)


def expert_back_kernel(steps, earlier, last, x_ref, g_ref, inner_ref, fa_ref, fb_ref, *refs):
    pieces, refs = refs[: 2 * steps], refs[2 * steps :]
    first, refs = (refs[0], refs[1:]) if earlier else (None, refs)
    dx_ref, dw_refs = refs[0], refs[1 : 1 + 2 * steps]
    acc_ref, term_buf, buf, sems = refs[1 + 2 * steps :]
    step = pl.program_id(0)
    units = pieces[0].shape[1]
    rows = acc_ref.shape[0]
    copies = Copies(sems)
    loads, stores = [], []
    for at in range(steps):
        loads.append(
            [
                copies.make(pieces[2 * at + side], buf.at[at % 2, :, pl.ds(side * units, units), :])
                for side in range(2)
            ]
        )
        stores.append(
            [
                copies.make(term_buf.at[at % 2, :, pl.ds(side * units, units), :], dw_refs[2 * at + side])
                for side in range(2)
            ]
        )
    for at in range(steps):

        @pl.when(step == at)
        def _():
            for ahead in (at, at + 1) if at == 0 else (at + 1,):
                if ahead < steps:
                    for copy in loads[ahead]:
                        copy.start()
            for copy in loads[at]:
                copy.wait()
            if at >= 2:
                for copy in stores[at - 2]:
                    copy.wait()

    slot = lax.rem(step, 2)
    weights = buf.at[slot]
    rows_in = x_ref[...].reshape(rows, x_ref.shape[2])
    grad_in = g_ref[...].reshape(rows, g_ref.shape[2])
    grad_inner = nt(grad_in, weights[2])
    grads = jnp.concatenate(
        [(grad_inner * ref[0].astype(f32)).astype(bf16) for ref in (fa_ref, fb_ref)], axis=1
    )
    both = (2, 2 * units, rows_in.shape[1])
    term_buf[slot, 0:2] = tn(grads, rows_in).astype(bf16).reshape(both)
    term_buf[slot, 2] = tn(inner_ref[0], grad_in).astype(bf16)
    for at in range(steps):

        @pl.when(step == at)
        def _():
            for copy in stores[at]:
                copy.start()

    out = nn(grads, weights[0:2].reshape(grads.shape[1], grad_in.shape[1]))

    @pl.when(step == 0)
    def _():
        acc_ref[...] = out if first is None else out + first[...]

    @pl.when((step > 0) & (step < steps - 1))
    def _():
        acc_ref[...] += out

    @pl.when(step == steps - 1)
    def _():
        total = acc_ref[...] + out if steps > 1 else acc_ref[...]
        dx_ref[...] = total.astype(bf16).reshape(dx_ref.shape) if last else total
        for at in range(max(0, steps - 2), steps):
            for copy in stores[at]:
                copy.wait()


def expert_specs(sent, pieces):
    experts, _, width = sent.shape
    chunks = len(pieces)
    units = pieces[0].shape[1]
    rows = experts * CAP
    return dict(
        rows=rows,
        steps=chunks // 2,
        units=units,
        width=width,
        any=[pl.BlockSpec(memory_space=pl.ANY)] * chunks,
        x=pl.BlockSpec((experts, CAP, width), lambda c: (0, 0, 0)),
        flops=6 * rows * width * chunks * units,
        nbytes=6 * chunks * units * (rows + width) + 4 * rows * width,
        acc=pltpu.VMEM((rows, width), f32),
        buf=pltpu.VMEM((2, 3, 2 * units, width), bf16),
    )


def expert_call(sent, pieces):
    s = expert_specs(sent, pieces)
    unit = pl.BlockSpec((1, s["rows"], 2 * s["units"]), lambda c: (c, 0, 0))
    hidden = ((s["steps"], s["rows"], 2 * s["units"]), bf16, unit)
    return call(
        functools.partial(expert_kernel, s["steps"]),
        (s["steps"],),
        [s["x"], *s["any"]],
        [(sent.shape, bf16, s["x"])] + [hidden] * 3,
        (sent, *pieces),
        scratch=[s["acc"], s["buf"], pltpu.SemaphoreType.DMA((2 * s["steps"],))],
        flops=s["flops"],
        nbytes=s["nbytes"],
    )


def expert_back_call(sent, sent_grads, pieces, inner, factor_a, factor_b, at, earlier=None):
    s = expert_specs(sent, pieces)
    steps = s["steps"]
    unit = pl.BlockSpec((1, s["rows"], 2 * s["units"]), lambda c: (c + at, 0, 0))
    sums = (s["rows"], s["width"])
    outs = call(
        functools.partial(expert_back_kernel, steps, earlier is not None, at == 0),
        (steps,),
        [s["x"], s["x"], unit, unit, unit, *s["any"]]
        + ([whole(sums)] if earlier is not None else []),
        [(sent.shape, bf16, s["x"]) if at == 0 else (sums, f32, whole(sums))]
        + [(pieces[0].shape, bf16, pl.BlockSpec(memory_space=pl.ANY))] * (2 * steps),
        (sent, sent_grads, inner, factor_a, factor_b, *pieces) + (() if earlier is None else (earlier,)),
        scratch=[s["acc"], s["buf"], s["buf"], pltpu.SemaphoreType.DMA((4 * steps,))],
        flops=2 * s["flops"],
        nbytes=2 * s["nbytes"],
    )
    return outs[0], outs[1:]


def combine_kernel(
    y_ref, res_ref, info_ref, table_ref, grad_ref, sw_ref, prev_ref, gating_ref,
    out_ref, part_ref, gprev_ref, gsw_ref, gvec_ref, ggat_ref,
):
    step = pl.program_id(0)
    choices = prev_ref.shape[0]
    experts = y_ref.shape[0]
    cols = columns_of(table_ref)
    slots = experts * CAP
    rows_out = y_ref[...].reshape(slots, y_ref.shape[2])
    residual = res_ref[...]
    info = info_ref[...]
    lane = lanes_of(info.shape)

    def column(at):
        return info[:, at : at + 1]

    gates = (column(choices + 4), column(choices + 5))
    small_weights = sw_ref[...]
    gain = small_weights[choices + 5 : choices + 6].astype(f32)
    normed = residual * column(choices + 6) * gain
    grad = grad_ref[...].astype(f32)
    vectors = [small_weights[choices + 6 + c : choices + 7 + c].astype(f32) for c in range(2)]
    dots = nt(grad_ref[...], small_weights)
    alphas = ((column(choices), column(choices + 1)), (column(choices + 2), column(choices + 3)))
    dot_normed = jnp.sum(grad * normed, axis=-1, keepdims=True)
    dot_vectors = [dots[:, choices + 6 + c : choices + 7 + c] for c in range(2)]
    mixed = residual
    weight_normed = jnp.zeros_like(dot_normed)
    weight_copy = jnp.zeros_like(dot_normed)
    weight_const = [jnp.zeros_like(dot_normed), jnp.zeros_like(dot_normed)]
    grad_probs = jnp.zeros_like(info)
    slot = lanes_of((TB, slots))
    for j in range(2):
        route = cols[:, j : j + 1]
        hot = jnp.where(cols[:, 2 + j : 3 + j] == slot, 1.0, 0.0).astype(bf16)
        rows_j = nn(hot, rows_out)
        is_copy = jnp.where(route == experts + 1, 1.0, 0.0)
        is_const = [jnp.where(route == experts + 2 + c, 1.0, 0.0) for c in range(2)]
        on_normed = is_copy + is_const[0] * alphas[0][0] + is_const[1] * alphas[1][0]
        grad_gate = jnp.sum(grad * rows_j, axis=-1, keepdims=True) + on_normed * dot_normed
        for c in range(2):
            grad_gate = grad_gate + is_const[c] * alphas[c][1] * dot_vectors[c]
            weight_const[c] = weight_const[c] + gates[j] * is_const[c]
        grad_probs = grad_probs + jnp.where(lane == route, grad_gate, 0.0)
        mixed = mixed + gates[j] * rows_j
        weight_normed = weight_normed + gates[j] * on_normed
        weight_copy = weight_copy + gates[j] * is_copy
    mixed = mixed + weight_normed * normed
    for c in range(2):
        mixed = mixed + weight_const[c] * alphas[c][1] * vectors[c]
    out_ref[...] = mixed.astype(bf16)
    is_choice = lane < choices
    probs = jnp.where(is_choice, info, 0.0)
    grad_small = probs * (grad_probs - jnp.sum(probs * grad_probs, axis=-1, keepdims=True))
    direct = weight_copy
    coefs = jnp.zeros_like(info)
    for c in range(2):
        grad_alpha = (weight_const[c] * dot_normed, weight_const[c] * dot_vectors[c])
        mean = alphas[c][0] * grad_alpha[0] + alphas[c][1] * grad_alpha[1]
        for k in range(2):
            grad_small = jnp.where(
                lane == choices + 2 * c + k, alphas[c][k] * (grad_alpha[k] - mean), grad_small
            )
        direct = direct + alphas[c][0] * weight_const[c]
        coefs = jnp.where(lane == c, alphas[c][1] * weight_const[c], coefs)
    high, mid, low = split3(grad_small)
    part_ref[...] = direct * grad + (
        nn(high, small_weights) + nn(mid, small_weights) + nn(low, small_weights)
    )
    gating = gating_ref[...]
    gprev_ref[...] = nt(gating, high) + nt(gating, mid) + nt(gating, low)
    normed_high, normed_mid = split2(normed)
    grad_sw = tn(high, normed_high) + tn(mid, normed_high) + tn(high, normed_mid)
    coef_high, coef_mid = split2(coefs)
    grad_vec = tn(coef_high, grad_ref[...]) + tn(coef_mid, grad_ref[...])
    prev = prev_ref[...]
    grad_gating = nn(prev, high) + nn(prev, mid) + nn(prev, low)

    @pl.when(step == 0)
    def _():
        gsw_ref[...] = grad_sw
        gvec_ref[...] = grad_vec
        ggat_ref[...] = grad_gating

    @pl.when(step > 0)
    def _():
        gsw_ref[...] += grad_sw
        gvec_ref[...] += grad_vec
        ggat_ref[...] += grad_gating


def combine_call(back, residual, info, table, grad, small_weights, prev, gating):
    rows, width = residual.shape
    wide = info.shape[1]
    choices = prev.shape[0]
    slots = back.shape[0] * CAP

    def block(cols):
        return pl.BlockSpec((TB, cols), lambda i: (i, 0))

    def across(count):
        return pl.BlockSpec((count, TB), lambda i: (0, i))

    return call(
        combine_kernel,
        (rows // TB,),
        [
            whole(back.shape), block(width), block(wide), across(8), block(width),
            whole(small_weights.shape), across(choices), whole(gating.shape),
        ],
        [
            ((rows, width), bf16, block(width)),
            ((rows, width), f32, block(width)),
            ((choices, rows), f32, across(choices)),
            ((wide, width), f32, whole((wide, width))),
            ((wide, width), f32, whole((wide, width))),
            ((choices, wide), f32, whole((choices, wide))),
        ],
        (back, residual, info, table, grad, small_weights, prev, gating),
        flops=4 * slots * rows * width,
        nbytes=14 * rows * width + 2 * slots * width,
    )


def residual_kernel(
    gain_at, dx_ref, part_ref, res_ref, table_ref, grad_ref, sw_ref, wo_ref, att_ref,
    gres_ref, gatt_ref, gwo_ref, ggain_ref, acc_ref,
):
    step = pl.program_id(0)
    experts = dx_ref.shape[0]
    slots = experts * CAP
    slot = lanes_of((TB, slots))
    cols = columns_of(table_ref)
    hot = jnp.where((cols[:, 2:3] == slot) | (cols[:, 3:4] == slot), 1.0, 0.0).astype(bf16)
    grad_normed = part_ref[...] + nn(hot, dx_ref[...].reshape(slots, dx_ref.shape[2]))
    residual = res_ref[...]
    scale = lax.rsqrt(jnp.mean(residual * residual, axis=-1, keepdims=True) + norm_eps)
    unit = residual * scale
    grad_gain = jnp.sum(grad_normed * unit, axis=0, keepdims=True)
    scaled = grad_normed * sw_ref[gain_at : gain_at + 1, :].astype(f32)
    grad_residual = grad_ref[...].astype(f32) + scale * (
        scaled - unit * jnp.mean(scaled * unit, axis=-1, keepdims=True)
    )
    gres_ref[...] = grad_residual
    low = grad_residual.astype(bf16)
    gatt_ref[...] = nt(low, wo_ref[...]).astype(bf16)
    grad_out = tn(att_ref[...], low)

    @pl.when(step == 0)
    def _():
        acc_ref[...] = grad_out
        ggain_ref[...] = grad_gain

    @pl.when(step > 0)
    def _():
        acc_ref[...] += grad_out
        ggain_ref[...] += grad_gain

    @pl.when(step == pl.num_programs(0) - 1)
    def _():
        gwo_ref[...] = acc_ref[...].astype(bf16)


def residual_call(dx, part, residual, table, grad, small_weights, gain_at, w_out, attended):
    rows, width = residual.shape
    slots = dx.shape[0] * CAP

    def block(cols):
        return pl.BlockSpec((TB, cols), lambda i: (i, 0))

    return call(
        functools.partial(residual_kernel, gain_at),
        (rows // TB,),
        [
            whole(dx.shape), block(width), block(width), pl.BlockSpec((8, TB), lambda i: (0, i)), block(width),
            whole(small_weights.shape),
            whole(w_out.shape), block(width),
        ],
        [
            ((rows, width), f32, block(width)),
            ((rows, width), bf16, block(width)),
            ((width, width), bf16, whole((width, width))),
            ((1, width), f32, whole((1, width))),
        ],
        (dx, part, residual, table, grad, small_weights, w_out, attended),
        scratch=[pltpu.VMEM((width, width), f32)],
        flops=2 * slots * rows * width + 4 * rows * width * width,
        nbytes=18 * rows * width + 2 * slots * width,
    )


def qkv_weights_kernel(
    gain_at, where_ref, dq_ref, dk_ref, dv_ref, n_ref, w_ref, small_ref, gwo_ref, ggain_ref, gsw_ref, gvec_ref,
    ggat_ref, own_ref, other_ref, acc_ref,
):
    step = pl.program_id(0)
    count, _, width = own_ref.shape
    part = width // count
    half = part // 2
    shards = dq_ref.shape[1] // part
    normed = n_ref[...]
    core = where_ref[count]
    gain_grad = jnp.zeros((1, width), f32)

    def put(side, shard, at, value):
        rel = where_ref[count + 1 + shard]

        @pl.when(core == side)
        def _():
            own_ref[rel, at : at + value.shape[0], :] = value

        @pl.when(core != side)
        def _():
            other_ref[rel, at : at + value.shape[0], :] = value

    for at, ref in enumerate((dq_ref, dk_ref, dv_ref, None)):
        if ref is None:
            term = gwo_ref[...]
        else:
            full = tn(ref[...], normed)
            gain_grad = gain_grad + jnp.sum(full * w_ref[at].astype(f32), axis=0, keepdims=True)
            term = full.astype(bf16)
        for m in range(shards):
            for side in range(2):
                row = m * part + side * half
                put(side, step * shards + m, at * half, term[row : row + half])

    @pl.when(step == 0)
    def _():
        acc_ref[...] = gain_grad

    @pl.when(step > 0)
    def _():
        acc_ref[...] += gain_grad

    @pl.when(step == pl.num_programs(0) - 1)
    def _():
        gain_one = acc_ref[...] / small_ref[gain_at : gain_at + 1, :].astype(f32)
        vectors = jnp.concatenate(
            [gsw_ref[:gain_at, :], gain_one, ggain_ref[...], gvec_ref[:2, :]], axis=0
        )
        gating_high = ggat_ref[...].astype(bf16).astype(f32)
        gating = (gating_high, ggat_ref[...] - gating_high)
        lanes = lanes_of((1, width)) < part
        split = vectors.shape[0] // 2
        spare = jnp.zeros((16 - split - 1, width), f32)
        for m in range(count):
            here = vectors if m == 0 else pltpu.roll(vectors, width - m * part, 1)
            here = jnp.where(lanes, here, 0.0)
            for side in range(2):
                block = jnp.concatenate(
                    [here[side * split : (side + 1) * split], gating[side], spare], axis=0
                )
                put(side, m, 4 * half, block.astype(bf16))


def qkv_weights_call(where, dq, dk, dv, normed, weights, small, gain_at, gwo, ggain, gsw, gvec, ggat, count):
    rows, width = normed.shape
    steps = 2
    cols = width // steps
    col = pl.BlockSpec((rows, cols), lambda c: (0, c))
    part = width // count
    shape = (count, 2 * part + 16, width)
    return call(
        functools.partial(qkv_weights_kernel, gain_at),
        (steps,),
        [
            pl.BlockSpec(memory_space=pltpu.SMEM), col, col, col, whole(normed.shape),
            pl.BlockSpec((3, cols, width), lambda c: (0, c, 0)), whole(small.shape),
            pl.BlockSpec((cols, width), lambda c: (c, 0)), whole(ggain.shape), whole(gsw.shape), whole(gvec.shape),
            whole(ggat.shape),
        ],
        [(shape, bf16, whole(shape))] * 2,
        (where, dq, dk, dv, normed, weights, small, gwo, ggain, gsw, gvec, ggat),
        scratch=[pltpu.VMEM((1, width), f32)],
        flops=6 * rows * width * width,
        nbytes=8 * rows * width + 18 * width * width,
    )


def finish_kernel(
    choices, where_ref, mine_ref, theirs_ref, gq_ref, gk_ref, gv_ref, gwo_ref, g1_ref, g2_ref, router_ref, gat_ref,
    const_ref, vec_ref,
):
    part, width = gwo_ref.shape
    half = part // 2
    core = where_ref[where_ref.shape[0] // 2]

    def side(which, at, size):
        first = mine_ref[at : at + size, :].astype(f32)
        second = theirs_ref[at : at + size, :].astype(f32)
        return jnp.where(core == which, first, second)

    for at, ref in enumerate((gq_ref, gk_ref, gv_ref, gwo_ref)):
        both = jnp.concatenate([side(0, at * half, half), side(1, at * half, half)], axis=0)
        ref[...] = both
    split = (choices + 8) // 2
    low, high = side(0, 4 * half, 16), side(1, 4 * half, 16)
    small = jnp.concatenate([low[:split, :WIDE], high[:split, :WIDE]], axis=0)
    router_ref[...] = small[:choices, :part]
    const_ref[...] = small[choices : choices + 4, :part]
    g1_ref[...] = small[choices + 4 : choices + 5, :part]
    g2_ref[...] = small[choices + 5 : choices + 6, :part]
    vec_ref[...] = small[choices + 6 : choices + 8, :part]
    gating = (low + high)[split : split + 1, :]
    for at in range(choices):
        moved = gating if at == 0 else pltpu.roll(gating, width - at * choices, 1)
        gat_ref[at : at + 1, :] = moved[:, :choices]


def finish_call(where, mine, theirs, part, choices):
    width = mine.shape[1]
    outs = [(part, width)] * 4 + [
        (1, part), (1, part), (choices, part), (choices, choices), (4, part), (2, part),
    ]
    return call(
        functools.partial(finish_kernel, choices),
        (1,),
        [pl.BlockSpec(memory_space=pltpu.SMEM), whole(mine.shape), whole(mine.shape)],
        [(shape, f32, whole(shape)) for shape in outs],
        (where, mine, theirs),
        flops=1 << 20,
        nbytes=20 * part * width,
    )


def plain_weights_kernel(dq_ref, dk_ref, dv_ref, n_ref, out_ref):
    normed = n_ref[...]
    for part, ref in enumerate((dq_ref, dk_ref, dv_ref)):
        out_ref[part] = tn(ref[...], normed)


def plain_weights_call(dq, dk, dv, normed):
    rows, width = normed.shape
    col = pl.BlockSpec((rows, 256), lambda c: (0, c))
    return call(
        plain_weights_kernel,
        (width // 256,),
        [col, col, col, whole((rows, width))],
        [((3, width, width), f32, pl.BlockSpec((3, 256, width), lambda c: (0, c, 0)))],
        (dq, dk, dv, normed),
        flops=6 * rows * width * width,
        nbytes=8 * rows * width + 12 * width * width,
    )[0]


def hidden_kernel(gain_at, dq_ref, dk_ref, dv_ref, w_ref, hid_ref, small_ref, gres_ref, out_ref):
    grad_normed = nn(dq_ref[...], w_ref[0]) + nn(dk_ref[...], w_ref[1]) + nn(dv_ref[...], w_ref[2])
    hidden = hid_ref[...].astype(f32)
    scale = lax.rsqrt(jnp.mean(hidden * hidden, axis=-1, keepdims=True) + norm_eps)
    unit = hidden * scale
    scaled = grad_normed * small_ref[gain_at : gain_at + 1, :].astype(f32)
    out_ref[...] = gres_ref[...] + scale * (
        scaled - unit * jnp.mean(scaled * unit, axis=-1, keepdims=True)
    )


def hidden_call(dq, dk, dv, weights, hidden, small, gain_at, grad_residual):
    rows, width = hidden.shape
    row = pl.BlockSpec((TB, width), lambda i: (i, 0))
    return call(
        functools.partial(hidden_kernel, gain_at),
        (rows // TB,),
        [row, row, row, whole(weights.shape), row, whole(small.shape), row],
        [((rows, width), f32, row)],
        (dq, dk, dv, weights, hidden, small, grad_residual),
        flops=1 << 20,
        nbytes=1 << 20,
    )[0]


def rope_wide(length):
    inverse = rope_base ** (-(2.0 * jnp.arange(HD // 2, dtype=f32)) / HD)
    angles = jnp.arange(length, dtype=f32)[:, None] * inverse[None, :]
    cosine, sine = jnp.cos(angles), jnp.sin(angles)
    return (
        jnp.concatenate([cosine] * 4, axis=1),
        jnp.concatenate([-sine, sine, -sine, sine], axis=1),
    )


def to_rows(flat, width):
    count = -(-flat.shape[1] // width)
    return jnp.pad(flat, ((0, 0), (0, count * width - flat.shape[1]))).reshape(
        flat.shape[0], count, width
    )


def per_device(
    hidden_in,
    prev_logits,
    seq_lengths,
    seq_order,
    routes,
    w_query,
    w_key,
    w_value,
    w_output,
    gain_attn,
    gain_moe,
    w_router,
    w_gating,
    w_const,
    v_const,
    w_gate,
    w_up,
    w_down,
    out_grad,
):
    rows, width = hidden_in.shape[1:]
    experts = lax.axis_size("expert")
    shards = lax.axis_size("fsdp")
    choices = w_router.shape[1]
    part = width // shards
    hidden = hidden_in.reshape(rows, width)
    grad = out_grad.reshape(rows, width)
    prev = prev_logits.reshape(rows, choices).T

    fsdp_here = lax.axis_index("fsdp")
    own = lax.axis_index("expert") * shards + fsdp_here
    live = lax.dynamic_slice(seq_lengths, (own,), (1,))
    dealt = lax.all_gather(routes.reshape(rows, 2).T, "expert", axis=0, tiled=False)
    peers = jnp.arange(experts, dtype=i32) * shards + fsdp_here
    table = deal_call((seq_order[peers] == own).astype(i32), dealt)
    cos_wide, sin_wide = rope_wide(rows)

    gain_at = choices + 4
    small_count = choices + 8
    order = ring_order(shards)
    place = jnp.asarray([order.index(m) for m in range(shards)], dtype=i32)
    spot = place[fsdp_here]
    core = lax.rem(lax.axis_index("expert"), 2)
    paired = part % 32 == 0 and small_count == 16 and shards % 2 == 0 and experts & (experts - 1) == 0
    ring = jnp.asarray(order, dtype=i32)
    where = jnp.concatenate(
        [ring[(spot + jnp.arange(shards, dtype=i32)) % shards], core[None], (place - spot) % shards]
    )
    expert_pack = pack_experts_call(w_gate, w_up, w_down)
    if paired:
        pack, spare = pack_call(
            core[None], w_query.T, w_key.T, w_value.T, w_output, w_router.T, w_const.T, gain_attn[None], gain_moe[None], v_const
        )
        own = ring_gather(pack, order, 0, [(), (cos_wide, sin_wide), (dealt,), (expert_pack, table)])
        other = [spare] + [swap(piece, experts, 1) for piece in own[1:]]
        expert_pack, _ = lax.optimization_barrier((expert_pack, own[shards // 2]))
        query, key, value, normed_one, qkv_weights, w_out, small = qkv_pieces_call(
            hidden, where, own, other, gain_at, part, cos_wide, sin_wide
        )
    else:
        small_parts = jnp.concatenate(
            [w_router.T, w_const.T, gain_attn[None], gain_moe[None], v_const], axis=0
        )
        first_pack = jnp.concatenate(
            [w_query.T, w_key.T, w_value.T, to_rows(small_parts.reshape(1, -1), width)[0]], axis=0
        )
        first = lax.all_gather(first_pack, "fsdp", axis=0, tiled=False)
        w_out = lax.all_gather(w_output, "fsdp", axis=0, tiled=True)
        qkv_weights = (
            first[:, : 3 * part]
            .reshape(shards, 3, part, width)
            .transpose(1, 0, 2, 3)
            .reshape(3, width, width)
        )
        small = (
            first[:, 3 * part :]
            .reshape(shards, -1)[:, : small_count * part]
            .reshape(shards, small_count, part)
            .transpose(1, 0, 2)
            .reshape(small_count, width)
        )
        small = jnp.pad(small, ((0, WIDE - small_count), (0, 0)))
        query, key, value, normed_one = qkv_call(
            hidden, small, gain_at, qkv_weights, cos_wide, sin_wide
        )
    pairs = width // PAIR
    some = pairs // 2
    early = attend_call(live, query, key, value, 0, some)
    expert_weights = ring_gather(expert_pack, order, 1, [()] + [early[:1]])
    farthest = shards // 2
    turns = [0] + [r for k in range(1, farthest) for r in (k, shards - k)] + [farthest]
    by_turn = [expert_weights[r] for r in turns]

    def after(value, step):
        if step >= farthest:
            return value
        return lax.optimization_barrier((value, expert_weights[step], expert_weights[-step]))[0]

    gating_wide = jnp.pad(w_gating, ((0, 0), (0, WIDE - choices)))

    attended, recip, expo = attend_call(
        live, after(query, 1), key, value, some, pairs - some, early
    )
    residual, info, send_rows, send_grads = route_call(
        attended, hidden, grad, w_out, small, prev, gating_wide, table, experts
    )
    sent = lax.all_to_all(send_rows, "expert", split_axis=0, concat_axis=0, tiled=True)
    sent_grads = lax.all_to_all(send_grads, "expert", split_axis=0, concat_axis=0, tiled=True)
    expert_out, inner, factor_a, factor_b = expert_call(sent, by_turn)
    returned = lax.all_to_all(expert_out, "expert", split_axis=0, concat_axis=0, tiled=True)
    lead = shards // 4
    cuts = [(lead, shards // 2), (0, lead)] if lead else [(0, shards // 2)]
    terms, sofar = [None] * shards, None
    for low, high in cuts:
        chosen = slice(2 * low, 2 * high)
        sofar, found = expert_back_call(
            sent, sent_grads, by_turn[chosen], inner, factor_a, factor_b, low, sofar
        )
        terms[chosen] = found
    sums = RingReduce([terms[turns.index(r)] for r in range(shards)], order, 1)
    sums.start()
    sums.flight, sofar = lax.optimization_barrier((sums.flight, sofar))
    returned_dx = lax.all_to_all(sofar, "expert", split_axis=0, concat_axis=0, tiled=True)

    def before(value):
        if not sums.left:
            return value
        sums.add()
        value, sums.ready = lax.optimization_barrier((value, sums.ready))
        sums.send()
        return value

    hidden_out, part_grad, grad_prev, grad_sw, grad_vec, grad_gating = combine_call(
        before(returned), residual, info, table, grad, small, prev, gating_wide
    )
    grad_residual, grad_attended, grad_wo, grad_gain_two = residual_call(
        returned_dx, before(part_grad), residual, table, grad, small, gain_at + 1, w_out, attended
    )
    dq, dk, dv = attend_back_call(
        query, key, value, expo, grad_attended, attended, recip, cos_wide, sin_wide
    )
    while sums.left:
        dq = before(dq)
    grad_hidden = hidden_call(dq, dk, dv, qkv_weights, hidden, small, gain_at, grad_residual)
    if paired:
        own, other = qkv_weights_call(
            where, dq, dk, dv, normed_one, qkv_weights, small, gain_at, grad_wo, grad_gain_two, grad_sw, grad_vec,
            jnp.pad(grad_gating[:, :choices].reshape(1, -1), ((0, 0), (0, width - choices * choices))), shards,
        )
        got = swap(other, experts, 1)
        sums.flight, grad_hidden = lax.optimization_barrier((sums.flight, grad_hidden))
        expert_grads = sums.finish()
        got, expert_grads = lax.optimization_barrier((got, expert_grads))
        shared = RingReduce([plus(own[r], got[r]) for r in range(shards)], order, 0)
        shared.start()
        while shared.left:
            shared.turn()
        mine = shared.result().astype(bf16)
        bit = 2
        while bit < experts:
            mine = plus(mine, swap(mine, experts, bit))
            bit *= 2
        theirs = swap(mine, experts, 1)
        shared_grads = finish_call(where, mine, theirs, part, choices)
        shared_grads = [
            g[0] if at in (4, 5) else g.T if at in (0, 1, 2, 6, 8) else g
            for at, g in enumerate(shared_grads)
        ]
    else:
        grad_qkv = plain_weights_call(dq, dk, dv, normed_one)
        grad_gain_one = jnp.sum(grad_qkv * qkv_weights.astype(f32), axis=(0, 1))[None] / small[
            gain_at : gain_at + 1
        ].astype(f32)
        small_grads = jnp.concatenate(
            [grad_sw[:gain_at], grad_gain_one, grad_gain_two, grad_vec[:2]], axis=0
        )
        small_flat = (
            small_grads.reshape(small_count, shards, part).transpose(1, 0, 2).reshape(shards, -1)
        )
        gating_flat = grad_gating[:, :choices].reshape(1, -1)
        gating_both = jnp.concatenate(split2(gating_flat), axis=1)
        flat = jnp.concatenate(
            [small_flat.astype(bf16), jnp.broadcast_to(gating_both, (shards, gating_both.shape[1]))], axis=1
        )
        shared = jnp.concatenate(
            [
                grad_qkv.astype(bf16)
                .reshape(3, shards, part, width)
                .transpose(1, 0, 2, 3)
                .reshape(shards, 3 * part, width),
                grad_wo.reshape(shards, part, width),
                to_rows(flat, width),
            ],
            axis=1,
        )
        scattered = lax.psum_scatter(shared, "fsdp", scatter_dimension=0, tiled=False)
        total = lax.psum(scattered, "expert").astype(f32)
        flat_total = total[4 * part :].reshape(-1)
        small_total = flat_total[: small_count * part].reshape(small_count, part)
        at = small_count * part
        gating_total = flat_total[at : at + 2 * choices * choices].reshape(2, choices, choices)
        shared_grads = [total[at * part : (at + 1) * part].T for at in range(3)] + [
            total[3 * part : 4 * part],
            small_total[gain_at],
            small_total[gain_at + 1],
            small_total[:choices].T,
            jnp.sum(gating_total, axis=0),
            small_total[choices:gain_at].T,
            small_total[gain_at + 2 :],
        ]
        expert_grads = sums.finish()
    return (hidden_out[None], grad_hidden[None], grad_prev.T[None], *shared_grads, *expert_grads)


def solution(mesh):
    rows = P(("expert", "fsdp"), None, None)
    ins = (
        rows, rows, P(), P(), rows,
        P(None, "fsdp"), P(None, "fsdp"), P(None, "fsdp"), P("fsdp", None),
        P("fsdp"), P("fsdp"), P("fsdp", None), P(), P("fsdp", None), P(None, "fsdp"),
        P("expert", None, "fsdp"), P("expert", None, "fsdp"), P("expert", "fsdp", None), rows,
    )
    outs = (
        rows, rows, rows,
        P(None, "fsdp"), P(None, "fsdp"), P(None, "fsdp"), P("fsdp", None),
        P("fsdp"), P("fsdp"), P("fsdp", None), P(), P("fsdp", None), P(None, "fsdp"),
        P("expert", None, "fsdp"), P("expert", None, "fsdp"), P("expert", "fsdp", None),
    )
    return jax.shard_map(per_device, mesh=mesh, in_specs=ins, out_specs=outs, check_vma=False)
```

```python
import functools

import jax
import jax.numpy as jnp
from jax import lax
from jax.experimental import pallas as pl
from jax.experimental.pallas import tpu as pltpu
from jax.sharding import PartitionSpec as P

HD = 64
CAP = 256
TB = 256
PAIR = 2 * HD
WIDE = 128
SLOW = 3.0
norm_eps = 1e-05
rope_base = 10000.0
masked_score = -1e30
f32 = jnp.float32
bf16 = jnp.bfloat16
i32 = jnp.int32


def nn(a, b):
    return lax.dot_general(a, b, (((1,), (0,)), ((), ())), preferred_element_type=f32)


def nt(a, b):
    return lax.dot_general(a, b, (((1,), (1,)), ((), ())), preferred_element_type=f32)


def tn(a, b):
    return lax.dot_general(a, b, (((0,), (0,)), ((), ())), preferred_element_type=f32)


def split2(x):
    high = x.astype(bf16)
    return high, (x - high.astype(f32)).astype(bf16)


def split3(x):
    high = x.astype(bf16)
    rest = x - high.astype(f32)
    mid = rest.astype(bf16)
    return high, mid, (rest - mid.astype(f32)).astype(bf16)


def call(kernel, grid, ins, outs, args, scratch=(), flops=0, nbytes=0, vmem=60 << 20, aliases=None):
    body = kernel.func if isinstance(kernel, functools.partial) else kernel
    return pl.pallas_call(
        kernel,
        name=body.__name__,
        grid=grid,
        in_specs=ins,
        out_specs=[o[2] for o in outs],
        out_shape=[jax.ShapeDtypeStruct(o[0], o[1]) for o in outs],
        scratch_shapes=list(scratch),
        input_output_aliases=aliases or {},
        compiler_params=pltpu.CompilerParams(
            dimension_semantics=("arbitrary",) * len(grid), vmem_limit_bytes=vmem
        ),
        cost_estimate=pl.CostEstimate(
            flops=int(flops * SLOW), bytes_accessed=nbytes, transcendentals=0
        ),
    )(*args)


def whole(shape):
    zeros = (0,) * len(shape)
    return pl.BlockSpec(shape, lambda *_: zeros)


def lanes_of(shape):
    return lax.broadcasted_iota(i32, shape, len(shape) - 1)


def turn(values, cos_wide, sin_wide):
    first = lanes_of((1, PAIR)) % HD < HD // 2
    partner = jnp.where(first, pltpu.roll(values, PAIR - HD // 2, 1), pltpu.roll(values, HD // 2, 1))
    return values * cos_wide + partner * sin_wide


def eye(size):
    at = (lax.broadcasted_iota(i32, (size, size), 0), lax.broadcasted_iota(i32, (size, size), 1))
    return jnp.where(at[0] == at[1], 1.0, 0.0).astype(bf16)


def pack_kernel(
    core_ref, wq_ref, wk_ref, wv_ref, wo_ref, router_ref, const_ref, g1_ref, g2_ref, vec_ref, own_ref, other_ref
):
    part, width = wq_ref.shape
    half = part // 2
    core = core_ref[0]
    small = jnp.concatenate(
        [ref[...].astype(f32) for ref in (router_ref, const_ref, g1_ref, g2_ref, vec_ref)], axis=0
    )
    small = jnp.concatenate([small, jnp.zeros((small.shape[0], width - part), f32)], axis=1).astype(bf16)
    split = small.shape[0] // 2
    for side in range(2):
        rows = [ref[side * half : (side + 1) * half, :] for ref in (wq_ref, wk_ref, wv_ref, wo_ref)]
        rows.append(small[side * split : (side + 1) * split])

        def put(ref):
            at = 0
            for piece in rows:
                ref[at : at + piece.shape[0], :] = piece
                at += piece.shape[0]

        @pl.when(core == side)
        def _():
            put(own_ref)

        @pl.when(core != side)
        def _():
            put(other_ref)


def pack_call(core, *weights):
    part, width = weights[0].shape
    count = sum(w.shape[0] for w in weights[4:])
    shape = (4 * (part // 2) + count // 2, width)
    return call(
        pack_kernel,
        (1,),
        [pl.BlockSpec(memory_space=pltpu.SMEM)] + [whole(w.shape) for w in weights],
        [(shape, bf16, whole(shape))] * 2,
        (core, *weights),
        flops=1 << 20,
        nbytes=12 * width * part,
    )


def deal_kernel(experts, mine_ref, dealt_ref, out_ref):
    count, _, rows = dealt_ref.shape
    routes = jnp.zeros((2, rows), i32)
    for e in range(count):
        routes = routes + dealt_ref[e] * mine_ref[e]
    at = lax.broadcasted_iota(i32, (experts, rows), 0)
    named = [routes[j : j + 1] == at for j in range(2)]
    hits = jnp.where(named[0] | named[1], 1.0, 0.0).astype(bf16)
    before = lax.broadcasted_iota(i32, (rows, rows), 0) < lax.broadcasted_iota(i32, (rows, rows), 1)
    counts = nn(hits, jnp.where(before, 1.0, 0.0).astype(bf16)) + (at * CAP).astype(f32)
    out_ref[...] = jnp.zeros(out_ref.shape, f32)
    out_ref[0:2, :] = routes.astype(f32)
    for j in range(2):
        slot = jnp.sum(jnp.where(named[j], counts, 0.0), axis=0, keepdims=True)
        out_ref[2 + j : 3 + j, :] = jnp.where(routes[j : j + 1] < experts, slot, -1.0)


def deal_call(mine, dealt):
    experts, _, rows = dealt.shape
    return call(
        functools.partial(deal_kernel, experts),
        (1,),
        [pl.BlockSpec(memory_space=pltpu.SMEM), whole(dealt.shape)],
        [((8, rows), f32, whole((8, rows)))],
        (mine, dealt),
        flops=2 * 128 * rows * rows,
        nbytes=64 * rows,
    )[0]


def columns_of(table_ref):
    return table_ref[...].T.astype(i32)


def pack_experts_kernel(gate_ref, up_ref, down_ref, out_ref):
    one = eye(gate_ref.shape[2])
    out_ref[0] = nt(one, gate_ref[0]).astype(bf16)
    out_ref[1] = nt(one, up_ref[0]).astype(bf16)
    out_ref[2] = down_ref[0]


def pack_experts_call(gate, up, down):
    _, width, units = gate.shape
    shape = (3, units, width)
    return call(
        pack_experts_kernel,
        (1,),
        [whole(gate.shape)] * 2 + [whole(down.shape)],
        [(shape, bf16, whole(shape))],
        (gate, up, down),
        flops=1 << 20,
        nbytes=12 * width * units,
    )[0]


def finish_experts_kernel(own_ref, ahead_ref, back_ref, gate_ref, up_ref, down_ref):
    for at, ref in enumerate((gate_ref, up_ref, down_ref)):
        total = own_ref[at].astype(f32) + ahead_ref[at].astype(f32) + back_ref[at].astype(f32)
        ref[0] = total if at == 2 else total.T


def finish_experts_call(own, ahead, back):
    _, units, width = own.shape
    outs = [(1, width, units)] * 2 + [(1, units, width)]
    return call(
        finish_experts_kernel,
        (1,),
        [whole(own.shape)] * 3,
        [(shape, f32, whole(shape)) for shape in outs],
        (own, ahead, back),
        flops=10**10,
        nbytes=30 * units * width,
    )


def qkv_rows(hid_ref, gain, w_ref, cos_ref, sin_ref, q_ref, k_ref, v_ref, n_ref):
    width = hid_ref.shape[1]
    hidden = hid_ref[...].astype(f32)
    scale = lax.rsqrt(jnp.mean(hidden * hidden, axis=-1, keepdims=True) + norm_eps)
    normed = (hidden * scale * gain).astype(bf16)
    n_ref[...] = normed
    cos_wide, sin_wide = cos_ref[...], sin_ref[...]
    for part, (out, factor) in enumerate(((q_ref, HD**-0.5), (k_ref, 1.0))):
        full = nt(normed, w_ref[part])
        for at in range(0, width, PAIR):
            lin = full[:, at : at + PAIR]
            out[:, at : at + PAIR] = (turn(lin, cos_wide, sin_wide) * factor).astype(bf16)
    v_ref[...] = nt(normed, w_ref[2]).astype(bf16)


def qkv_kernel(gain_at, hid_ref, small_ref, w_ref, *refs):
    gain = small_ref[gain_at : gain_at + 1, :].astype(f32)
    qkv_rows(hid_ref, gain, w_ref, *refs)


def qkv_pieces_kernel(gain_at, part, where_ref, hid_ref, cos_ref, sin_ref, *refs):
    pieces, (q_ref, k_ref, v_ref, n_ref, w_ref, wo_ref, small_ref, vec_ref) = refs[:-8], refs[-8:]
    count = len(pieces) // 2
    half = part // 2
    vectors = pieces[0].shape[0] - 4 * half

    @pl.when(pl.program_id(0) == 0)
    def _():
        vec_ref[...] = jnp.zeros_like(vec_ref)
        core = where_ref[count]
        for own in range(2):
            side = core if own == 0 else 1 - core
            total = None
            for r in range(count):
                ref = pieces[own * count + r]
                shard = where_ref[r]
                row = pl.multiple_of(shard * part + side * half, 16)
                for at in range(3):
                    w_ref[at, pl.ds(row, half), :] = ref[at * half : (at + 1) * half, :]
                wo_ref[pl.ds(row, half), :] = ref[3 * half : 4 * half, :]
                moved = pltpu.roll(ref[4 * half :, :].astype(f32), shard * part, 1)
                total = moved if total is None else total + moved
            vec_ref[pl.ds(pl.multiple_of(side * vectors, 8), vectors), :] = total
        small_ref[...] = vec_ref[...].astype(bf16)

    gain = small_ref[gain_at : gain_at + 1, :].astype(f32)
    qkv_rows(hid_ref, gain, w_ref, cos_ref, sin_ref, q_ref, k_ref, v_ref, n_ref)


def qkv_specs(hidden):
    rows, width = hidden.shape
    row = pl.BlockSpec((TB, width), lambda i: (i, 0))
    return dict(
        row=row,
        tab=pl.BlockSpec((TB, PAIR), lambda i: (i, 0)),
        outs=[((rows, width), bf16, row)] * 4,
        flops=6 * rows * width * width,
        nbytes=10 * rows * width + 6 * width * width,
    )


def qkv_call(hidden, small, gain_at, weights, cos_wide, sin_wide):
    s = qkv_specs(hidden)
    return call(
        functools.partial(qkv_kernel, gain_at),
        (hidden.shape[0] // TB,),
        [s["row"], whole(small.shape), whole(weights.shape), s["tab"], s["tab"]],
        s["outs"],
        (hidden, small, weights, cos_wide, sin_wide),
        flops=s["flops"],
        nbytes=s["nbytes"],
    )


def qkv_pieces_call(hidden, where, own, other, gain_at, part, cos_wide, sin_wide):
    s = qkv_specs(hidden)
    width = hidden.shape[1]
    pieces = list(own) + list(other)
    return call(
        functools.partial(qkv_pieces_kernel, gain_at, part),
        (hidden.shape[0] // TB,),
        [pl.BlockSpec(memory_space=pltpu.SMEM), s["row"], s["tab"], s["tab"]]
        + [whole(piece.shape) for piece in pieces],
        s["outs"]
        + [
            ((3, width, width), bf16, whole((3, width, width))),
            ((width, width), bf16, whole((width, width))),
            ((WIDE, width), bf16, whole((WIDE, width))),
        ],
        (where, hidden, cos_wide, sin_wide, *pieces),
        scratch=[pltpu.VMEM((WIDE, width), f32)],
        flops=s["flops"],
        nbytes=s["nbytes"],
    )


def attend_kernel(len_ref, q_ref, k_ref, v_ref, *refs):
    o_ref, r_ref, e_ref = refs[-3:]
    rows = q_ref.shape[0]
    live = len_ref[0]
    low_lanes = lanes_of((1, PAIR)) < HD
    keys = k_ref[...]
    nil = jnp.zeros_like(keys)
    key_heads = (jnp.where(low_lanes, keys, nil), jnp.where(low_lanes, nil, keys))
    value_t = v_ref[...].T
    zeros = jnp.zeros((HD, rows), bf16)
    ones = jnp.ones((HD, rows), bf16)
    value_heads = (
        jnp.concatenate([value_t[:HD], zeros, ones, zeros], axis=0),
        jnp.concatenate([zeros, value_t[HD:], zeros, ones], axis=0),
    )
    key_at = lax.broadcasted_iota(i32, (TB, TB), 0)
    causal = key_at <= lax.broadcasted_iota(i32, (TB, TB), 1)
    for i in range(rows // TB):
        query = q_ref[i * TB : (i + 1) * TB, :]
        tall = (i + 1) * TB
        both = nt(jnp.concatenate([k[:tall] for k in key_heads], axis=0), query)
        expos = []
        for head in range(2):
            blocks = []
            for j in range(i + 1):
                at = head * tall + j * TB
                score = both[at : at + TB]
                keep = None
                if j > 0:
                    keep = key_at < live - j * TB
                if j == i:
                    keep = causal if keep is None else keep & causal
                if keep is not None:
                    score = jnp.where(keep, score, masked_score)
                blocks.append(score)
            top = jnp.max(blocks[0], axis=0, keepdims=True)
            for block in blocks[1:]:
                top = jnp.maximum(top, jnp.max(block, axis=0, keepdims=True))
            for j, block in enumerate(blocks):
                expo = jnp.exp(block - top).astype(bf16)
                e_ref[0, head, i * (i + 1) // 2 + j] = expo
                expos.append(expo)
        total = nn(
            jnp.concatenate([v[:, :tall] for v in value_heads], axis=1), jnp.concatenate(expos, axis=0)
        )
        recip = 1.0 / total[PAIR:]
        o_ref[i * TB : (i + 1) * TB, :] = (total[:PAIR] * recip).T.astype(bf16)
        r_ref[i * TB : (i + 1) * TB, :] = recip.T


def attend_call(live, query, key, value, first, count, earlier=()):
    rows, width = query.shape
    pairs = width // PAIR
    steps = rows // TB
    tiles = steps * (steps + 1) // 2
    col = pl.BlockSpec((rows, PAIR), lambda p: (0, p + first))
    expo = (1, 2, tiles, TB, TB)
    return call(
        attend_kernel,
        (count,),
        [pl.BlockSpec(memory_space=pltpu.SMEM), col, col, col]
        + [pl.BlockSpec(memory_space=pl.ANY)] * len(earlier),
        [
            ((rows, width), bf16, col),
            ((rows, width), f32, col),
            ((pairs,) + expo[1:], bf16, pl.BlockSpec(expo, lambda p: (p + first, 0, 0, 0, 0))),
        ],
        (live, query, key, value, *earlier),
        flops=count * 2 * tiles * TB * TB * 8 * PAIR,
        nbytes=count * (2 * tiles * TB * TB * 2 + 12 * rows * PAIR),
        aliases={4 + at: at for at in range(len(earlier))},
    )


def attend_back_kernel(
    q_ref, k_ref, v_ref, e_ref, do_ref, att_ref, r_ref, cos_ref, sin_ref, dq_ref, dk_ref, dv_ref, dqt_ref,
    dva_ref, dka_ref,
):
    rows = q_ref.shape[0]
    steps = rows // TB
    low_lanes = lanes_of((1, PAIR)) < HD

    def halves(x):
        nil = jnp.zeros_like(x)
        return jnp.where(low_lanes, x, nil), jnp.where(low_lanes, nil, x)

    scaled = do_ref[...].astype(f32) * r_ref[...]
    product_t = (scaled * att_ref[...].astype(f32)).T
    deltas = (
        jnp.sum(product_t[:HD], axis=0, keepdims=True),
        jnp.sum(product_t[HD:], axis=0, keepdims=True),
    )
    grad = scaled.astype(bf16)
    grad_heads = halves(grad)
    query_heads = halves(q_ref[...])
    value_heads = halves(v_ref[...])
    key_t = k_ref[...].T
    zeros = jnp.zeros((HD, rows), bf16)
    key_heads = (
        jnp.concatenate([key_t[:HD], zeros], axis=0),
        jnp.concatenate([zeros, key_t[HD:]], axis=0),
    )
    for i in range(steps):
        rs = slice(i * TB, (i + 1) * TB)
        tall = (i + 1) * TB
        first = i * (i + 1) // 2
        grad_prob = nt(jnp.concatenate([v[:tall] for v in value_heads], axis=0), grad[rs])
        expos = [e_ref[0, head, first : first + i + 1].reshape(tall, TB) for head in range(2)]
        scores = [
            (expos[head].astype(f32) * (grad_prob[head * tall : (head + 1) * tall] - deltas[head][:, rs])).astype(bf16)
            for head in range(2)
        ]
        value_grad = nn(
            jnp.concatenate(expos, axis=1),
            jnp.concatenate([grad_heads[0][rs], grad_heads[1][rs]], axis=0),
        )
        key_grad = nn(
            jnp.concatenate(scores, axis=1),
            jnp.concatenate([query_heads[0][rs], query_heads[1][rs]], axis=0),
        )
        dqt_ref[:, rs] = nn(
            jnp.concatenate([k[:, :tall] for k in key_heads], axis=1), jnp.concatenate(scores, axis=0)
        )
        last = i * TB
        if i > 0:
            dva_ref[:last, :] += value_grad[:last]
            dka_ref[:last, :] += key_grad[:last]
        dva_ref[last:tall, :] = value_grad[last:]
        dka_ref[last:tall, :] = key_grad[last:]
    dv_ref[...] = dva_ref[...].astype(bf16)
    dk_ref[...] = turn(dka_ref[...], cos_ref[...], -sin_ref[...]).astype(bf16)
    query_grad = dqt_ref[...].T * (HD**-0.5)
    dq_ref[...] = turn(query_grad, cos_ref[...], -sin_ref[...]).astype(bf16)


def attend_back_call(query, key, value, expo, grad, attended, recip, cos_wide, sin_wide):
    rows, width = query.shape
    pairs, _, tiles = expo.shape[:3]
    col = pl.BlockSpec((rows, PAIR), lambda p: (0, p))
    tab = whole((rows, PAIR))
    e_spec = pl.BlockSpec((1,) + expo.shape[1:], lambda p: (p, 0, 0, 0, 0))
    return call(
        attend_back_kernel,
        (pairs,),
        [col, col, col, e_spec, col, col, col, tab, tab],
        [((rows, width), bf16, col)] * 3,
        (query, key, value, expo, grad, attended, recip, cos_wide, sin_wide),
        scratch=[pltpu.VMEM((PAIR, rows), f32)] + [pltpu.VMEM((rows, PAIR), f32)] * 2,
        flops=pairs * 2 * tiles * TB * TB * 8 * PAIR,
        nbytes=pairs * 2 * tiles * TB * TB * 2 + 22 * rows * width,
    )


def padded(count):
    return -(-count // 8) * 8


def filled(rows, count):
    missing = count - sum(row.shape[0] for row in rows)
    if missing:
        rows = [*rows, jnp.zeros((missing, rows[0].shape[1]), f32)]
    return jnp.concatenate(rows, axis=0)


def rows_to_columns(rows):
    return filled(rows, 8).T


def columns_to_rows(columns):
    lane = lanes_of((columns[0].shape[0], WIDE))
    wide = jnp.zeros(lane.shape, f32)
    for k, column in enumerate(columns):
        wide = jnp.where(lane == k, column, wide)
    return wide.T


def route_kernel(
    att_ref, hid_ref, grad_ref, wo_ref, sw_ref, prev_ref, gating_ref, table_ref, all_ref,
    res_ref, info_ref, rows_ref, grads_ref, nlow_ref, rg_ref,
):
    step = pl.program_id(0)
    rows = nlow_ref.shape[0]
    blocks = rows // TB
    choices = prev_ref.shape[0]

    @pl.when(step < blocks)
    def _():
        residual = hid_ref[...].astype(f32) + nn(att_ref[...], wo_ref[...])
        res_ref[...] = residual
        scale = lax.rsqrt(jnp.mean(residual * residual, axis=-1, keepdims=True) + norm_eps)
        gain = sw_ref[choices + 5 : choices + 6, :].astype(f32)
        high, mid, low = split3(residual * scale * gain)
        some = sw_ref[: padded(choices + 8), :]
        small = nt(some, high) + nt(some, mid) + nt(some, low)
        logits = small[:choices] + tn(gating_ref[...], prev_ref[...])[:choices]
        expo = jnp.exp(logits - jnp.max(logits, axis=0, keepdims=True))
        probs = expo / jnp.sum(expo, axis=0, keepdims=True)
        alphas = []
        for c in range(2):
            pair = [small[choices + 2 * c + k : choices + 2 * c + k + 1] for k in range(2)]
            top = jnp.maximum(pair[0], pair[1])
            pair = [jnp.exp(x - top) for x in pair]
            alphas += [x / (pair[0] + pair[1]) for x in pair]
        choice = lax.broadcasted_iota(i32, logits.shape, 0).astype(f32)
        gates = [
            jnp.sum(jnp.where(choice == table_ref[j : j + 1, :], probs, 0.0), axis=0, keepdims=True)
            for j in range(2)
        ]
        scale_row = columns_to_rows([scale])[0:1]
        info_ref[...] = filled([probs, *alphas, *gates, scale_row], info_ref.shape[0])
        here = pl.ds(pl.multiple_of(step * TB, TB), TB)
        nlow_ref[here, :] = high
        grad = grad_ref[...].astype(f32)
        gate_cols = rows_to_columns(gates)
        rg_ref[0, here, :] = (gate_cols[:, 0:1] * grad).astype(bf16)
        rg_ref[1, here, :] = (gate_cols[:, 1:2] * grad).astype(bf16)

    @pl.when(step >= blocks)
    def _():
        slot = (step - blocks) * CAP + lax.broadcasted_iota(i32, (CAP, rows), 0)
        places = all_ref[...].astype(i32)
        hot = [jnp.where(places[2 + j : 3 + j] == slot, 1.0, 0.0).astype(bf16) for j in range(2)]
        rows_ref[0] = nn(hot[0] + hot[1], nlow_ref[...]).astype(bf16)
        grads_ref[0] = (nn(hot[0], rg_ref[0]) + nn(hot[1], rg_ref[1])).astype(bf16)


def route_call(attended, hidden, grad, w_out, small_weights, prev, gating, table, experts):
    rows, width = attended.shape
    blocks = rows // TB
    wide = padded(prev.shape[0] + 8)

    def block(cols):
        return pl.BlockSpec((TB, cols), lambda i: (jnp.minimum(i, blocks - 1), 0))

    def across(count):
        return pl.BlockSpec((count, TB), lambda i: (0, jnp.minimum(i, blocks - 1)))

    return call(
        route_kernel,
        (blocks + experts,),
        [
            block(width), block(width), block(width), whole(w_out.shape),
            whole(small_weights.shape), across(prev.shape[0]), whole(gating.shape), across(8), whole(table.shape),
        ],
        [
            ((rows, width), f32, block(width)),
            ((wide, rows), f32, across(wide)),
        ]
        + [
            (
                (experts, CAP, width),
                bf16,
                pl.BlockSpec((1, CAP, width), lambda i: (jnp.maximum(i - blocks, 0), 0, 0)),
            )
        ]
        * 2,
        (attended, hidden, grad, w_out, small_weights, prev, gating, table, table),
        scratch=[pltpu.VMEM((rows, width), bf16), pltpu.VMEM((2, rows, width), bf16)],
        flops=2 * rows * width * width + 6 * experts * CAP * rows * width,
        nbytes=10 * rows * width + 2 * width * width + 4 * experts * CAP * width,
    )


def ring_order(count):
    wide = 1 << ((count.bit_length() - 1) // 2)
    tall = count // wide
    if wide < 2 or wide * tall != count or tall % 2:
        return list(range(count))
    order = [z * wide for z in range(tall)]
    for turn_at in range(tall):
        z = tall - 1 - turn_at
        across = range(1, wide) if turn_at % 2 == 0 else range(wide - 1, 0, -1)
        order.extend(z * wide + y for y in across)
    return order


def ring_send(x, order, step):
    count = len(order)
    pairs = [(order[i], order[(i + step) % count]) for i in range(count)]
    return lax.ppermute(x, "fsdp", pairs)


def swap(x, experts, bit):
    return lax.ppermute(x, "expert", [(e, e ^ bit) for e in range(experts)])


def cut(x, axis):
    size = x.shape[axis]
    half = -(-size // 32) * 16
    return lax.slice_in_dim(x, 0, half, axis=axis), lax.slice_in_dim(x, half, size, axis=axis)


def ring_gather(x, order, axis, ahead_of=()):
    count = len(order)
    half = count // 2
    pieces = [None] * count
    pieces[0] = x
    ahead, back = x, x
    for k in range(half):
        if k < len(ahead_of) and ahead_of[k]:
            ahead, back, _ = lax.optimization_barrier((ahead, back, ahead_of[k]))
        if k < half - 1:
            ahead = ring_send(ahead, order, 1)
            back = ring_send(back, order, -1)
            pieces[count - k - 1] = ahead
            pieces[k + 1] = back
    first = ring_send(cut(ahead, axis)[0], order, 1)
    second = ring_send(cut(back, axis)[1], order, -1)
    pieces[half] = jnp.concatenate([first, second], axis=axis)
    return pieces


def plus(a, b):
    return (a.astype(f32) + b.astype(f32)).astype(bf16)


class RingReduce:
    def __init__(self, parts, order, axis):
        self.parts, self.order, self.axis = parts, order, axis
        self.left = len(order) // 2 - 1
        self.flight = None

    def start(self):
        first, second = cut(self.parts[len(self.order) // 2], self.axis)
        self.flight = (ring_send(first, self.order, 1), ring_send(second, self.order, -1))

    def add(self):
        k, axis = self.left, self.axis
        ahead, back = self.flight
        mine, other = self.parts[k], self.parts[len(self.order) - k]
        if k == len(self.order) // 2 - 1:
            low, high = cut(mine, axis)
            mine = jnp.concatenate([plus(low, ahead), high], axis=axis)
            low, high = cut(other, axis)
            other = jnp.concatenate([low, plus(high, back)], axis=axis)
        else:
            mine, other = plus(mine, ahead), plus(other, back)
        self.ready = (mine, other)
        self.left = k - 1

    def send(self):
        mine, other = self.ready
        self.flight = (ring_send(mine, self.order, 1), ring_send(other, self.order, -1))

    def turn(self):
        self.add()
        self.send()

    def finish(self):
        return finish_experts_call(self.parts[0], *self.flight)

    def result(self):
        return self.parts[0].astype(f32) + self.flight[0].astype(f32) + self.flight[1].astype(f32)


class Copies:
    def __init__(self, sems):
        self.sems, self.count = sems, 0

    def make(self, src, dst):
        self.count += 1
        return pltpu.make_async_copy(src, dst, self.sems.at[self.count - 1])


def expert_kernel(steps, x_ref, *refs):
    pieces, refs = refs[: 2 * steps], refs[2 * steps :]
    y_ref, inner_ref, fa_ref, fb_ref, acc_ref, buf, sems = refs
    step = pl.program_id(0)
    units = pieces[0].shape[1]
    copies = Copies(sems)
    loads = [
        [
            copies.make(pieces[2 * at + side], buf.at[at % 2, :, pl.ds(side * units, units), :])
            for side in range(2)
        ]
        for at in range(steps)
    ]
    for at in range(steps):

        @pl.when(step == at)
        def _():
            for ahead in (at, at + 1) if at == 0 else (at + 1,):
                if ahead < steps:
                    for copy in loads[ahead]:
                        copy.start()
            for copy in loads[at]:
                copy.wait()

    weights = buf.at[lax.rem(step, 2)]
    rows_in = x_ref[...].reshape(acc_ref.shape[0], x_ref.shape[2])
    gate = nt(rows_in, weights[0])
    up = nt(rows_in, weights[1])
    sig = 0.5 * jnp.tanh(0.5 * gate) + 0.5
    act = gate * sig
    inner = (act * up).astype(bf16)
    inner_ref[0] = inner
    fa_ref[0] = (up * (sig + act * (1.0 - sig))).astype(bf16)
    fb_ref[0] = act.astype(bf16)
    out = nn(inner, weights[2])

    @pl.when(step == 0)
    def _():
        acc_ref[...] = out

    @pl.when((step > 0) & (step < steps - 1))
    def _():
        acc_ref[...] += out

    @pl.when(step == steps - 1)
    def _():
        y_ref[...] = (acc_ref[...] + out).astype(bf16).reshape(y_ref.shape)


def expert_back_kernel(steps, earlier, last, x_ref, g_ref, inner_ref, fa_ref, fb_ref, *refs):
    pieces, refs = refs[: 2 * steps], refs[2 * steps :]
    first, refs = (refs[0], refs[1:]) if earlier else (None, refs)
    dx_ref, dw_refs = refs[0], refs[1 : 1 + 2 * steps]
    acc_ref, term_buf, buf, sems = refs[1 + 2 * steps :]
    step = pl.program_id(0)
    units = pieces[0].shape[1]
    rows = acc_ref.shape[0]
    copies = Copies(sems)
    loads, stores = [], []
    for at in range(steps):
        loads.append(
            [
                copies.make(pieces[2 * at + side], buf.at[at % 2, :, pl.ds(side * units, units), :])
                for side in range(2)
            ]
        )
        stores.append(
            [
                copies.make(term_buf.at[at % 2, :, pl.ds(side * units, units), :], dw_refs[2 * at + side])
                for side in range(2)
            ]
        )
    for at in range(steps):

        @pl.when(step == at)
        def _():
            for ahead in (at, at + 1) if at == 0 else (at + 1,):
                if ahead < steps:
                    for copy in loads[ahead]:
                        copy.start()
            for copy in loads[at]:
                copy.wait()
            if at >= 2:
                for copy in stores[at - 2]:
                    copy.wait()

    slot = lax.rem(step, 2)
    weights = buf.at[slot]
    rows_in = x_ref[...].reshape(rows, x_ref.shape[2])
    grad_in = g_ref[...].reshape(rows, g_ref.shape[2])
    grad_inner = nt(grad_in, weights[2])
    grads = jnp.concatenate(
        [(grad_inner * ref[0].astype(f32)).astype(bf16) for ref in (fa_ref, fb_ref)], axis=1
    )
    both = (2, 2 * units, rows_in.shape[1])
    term_buf[slot, 0:2] = tn(grads, rows_in).astype(bf16).reshape(both)
    term_buf[slot, 2] = tn(inner_ref[0], grad_in).astype(bf16)
    for at in range(steps):

        @pl.when(step == at)
        def _():
            for copy in stores[at]:
                copy.start()

    out = nn(grads, weights[0:2].reshape(grads.shape[1], grad_in.shape[1]))

    @pl.when(step == 0)
    def _():
        acc_ref[...] = out if first is None else out + first[...]

    @pl.when((step > 0) & (step < steps - 1))
    def _():
        acc_ref[...] += out

    @pl.when(step == steps - 1)
    def _():
        total = acc_ref[...] + out if steps > 1 else acc_ref[...]
        dx_ref[...] = total.astype(bf16).reshape(dx_ref.shape) if last else total
        for at in range(max(0, steps - 2), steps):
            for copy in stores[at]:
                copy.wait()


def expert_specs(sent, pieces):
    experts, _, width = sent.shape
    chunks = len(pieces)
    units = pieces[0].shape[1]
    rows = experts * CAP
    return dict(
        rows=rows,
        steps=chunks // 2,
        units=units,
        width=width,
        any=[pl.BlockSpec(memory_space=pl.ANY)] * chunks,
        x=pl.BlockSpec((experts, CAP, width), lambda c: (0, 0, 0)),
        flops=6 * rows * width * chunks * units,
        nbytes=6 * chunks * units * (rows + width) + 4 * rows * width,
        acc=pltpu.VMEM((rows, width), f32),
        buf=pltpu.VMEM((2, 3, 2 * units, width), bf16),
    )


def expert_call(sent, pieces):
    s = expert_specs(sent, pieces)
    unit = pl.BlockSpec((1, s["rows"], 2 * s["units"]), lambda c: (c, 0, 0))
    hidden = ((s["steps"], s["rows"], 2 * s["units"]), bf16, unit)
    return call(
        functools.partial(expert_kernel, s["steps"]),
        (s["steps"],),
        [s["x"], *s["any"]],
        [(sent.shape, bf16, s["x"])] + [hidden] * 3,
        (sent, *pieces),
        scratch=[s["acc"], s["buf"], pltpu.SemaphoreType.DMA((2 * s["steps"],))],
        flops=s["flops"],
        nbytes=s["nbytes"],
    )


def expert_back_call(sent, sent_grads, pieces, inner, factor_a, factor_b, at, earlier=None):
    s = expert_specs(sent, pieces)
    steps = s["steps"]
    unit = pl.BlockSpec((1, s["rows"], 2 * s["units"]), lambda c: (c + at, 0, 0))
    sums = (s["rows"], s["width"])
    outs = call(
        functools.partial(expert_back_kernel, steps, earlier is not None, at == 0),
        (steps,),
        [s["x"], s["x"], unit, unit, unit, *s["any"]]
        + ([whole(sums)] if earlier is not None else []),
        [(sent.shape, bf16, s["x"]) if at == 0 else (sums, f32, whole(sums))]
        + [(pieces[0].shape, bf16, pl.BlockSpec(memory_space=pl.ANY))] * (2 * steps),
        (sent, sent_grads, inner, factor_a, factor_b, *pieces) + (() if earlier is None else (earlier,)),
        scratch=[s["acc"], s["buf"], s["buf"], pltpu.SemaphoreType.DMA((4 * steps,))],
        flops=2 * s["flops"],
        nbytes=2 * s["nbytes"],
    )
    return outs[0], outs[1:]


def combine_kernel(
    y_ref, res_ref, info_ref, table_ref, grad_ref, sw_ref, prev_ref, gating_ref,
    out_ref, part_ref, gprev_ref, gsw_ref, gvec_ref, ggat_ref,
):
    step = pl.program_id(0)
    choices = prev_ref.shape[0]
    experts = y_ref.shape[0]
    slots = experts * CAP
    some = sw_ref[: info_ref.shape[0], :]
    gain = some[choices + 5 : choices + 6].astype(f32)
    vectors = [some[choices + 6 + c : choices + 7 + c].astype(f32) for c in range(2)]

    def info(at):
        return info_ref[at : at + 1, :]

    routes = [table_ref[j : j + 1, :] for j in range(2)]
    gates = [info(choices + 4), info(choices + 5)]
    alphas = [[info(choices + 2 * c + k) for k in range(2)] for c in range(2)]
    is_const = [[jnp.where(r == experts + 2 + c, 1.0, 0.0) for c in range(2)] for r in routes]
    on_normed = [
        jnp.where(routes[j] == experts + 1, 1.0, 0.0)
        + is_const[j][0] * alphas[0][0]
        + is_const[j][1] * alphas[1][0]
        for j in range(2)
    ]
    weight_const = [gates[0] * is_const[0][c] + gates[1] * is_const[1][c] for c in range(2)]
    weight_vector = [weight_const[c] * alphas[c][1] for c in range(2)]
    direct = gates[0] * on_normed[0] + gates[1] * on_normed[1]
    cols = rows_to_columns(
        [*gates, info(choices + 6), direct, *weight_vector, table_ref[2:3, :], table_ref[3:4, :]]
    )

    grad_low = grad_ref[...]
    grad = grad_low.astype(f32)
    residual = res_ref[...]
    normed = residual * cols[:, 2:3] * gain
    normed_high, normed_mid = split2(normed)
    rows_out = y_ref[...].reshape(slots, y_ref.shape[2])
    slot = lanes_of((TB, slots))
    mixed = residual + cols[:, 3:4] * normed
    for c in range(2):
        mixed = mixed + cols[:, 4 + c : 5 + c] * vectors[c]
    dots = []
    for j in range(2):
        hot = jnp.where(cols[:, 6 + j : 7 + j].astype(i32) == slot, 1.0, 0.0).astype(bf16)
        rows_j = nn(hot, rows_out)
        mixed = mixed + cols[:, j : j + 1] * rows_j
        dots.append(jnp.sum(grad * rows_j, axis=-1, keepdims=True))
    out_ref[...] = mixed.astype(bf16)
    dots.append(jnp.sum(grad * normed, axis=-1, keepdims=True))
    dots = columns_to_rows(dots)
    dot_normed = dots[2:3]
    by_small = nt(some, grad_low)
    dot_vectors = [by_small[choices + 6 + c : choices + 7 + c] for c in range(2)]

    probs = info_ref[:choices, :]
    choice = lax.broadcasted_iota(i32, probs.shape, 0).astype(f32)
    grad_probs = jnp.zeros_like(probs)
    for j in range(2):
        grad_gate = dots[j : j + 1] + on_normed[j] * dot_normed
        for c in range(2):
            grad_gate = grad_gate + is_const[j][c] * alphas[c][1] * dot_vectors[c]
        grad_probs = grad_probs + jnp.where(choice == routes[j], grad_gate, 0.0)
    pieces = [probs * (grad_probs - jnp.sum(probs * grad_probs, axis=0, keepdims=True))]
    for c in range(2):
        grad_alpha = (weight_const[c] * dot_normed, weight_const[c] * dot_vectors[c])
        mean = alphas[c][0] * grad_alpha[0] + alphas[c][1] * grad_alpha[1]
        pieces += [alphas[c][k] * (grad_alpha[k] - mean) for k in range(2)]
    high, mid, low = split3(filled(pieces, some.shape[0]))
    part_ref[...] = cols[:, 3:4] * grad + tn(
        jnp.concatenate([high, mid, low], axis=0), jnp.concatenate([some] * 3, axis=0)
    )
    gating = gating_ref[...]
    gprev_ref[...] = (
        tn(gating, high[:choices]) + tn(gating, mid[:choices]) + tn(gating, low[:choices])
    )[:choices]
    grad_sw = nn(high, normed_high) + nn(mid, normed_high) + nn(high, normed_mid)
    coef_high, coef_mid = split2(filled(weight_vector, gvec_ref.shape[0]))
    grad_vec = nn(coef_high, grad_low) + nn(coef_mid, grad_low)
    prev = prev_ref[...]
    grad_gating = nt(prev, high) + nt(prev, mid) + nt(prev, low)

    @pl.when(step == 0)
    def _():
        gsw_ref[...] = grad_sw
        gvec_ref[...] = grad_vec
        ggat_ref[...] = grad_gating

    @pl.when(step > 0)
    def _():
        gsw_ref[...] += grad_sw
        gvec_ref[...] += grad_vec
        ggat_ref[...] += grad_gating


def combine_call(back, residual, info, table, grad, small_weights, prev, gating_back):
    rows, width = residual.shape
    wide = info.shape[0]
    choices = prev.shape[0]
    slots = back.shape[0] * CAP

    def block(cols):
        return pl.BlockSpec((TB, cols), lambda i: (i, 0))

    def across(count):
        return pl.BlockSpec((count, TB), lambda i: (0, i))

    return call(
        combine_kernel,
        (rows // TB,),
        [
            whole(back.shape), block(width), across(wide), across(8), block(width),
            whole(small_weights.shape), across(choices), whole(gating_back.shape),
        ],
        [
            ((rows, width), bf16, block(width)),
            ((rows, width), f32, block(width)),
            ((choices, rows), f32, across(choices)),
            ((wide, width), f32, whole((wide, width))),
            ((8, width), f32, whole((8, width))),
            ((choices, wide), f32, whole((choices, wide))),
        ],
        (back, residual, info, table, grad, small_weights, prev, gating_back),
        flops=1 << 20,
        nbytes=1 << 20,
    )


def residual_kernel(
    gain_at, dx_ref, part_ref, res_ref, table_ref, grad_ref, sw_ref, wo_ref, att_ref,
    gres_ref, gatt_ref, gwo_ref, ggain_ref, acc_ref,
):
    step = pl.program_id(0)
    experts = dx_ref.shape[0]
    slots = experts * CAP
    slot = lanes_of((TB, slots))
    cols = columns_of(table_ref)
    hot = jnp.where((cols[:, 2:3] == slot) | (cols[:, 3:4] == slot), 1.0, 0.0).astype(bf16)
    grad_normed = part_ref[...] + nn(hot, dx_ref[...].reshape(slots, dx_ref.shape[2]))
    residual = res_ref[...]
    scale = lax.rsqrt(jnp.mean(residual * residual, axis=-1, keepdims=True) + norm_eps)
    unit = residual * scale
    grad_gain = jnp.sum(grad_normed * unit, axis=0, keepdims=True)
    scaled = grad_normed * sw_ref[gain_at : gain_at + 1, :].astype(f32)
    grad_residual = grad_ref[...].astype(f32) + scale * (
        scaled - unit * jnp.mean(scaled * unit, axis=-1, keepdims=True)
    )
    gres_ref[...] = grad_residual
    low = grad_residual.astype(bf16)
    gatt_ref[...] = nt(low, wo_ref[...]).astype(bf16)
    grad_out = tn(att_ref[...], low)

    @pl.when(step == 0)
    def _():
        acc_ref[...] = grad_out
        ggain_ref[...] = grad_gain

    @pl.when(step > 0)
    def _():
        acc_ref[...] += grad_out
        ggain_ref[...] += grad_gain

    @pl.when(step == pl.num_programs(0) - 1)
    def _():
        gwo_ref[...] = acc_ref[...].astype(bf16)


def residual_call(dx, part, residual, table, grad, small_weights, gain_at, w_out, attended):
    rows, width = residual.shape
    slots = dx.shape[0] * CAP

    def block(cols):
        return pl.BlockSpec((TB, cols), lambda i: (i, 0))

    return call(
        functools.partial(residual_kernel, gain_at),
        (rows // TB,),
        [
            whole(dx.shape), block(width), block(width), pl.BlockSpec((8, TB), lambda i: (0, i)), block(width),
            whole(small_weights.shape),
            whole(w_out.shape), block(width),
        ],
        [
            ((rows, width), f32, block(width)),
            ((rows, width), bf16, block(width)),
            ((width, width), bf16, whole((width, width))),
            ((1, width), f32, whole((1, width))),
        ],
        (dx, part, residual, table, grad, small_weights, w_out, attended),
        scratch=[pltpu.VMEM((width, width), f32)],
        flops=2 * slots * rows * width + 4 * rows * width * width,
        nbytes=18 * rows * width + 2 * slots * width,
    )


def qkv_weights_kernel(
    gain_at, where_ref, dq_ref, dk_ref, dv_ref, n_ref, w_ref, small_ref, gwo_ref, ggain_ref, gsw_ref, gvec_ref,
    ggat_ref, own_ref, other_ref, acc_ref,
):
    step = pl.program_id(0)
    count, _, width = own_ref.shape
    part = width // count
    half = part // 2
    shards = dq_ref.shape[1] // part
    normed = n_ref[...]
    core = where_ref[count]
    gain_grad = jnp.zeros((1, width), f32)

    def put(side, shard, at, value):
        rel = where_ref[count + 1 + shard]

        @pl.when(core == side)
        def _():
            own_ref[rel, at : at + value.shape[0], :] = value

        @pl.when(core != side)
        def _():
            other_ref[rel, at : at + value.shape[0], :] = value

    for at, ref in enumerate((dq_ref, dk_ref, dv_ref, None)):
        if ref is None:
            term = gwo_ref[...]
        else:
            full = tn(ref[...], normed)
            gain_grad = gain_grad + jnp.sum(full * w_ref[at].astype(f32), axis=0, keepdims=True)
            term = full.astype(bf16)
        for m in range(shards):
            for side in range(2):
                row = m * part + side * half
                put(side, step * shards + m, at * half, term[row : row + half])

    @pl.when(step == 0)
    def _():
        acc_ref[...] = gain_grad

    @pl.when(step > 0)
    def _():
        acc_ref[...] += gain_grad

    @pl.when(step == pl.num_programs(0) - 1)
    def _():
        gain_one = acc_ref[...] / small_ref[gain_at : gain_at + 1, :].astype(f32)
        vectors = jnp.concatenate(
            [gsw_ref[:gain_at, :], gain_one, ggain_ref[...], gvec_ref[:2, :]], axis=0
        )
        gating_high = ggat_ref[...].astype(bf16).astype(f32)
        gating = (gating_high, ggat_ref[...] - gating_high)
        lanes = lanes_of((1, width)) < part
        split = vectors.shape[0] // 2
        spare = jnp.zeros((16 - split - 1, width), f32)
        for m in range(count):
            here = vectors if m == 0 else pltpu.roll(vectors, width - m * part, 1)
            here = jnp.where(lanes, here, 0.0)
            for side in range(2):
                block = jnp.concatenate(
                    [here[side * split : (side + 1) * split], gating[side], spare], axis=0
                )
                put(side, m, 4 * half, block.astype(bf16))


def qkv_weights_call(where, dq, dk, dv, normed, weights, small, gain_at, gwo, ggain, gsw, gvec, ggat, count):
    rows, width = normed.shape
    steps = 2
    cols = width // steps
    col = pl.BlockSpec((rows, cols), lambda c: (0, c))
    part = width // count
    shape = (count, 2 * part + 16, width)
    return call(
        functools.partial(qkv_weights_kernel, gain_at),
        (steps,),
        [
            pl.BlockSpec(memory_space=pltpu.SMEM), col, col, col, whole(normed.shape),
            pl.BlockSpec((3, cols, width), lambda c: (0, c, 0)), whole(small.shape),
            pl.BlockSpec((cols, width), lambda c: (c, 0)), whole(ggain.shape), whole(gsw.shape), whole(gvec.shape),
            whole(ggat.shape),
        ],
        [(shape, bf16, whole(shape))] * 2,
        (where, dq, dk, dv, normed, weights, small, gwo, ggain, gsw, gvec, ggat),
        scratch=[pltpu.VMEM((1, width), f32)],
        flops=6 * rows * width * width,
        nbytes=8 * rows * width + 18 * width * width,
    )


def finish_kernel(
    choices, where_ref, mine_ref, theirs_ref, gq_ref, gk_ref, gv_ref, gwo_ref, g1_ref, g2_ref, router_ref, gat_ref,
    const_ref, vec_ref,
):
    part, width = gwo_ref.shape
    half = part // 2
    core = where_ref[where_ref.shape[0] // 2]

    def side(which, at, size):
        first = mine_ref[at : at + size, :].astype(f32)
        second = theirs_ref[at : at + size, :].astype(f32)
        return jnp.where(core == which, first, second)

    for at, ref in enumerate((gq_ref, gk_ref, gv_ref, gwo_ref)):
        both = jnp.concatenate([side(0, at * half, half), side(1, at * half, half)], axis=0)
        ref[...] = both
    split = (choices + 8) // 2
    low, high = side(0, 4 * half, 16), side(1, 4 * half, 16)
    small = jnp.concatenate([low[:split, :WIDE], high[:split, :WIDE]], axis=0)
    router_ref[...] = small[:choices, :part]
    const_ref[...] = small[choices : choices + 4, :part]
    g1_ref[...] = small[choices + 4 : choices + 5, :part]
    g2_ref[...] = small[choices + 5 : choices + 6, :part]
    vec_ref[...] = small[choices + 6 : choices + 8, :part]
    gating = (low + high)[split : split + 1, :]
    for at in range(choices):
        moved = gating if at == 0 else pltpu.roll(gating, width - at * choices, 1)
        gat_ref[at : at + 1, :] = moved[:, :choices]


def finish_call(where, mine, theirs, part, choices):
    width = mine.shape[1]
    outs = [(part, width)] * 4 + [
        (1, part), (1, part), (choices, part), (choices, choices), (4, part), (2, part),
    ]
    return call(
        functools.partial(finish_kernel, choices),
        (1,),
        [pl.BlockSpec(memory_space=pltpu.SMEM), whole(mine.shape), whole(mine.shape)],
        [(shape, f32, whole(shape)) for shape in outs],
        (where, mine, theirs),
        flops=1 << 20,
        nbytes=20 * part * width,
    )


def plain_weights_kernel(dq_ref, dk_ref, dv_ref, n_ref, out_ref):
    normed = n_ref[...]
    for part, ref in enumerate((dq_ref, dk_ref, dv_ref)):
        out_ref[part] = tn(ref[...], normed)


def plain_weights_call(dq, dk, dv, normed):
    rows, width = normed.shape
    col = pl.BlockSpec((rows, 256), lambda c: (0, c))
    return call(
        plain_weights_kernel,
        (width // 256,),
        [col, col, col, whole((rows, width))],
        [((3, width, width), f32, pl.BlockSpec((3, 256, width), lambda c: (0, c, 0)))],
        (dq, dk, dv, normed),
        flops=6 * rows * width * width,
        nbytes=8 * rows * width + 12 * width * width,
    )[0]


def hidden_kernel(gain_at, dq_ref, dk_ref, dv_ref, w_ref, hid_ref, small_ref, gres_ref, out_ref):
    grad_normed = nn(dq_ref[...], w_ref[0]) + nn(dk_ref[...], w_ref[1]) + nn(dv_ref[...], w_ref[2])
    hidden = hid_ref[...].astype(f32)
    scale = lax.rsqrt(jnp.mean(hidden * hidden, axis=-1, keepdims=True) + norm_eps)
    unit = hidden * scale
    scaled = grad_normed * small_ref[gain_at : gain_at + 1, :].astype(f32)
    out_ref[...] = gres_ref[...] + scale * (
        scaled - unit * jnp.mean(scaled * unit, axis=-1, keepdims=True)
    )


def hidden_call(dq, dk, dv, weights, hidden, small, gain_at, grad_residual):
    rows, width = hidden.shape
    row = pl.BlockSpec((TB, width), lambda i: (i, 0))
    return call(
        functools.partial(hidden_kernel, gain_at),
        (rows // TB,),
        [row, row, row, whole(weights.shape), row, whole(small.shape), row],
        [((rows, width), f32, row)],
        (dq, dk, dv, weights, hidden, small, grad_residual),
        flops=1 << 20,
        nbytes=1 << 20,
    )[0]


def rope_wide(length):
    inverse = rope_base ** (-(2.0 * jnp.arange(HD // 2, dtype=f32)) / HD)
    angles = jnp.arange(length, dtype=f32)[:, None] * inverse[None, :]
    cosine, sine = jnp.cos(angles), jnp.sin(angles)
    return (
        jnp.concatenate([cosine] * 4, axis=1),
        jnp.concatenate([-sine, sine, -sine, sine], axis=1),
    )


def to_rows(flat, width):
    count = -(-flat.shape[1] // width)
    return jnp.pad(flat, ((0, 0), (0, count * width - flat.shape[1]))).reshape(
        flat.shape[0], count, width
    )


def per_device(
    hidden_in,
    prev_logits,
    seq_lengths,
    seq_order,
    routes,
    w_query,
    w_key,
    w_value,
    w_output,
    gain_attn,
    gain_moe,
    w_router,
    w_gating,
    w_const,
    v_const,
    w_gate,
    w_up,
    w_down,
    out_grad,
):
    rows, width = hidden_in.shape[1:]
    experts = lax.axis_size("expert")
    shards = lax.axis_size("fsdp")
    choices = w_router.shape[1]
    part = width // shards
    hidden = hidden_in.reshape(rows, width)
    grad = out_grad.reshape(rows, width)
    prev = prev_logits.reshape(rows, choices).T

    fsdp_here = lax.axis_index("fsdp")
    own = lax.axis_index("expert") * shards + fsdp_here
    live = lax.dynamic_slice(seq_lengths, (own,), (1,))
    dealt = lax.all_gather(routes.reshape(rows, 2).T, "expert", axis=0, tiled=False)
    peers = jnp.arange(experts, dtype=i32) * shards + fsdp_here
    table = deal_call((seq_order[peers] == own).astype(i32), dealt)
    cos_wide, sin_wide = rope_wide(rows)

    gain_at = choices + 4
    small_count = choices + 8
    order = ring_order(shards)
    place = jnp.asarray([order.index(m) for m in range(shards)], dtype=i32)
    spot = place[fsdp_here]
    core = lax.rem(lax.axis_index("expert"), 2)
    paired = part % 32 == 0 and small_count == 16 and shards % 2 == 0 and experts & (experts - 1) == 0
    ring = jnp.asarray(order, dtype=i32)
    where = jnp.concatenate(
        [ring[(spot + jnp.arange(shards, dtype=i32)) % shards], core[None], (place - spot) % shards]
    )
    expert_pack = pack_experts_call(w_gate, w_up, w_down)
    if paired:
        pack, spare = pack_call(
            core[None], w_query.T, w_key.T, w_value.T, w_output, w_router.T, w_const.T, gain_attn[None], gain_moe[None], v_const
        )
        own = ring_gather(pack, order, 0, [(), (cos_wide, sin_wide), (dealt,), (expert_pack, table)])
        other = [spare] + [swap(piece, experts, 1) for piece in own[1:]]
        expert_pack, _ = lax.optimization_barrier((expert_pack, own[shards // 2]))
        query, key, value, normed_one, qkv_weights, w_out, small = qkv_pieces_call(
            hidden, where, own, other, gain_at, part, cos_wide, sin_wide
        )
    else:
        small_parts = jnp.concatenate(
            [w_router.T, w_const.T, gain_attn[None], gain_moe[None], v_const], axis=0
        )
        first_pack = jnp.concatenate(
            [w_query.T, w_key.T, w_value.T, to_rows(small_parts.reshape(1, -1), width)[0]], axis=0
        )
        first = lax.all_gather(first_pack, "fsdp", axis=0, tiled=False)
        w_out = lax.all_gather(w_output, "fsdp", axis=0, tiled=True)
        qkv_weights = (
            first[:, : 3 * part]
            .reshape(shards, 3, part, width)
            .transpose(1, 0, 2, 3)
            .reshape(3, width, width)
        )
        small = (
            first[:, 3 * part :]
            .reshape(shards, -1)[:, : small_count * part]
            .reshape(shards, small_count, part)
            .transpose(1, 0, 2)
            .reshape(small_count, width)
        )
        small = jnp.pad(small, ((0, WIDE - small_count), (0, 0)))
        query, key, value, normed_one = qkv_call(
            hidden, small, gain_at, qkv_weights, cos_wide, sin_wide
        )
    pairs = width // PAIR
    some = pairs // 2
    early = attend_call(live, query, key, value, 0, some)
    expert_weights = ring_gather(expert_pack, order, 1, [()] + [early[:1]])
    farthest = shards // 2
    turns = [0] + [r for k in range(1, farthest) for r in (k, shards - k)] + [farthest]
    by_turn = [expert_weights[r] for r in turns]

    def after(value, step):
        if step >= farthest:
            return value
        return lax.optimization_barrier((value, expert_weights[step], expert_weights[-step]))[0]

    gating_wide = jnp.pad(w_gating, ((0, 0), (0, WIDE - choices)))
    gating_back = jnp.pad(w_gating.T, ((0, 0), (0, WIDE - choices)))

    attended, recip, expo = attend_call(
        live, after(query, 1), key, value, some, pairs - some, early
    )
    residual, info, send_rows, send_grads = route_call(
        attended, hidden, grad, w_out, small, prev, gating_wide, table, experts
    )
    sent = lax.all_to_all(send_rows, "expert", split_axis=0, concat_axis=0, tiled=True)
    sent_grads = lax.all_to_all(send_grads, "expert", split_axis=0, concat_axis=0, tiled=True)
    expert_out, inner, factor_a, factor_b = expert_call(sent, by_turn)
    returned = lax.all_to_all(expert_out, "expert", split_axis=0, concat_axis=0, tiled=True)
    lead = shards // 4
    cuts = [(lead, shards // 2), (0, lead)] if lead else [(0, shards // 2)]
    terms, sofar = [None] * shards, None
    for low, high in cuts:
        chosen = slice(2 * low, 2 * high)
        sofar, found = expert_back_call(
            sent, sent_grads, by_turn[chosen], inner, factor_a, factor_b, low, sofar
        )
        terms[chosen] = found
    sums = RingReduce([terms[turns.index(r)] for r in range(shards)], order, 1)
    sums.start()
    sums.flight, sofar = lax.optimization_barrier((sums.flight, sofar))
    returned_dx = lax.all_to_all(sofar, "expert", split_axis=0, concat_axis=0, tiled=True)

    def before(value):
        if not sums.left:
            return value
        sums.add()
        value, sums.ready = lax.optimization_barrier((value, sums.ready))
        sums.send()
        return value

    hidden_out, part_grad, grad_prev, grad_sw, grad_vec, grad_gating = combine_call(
        before(returned), residual, info, table, grad, small, prev, gating_back
    )
    grad_residual, grad_attended, grad_wo, grad_gain_two = residual_call(
        returned_dx, part_grad, residual, table, grad, small, gain_at + 1, w_out, attended
    )
    dq, dk, dv = attend_back_call(
        query, key, value, expo, before(grad_attended), attended, recip, cos_wide, sin_wide
    )
    while sums.left:
        dq = before(dq)
    grad_hidden = hidden_call(dq, dk, dv, qkv_weights, hidden, small, gain_at, grad_residual)
    if paired:
        own, other = qkv_weights_call(
            where, dq, dk, dv, normed_one, qkv_weights, small, gain_at, grad_wo, grad_gain_two, grad_sw, grad_vec,
            jnp.pad(grad_gating[:, :choices].reshape(1, -1), ((0, 0), (0, width - choices * choices))), shards,
        )
        got = swap(other, experts, 1)
        sums.flight, grad_hidden = lax.optimization_barrier((sums.flight, grad_hidden))
        expert_grads = sums.finish()
        got, expert_grads = lax.optimization_barrier((got, expert_grads))
        shared = RingReduce([plus(own[r], got[r]) for r in range(shards)], order, 0)
        shared.start()
        while shared.left:
            shared.turn()
        mine = shared.result().astype(bf16)
        bit = 2
        while bit < experts:
            mine = plus(mine, swap(mine, experts, bit))
            bit *= 2
        theirs = swap(mine, experts, 1)
        shared_grads = finish_call(where, mine, theirs, part, choices)
        shared_grads = [
            g[0] if at in (4, 5) else g.T if at in (0, 1, 2, 6, 8) else g
            for at, g in enumerate(shared_grads)
        ]
    else:
        grad_qkv = plain_weights_call(dq, dk, dv, normed_one)
        grad_gain_one = jnp.sum(grad_qkv * qkv_weights.astype(f32), axis=(0, 1))[None] / small[
            gain_at : gain_at + 1
        ].astype(f32)
        small_grads = jnp.concatenate(
            [grad_sw[:gain_at], grad_gain_one, grad_gain_two, grad_vec[:2]], axis=0
        )
        small_flat = (
            small_grads.reshape(small_count, shards, part).transpose(1, 0, 2).reshape(shards, -1)
        )
        gating_flat = grad_gating[:, :choices].reshape(1, -1)
        gating_both = jnp.concatenate(split2(gating_flat), axis=1)
        flat = jnp.concatenate(
            [small_flat.astype(bf16), jnp.broadcast_to(gating_both, (shards, gating_both.shape[1]))], axis=1
        )
        shared = jnp.concatenate(
            [
                grad_qkv.astype(bf16)
                .reshape(3, shards, part, width)
                .transpose(1, 0, 2, 3)
                .reshape(shards, 3 * part, width),
                grad_wo.reshape(shards, part, width),
                to_rows(flat, width),
            ],
            axis=1,
        )
        scattered = lax.psum_scatter(shared, "fsdp", scatter_dimension=0, tiled=False)
        total = lax.psum(scattered, "expert").astype(f32)
        flat_total = total[4 * part :].reshape(-1)
        small_total = flat_total[: small_count * part].reshape(small_count, part)
        at = small_count * part
        gating_total = flat_total[at : at + 2 * choices * choices].reshape(2, choices, choices)
        shared_grads = [total[at * part : (at + 1) * part].T for at in range(3)] + [
            total[3 * part : 4 * part],
            small_total[gain_at],
            small_total[gain_at + 1],
            small_total[:choices].T,
            jnp.sum(gating_total, axis=0),
            small_total[choices:gain_at].T,
            small_total[gain_at + 2 :],
        ]
        expert_grads = sums.finish()
    return (hidden_out[None], grad_hidden[None], grad_prev.T[None], *shared_grads, *expert_grads)


def solution(mesh):
    rows = P(("expert", "fsdp"), None, None)
    ins = (
        rows, rows, P(), P(), rows,
        P(None, "fsdp"), P(None, "fsdp"), P(None, "fsdp"), P("fsdp", None),
        P("fsdp"), P("fsdp"), P("fsdp", None), P(), P("fsdp", None), P(None, "fsdp"),
        P("expert", None, "fsdp"), P("expert", None, "fsdp"), P("expert", "fsdp", None), rows,
    )
    outs = (
        rows, rows, rows,
        P(None, "fsdp"), P(None, "fsdp"), P(None, "fsdp"), P("fsdp", None),
        P("fsdp"), P("fsdp"), P("fsdp", None), P(), P("fsdp", None), P(None, "fsdp"),
        P("expert", None, "fsdp"), P("expert", None, "fsdp"), P("expert", "fsdp", None),
    )
    return jax.shard_map(per_device, mesh=mesh, in_specs=ins, out_specs=outs, check_vma=False)
```

```python
import functools

import jax
import jax.numpy as jnp
from jax import lax
from jax.experimental import pallas as pl
from jax.experimental.pallas import tpu as pltpu
from jax.sharding import PartitionSpec as P

HD = 64
CAP = 256
TB = 256
PAIR = 2 * HD
WIDE = 128
SLOW = 3.0
norm_eps = 1e-05
rope_base = 10000.0
masked_score = -1e30
f32 = jnp.float32
bf16 = jnp.bfloat16
i32 = jnp.int32


def nn(a, b):
    return lax.dot_general(a, b, (((1,), (0,)), ((), ())), preferred_element_type=f32)


def nt(a, b):
    return lax.dot_general(a, b, (((1,), (1,)), ((), ())), preferred_element_type=f32)


def tn(a, b):
    return lax.dot_general(a, b, (((0,), (0,)), ((), ())), preferred_element_type=f32)


def split2(x):
    high = x.astype(bf16)
    return high, (x - high.astype(f32)).astype(bf16)


def split3(x):
    high = x.astype(bf16)
    rest = x - high.astype(f32)
    mid = rest.astype(bf16)
    return high, mid, (rest - mid.astype(f32)).astype(bf16)


def call(kernel, grid, ins, outs, args, scratch=(), flops=0, nbytes=0, vmem=60 << 20, aliases=None):
    body = kernel.func if isinstance(kernel, functools.partial) else kernel
    return pl.pallas_call(
        kernel,
        name=body.__name__,
        grid=grid,
        in_specs=ins,
        out_specs=[o[2] for o in outs],
        out_shape=[jax.ShapeDtypeStruct(o[0], o[1]) for o in outs],
        scratch_shapes=list(scratch),
        input_output_aliases=aliases or {},
        compiler_params=pltpu.CompilerParams(
            dimension_semantics=("arbitrary",) * len(grid), vmem_limit_bytes=vmem
        ),
        cost_estimate=pl.CostEstimate(
            flops=int(flops * SLOW), bytes_accessed=nbytes, transcendentals=0
        ),
    )(*args)


def whole(shape):
    zeros = (0,) * len(shape)
    return pl.BlockSpec(shape, lambda *_: zeros)


def lanes_of(shape):
    return lax.broadcasted_iota(i32, shape, len(shape) - 1)


def turn(values, cos_wide, sin_wide):
    first = lanes_of((1, PAIR)) % HD < HD // 2
    partner = jnp.where(first, pltpu.roll(values, PAIR - HD // 2, 1), pltpu.roll(values, HD // 2, 1))
    return values * cos_wide + partner * sin_wide


def eye(size):
    at = (lax.broadcasted_iota(i32, (size, size), 0), lax.broadcasted_iota(i32, (size, size), 1))
    return jnp.where(at[0] == at[1], 1.0, 0.0).astype(bf16)


def pack_kernel(
    core_ref, wq_ref, wk_ref, wv_ref, wo_ref, router_ref, const_ref, g1_ref, g2_ref, vec_ref, own_ref, other_ref
):
    part, width = wq_ref.shape
    half = part // 2
    core = core_ref[0]
    small = jnp.concatenate(
        [ref[...].astype(f32) for ref in (router_ref, const_ref, g1_ref, g2_ref, vec_ref)], axis=0
    )
    small = jnp.concatenate([small, jnp.zeros((small.shape[0], width - part), f32)], axis=1).astype(bf16)
    split = small.shape[0] // 2
    for side in range(2):
        rows = [ref[side * half : (side + 1) * half, :] for ref in (wq_ref, wk_ref, wv_ref, wo_ref)]
        rows.append(small[side * split : (side + 1) * split])

        def put(ref):
            at = 0
            for piece in rows:
                ref[at : at + piece.shape[0], :] = piece
                at += piece.shape[0]

        @pl.when(core == side)
        def _():
            put(own_ref)

        @pl.when(core != side)
        def _():
            put(other_ref)


def pack_call(core, *weights):
    part, width = weights[0].shape
    count = sum(w.shape[0] for w in weights[4:])
    shape = (4 * (part // 2) + count // 2, width)
    return call(
        pack_kernel,
        (1,),
        [pl.BlockSpec(memory_space=pltpu.SMEM)] + [whole(w.shape) for w in weights],
        [(shape, bf16, whole(shape))] * 2,
        (core, *weights),
        flops=1 << 20,
        nbytes=12 * width * part,
    )


def deal_kernel(experts, mine_ref, dealt_ref, out_ref):
    count, _, rows = dealt_ref.shape
    routes = jnp.zeros((2, rows), i32)
    for e in range(count):
        routes = routes + dealt_ref[e] * mine_ref[e]
    at = lax.broadcasted_iota(i32, (experts, rows), 0)
    named = [routes[j : j + 1] == at for j in range(2)]
    hits = jnp.where(named[0] | named[1], 1.0, 0.0).astype(bf16)
    before = lax.broadcasted_iota(i32, (rows, rows), 0) < lax.broadcasted_iota(i32, (rows, rows), 1)
    counts = nn(hits, jnp.where(before, 1.0, 0.0).astype(bf16)) + (at * CAP).astype(f32)
    out_ref[...] = jnp.zeros(out_ref.shape, f32)
    out_ref[0:2, :] = routes.astype(f32)
    for j in range(2):
        slot = jnp.sum(jnp.where(named[j], counts, 0.0), axis=0, keepdims=True)
        out_ref[2 + j : 3 + j, :] = jnp.where(routes[j : j + 1] < experts, slot, -1.0)


def deal_call(mine, dealt):
    experts, _, rows = dealt.shape
    return call(
        functools.partial(deal_kernel, experts),
        (1,),
        [pl.BlockSpec(memory_space=pltpu.SMEM), whole(dealt.shape)],
        [((8, rows), f32, whole((8, rows)))],
        (mine, dealt),
        flops=2 * 128 * rows * rows,
        nbytes=64 * rows,
    )[0]


def columns_of(table_ref):
    return table_ref[...].T.astype(i32)


def pack_experts_kernel(gate_ref, up_ref, down_ref, out_ref):
    one = eye(gate_ref.shape[2])
    out_ref[0] = nt(one, gate_ref[0]).astype(bf16)
    out_ref[1] = nt(one, up_ref[0]).astype(bf16)
    out_ref[2] = down_ref[0]


def pack_experts_call(gate, up, down):
    _, width, units = gate.shape
    shape = (3, units, width)
    return call(
        pack_experts_kernel,
        (1,),
        [whole(gate.shape)] * 2 + [whole(down.shape)],
        [(shape, bf16, whole(shape))],
        (gate, up, down),
        flops=1 << 20,
        nbytes=12 * width * units,
    )[0]


def finish_experts_kernel(own_ref, ahead_ref, back_ref, gate_ref, up_ref, down_ref):
    for at, ref in enumerate((gate_ref, up_ref, down_ref)):
        total = own_ref[at].astype(f32) + ahead_ref[at].astype(f32) + back_ref[at].astype(f32)
        ref[0] = total if at == 2 else total.T


def finish_experts_call(own, ahead, back):
    _, units, width = own.shape
    outs = [(1, width, units)] * 2 + [(1, units, width)]
    return call(
        finish_experts_kernel,
        (1,),
        [whole(own.shape)] * 3,
        [(shape, f32, whole(shape)) for shape in outs],
        (own, ahead, back),
        flops=10**10,
        nbytes=30 * units * width,
    )


def qkv_rows(hid_ref, gain, w_ref, cos_ref, sin_ref, q_ref, k_ref, v_ref, n_ref):
    width = hid_ref.shape[1]
    hidden = hid_ref[...].astype(f32)
    scale = lax.rsqrt(jnp.mean(hidden * hidden, axis=-1, keepdims=True) + norm_eps)
    normed = (hidden * scale * gain).astype(bf16)
    n_ref[...] = normed
    cos_wide, sin_wide = cos_ref[...], sin_ref[...]
    for part, (out, factor) in enumerate(((q_ref, HD**-0.5), (k_ref, 1.0))):
        full = nt(normed, w_ref[part])
        for at in range(0, width, PAIR):
            lin = full[:, at : at + PAIR]
            out[:, at : at + PAIR] = (turn(lin, cos_wide, sin_wide) * factor).astype(bf16)
    v_ref[...] = nt(normed, w_ref[2]).astype(bf16)


def qkv_kernel(gain_at, hid_ref, small_ref, w_ref, *refs):
    gain = small_ref[gain_at : gain_at + 1, :].astype(f32)
    qkv_rows(hid_ref, gain, w_ref, *refs)


def qkv_pieces_kernel(gain_at, part, where_ref, hid_ref, cos_ref, sin_ref, *refs):
    pieces, (q_ref, k_ref, v_ref, n_ref, w_ref, wo_ref, small_ref, vec_ref) = refs[:-8], refs[-8:]
    count = len(pieces) // 2
    half = part // 2
    vectors = pieces[0].shape[0] - 4 * half

    @pl.when(pl.program_id(0) == 0)
    def _():
        vec_ref[...] = jnp.zeros_like(vec_ref)
        core = where_ref[count]
        for own in range(2):
            side = core if own == 0 else 1 - core
            total = None
            for r in range(count):
                ref = pieces[own * count + r]
                shard = where_ref[r]
                row = pl.multiple_of(shard * part + side * half, 16)
                for at in range(3):
                    w_ref[at, pl.ds(row, half), :] = ref[at * half : (at + 1) * half, :]
                wo_ref[pl.ds(row, half), :] = ref[3 * half : 4 * half, :]
                moved = pltpu.roll(ref[4 * half :, :].astype(f32), shard * part, 1)
                total = moved if total is None else total + moved
            vec_ref[pl.ds(pl.multiple_of(side * vectors, 8), vectors), :] = total
        small_ref[...] = vec_ref[...].astype(bf16)

    gain = small_ref[gain_at : gain_at + 1, :].astype(f32)
    qkv_rows(hid_ref, gain, w_ref, cos_ref, sin_ref, q_ref, k_ref, v_ref, n_ref)


def qkv_specs(hidden):
    rows, width = hidden.shape
    row = pl.BlockSpec((TB, width), lambda i: (i, 0))
    return dict(
        row=row,
        tab=pl.BlockSpec((TB, PAIR), lambda i: (i, 0)),
        outs=[((rows, width), bf16, row)] * 4,
        flops=6 * rows * width * width,
        nbytes=10 * rows * width + 6 * width * width,
    )


def qkv_call(hidden, small, gain_at, weights, cos_wide, sin_wide):
    s = qkv_specs(hidden)
    return call(
        functools.partial(qkv_kernel, gain_at),
        (hidden.shape[0] // TB,),
        [s["row"], whole(small.shape), whole(weights.shape), s["tab"], s["tab"]],
        s["outs"],
        (hidden, small, weights, cos_wide, sin_wide),
        flops=s["flops"],
        nbytes=s["nbytes"],
    )


def qkv_pieces_call(hidden, where, own, other, gain_at, part, cos_wide, sin_wide):
    s = qkv_specs(hidden)
    width = hidden.shape[1]
    pieces = list(own) + list(other)
    return call(
        functools.partial(qkv_pieces_kernel, gain_at, part),
        (hidden.shape[0] // TB,),
        [pl.BlockSpec(memory_space=pltpu.SMEM), s["row"], s["tab"], s["tab"]]
        + [whole(piece.shape) for piece in pieces],
        s["outs"]
        + [
            ((3, width, width), bf16, whole((3, width, width))),
            ((width, width), bf16, whole((width, width))),
            ((WIDE, width), bf16, whole((WIDE, width))),
        ],
        (where, hidden, cos_wide, sin_wide, *pieces),
        scratch=[pltpu.VMEM((WIDE, width), f32)],
        flops=s["flops"],
        nbytes=s["nbytes"],
    )


def attend_kernel(len_ref, q_ref, k_ref, v_ref, *refs):
    o_ref, r_ref, e_ref = refs[-3:]
    rows = q_ref.shape[0]
    live = len_ref[0]
    low_lanes = lanes_of((1, PAIR)) < HD
    keys = k_ref[...]
    nil = jnp.zeros_like(keys)
    key_heads = (jnp.where(low_lanes, keys, nil), jnp.where(low_lanes, nil, keys))
    value_t = v_ref[...].T
    zeros = jnp.zeros((HD, rows), bf16)
    ones = jnp.ones((HD, rows), bf16)
    value_heads = (
        jnp.concatenate([value_t[:HD], zeros, ones, zeros], axis=0),
        jnp.concatenate([zeros, value_t[HD:], zeros, ones], axis=0),
    )
    key_at = lax.broadcasted_iota(i32, (TB, TB), 0)
    causal = key_at <= lax.broadcasted_iota(i32, (TB, TB), 1)
    for i in range(rows // TB):
        query = q_ref[i * TB : (i + 1) * TB, :]
        tall = (i + 1) * TB
        both = nt(jnp.concatenate([k[:tall] for k in key_heads], axis=0), query)
        expos = []
        for head in range(2):
            blocks = []
            for j in range(i + 1):
                at = head * tall + j * TB
                score = both[at : at + TB]
                keep = None
                if j > 0:
                    keep = key_at < live - j * TB
                if j == i:
                    keep = causal if keep is None else keep & causal
                if keep is not None:
                    score = jnp.where(keep, score, masked_score)
                blocks.append(score)
            top = jnp.max(blocks[0], axis=0, keepdims=True)
            for block in blocks[1:]:
                top = jnp.maximum(top, jnp.max(block, axis=0, keepdims=True))
            for j, block in enumerate(blocks):
                expo = jnp.exp(block - top).astype(bf16)
                e_ref[0, head, i * (i + 1) // 2 + j] = expo
                expos.append(expo)
        total = nn(
            jnp.concatenate([v[:, :tall] for v in value_heads], axis=1), jnp.concatenate(expos, axis=0)
        )
        recip = 1.0 / total[PAIR:]
        o_ref[i * TB : (i + 1) * TB, :] = (total[:PAIR] * recip).T.astype(bf16)
        r_ref[i * TB : (i + 1) * TB, :] = recip.T


def attend_call(live, query, key, value, first, count, earlier=()):
    rows, width = query.shape
    pairs = width // PAIR
    steps = rows // TB
    tiles = steps * (steps + 1) // 2
    col = pl.BlockSpec((rows, PAIR), lambda p: (0, p + first))
    expo = (1, 2, tiles, TB, TB)
    return call(
        attend_kernel,
        (count,),
        [pl.BlockSpec(memory_space=pltpu.SMEM), col, col, col]
        + [pl.BlockSpec(memory_space=pl.ANY)] * len(earlier),
        [
            ((rows, width), bf16, col),
            ((rows, width), f32, col),
            ((pairs,) + expo[1:], bf16, pl.BlockSpec(expo, lambda p: (p + first, 0, 0, 0, 0))),
        ],
        (live, query, key, value, *earlier),
        flops=count * 2 * tiles * TB * TB * 8 * PAIR,
        nbytes=count * (2 * tiles * TB * TB * 2 + 12 * rows * PAIR),
        aliases={4 + at: at for at in range(len(earlier))},
    )


def attend_back_kernel(
    q_ref, k_ref, v_ref, e_ref, do_ref, att_ref, r_ref, cos_ref, sin_ref, dq_ref, dk_ref, dv_ref, dqt_ref,
    dva_ref, dka_ref,
):
    rows = q_ref.shape[0]
    steps = rows // TB
    low_lanes = lanes_of((1, PAIR)) < HD

    def halves(x):
        nil = jnp.zeros_like(x)
        return jnp.where(low_lanes, x, nil), jnp.where(low_lanes, nil, x)

    scaled = do_ref[...].astype(f32) * r_ref[...]
    product_t = (scaled * att_ref[...].astype(f32)).T
    deltas = (
        jnp.sum(product_t[:HD], axis=0, keepdims=True),
        jnp.sum(product_t[HD:], axis=0, keepdims=True),
    )
    grad = scaled.astype(bf16)
    grad_heads = halves(grad)
    query_heads = halves(q_ref[...])
    value_heads = halves(v_ref[...])
    key_t = k_ref[...].T
    zeros = jnp.zeros((HD, rows), bf16)
    key_heads = (
        jnp.concatenate([key_t[:HD], zeros], axis=0),
        jnp.concatenate([zeros, key_t[HD:]], axis=0),
    )
    for i in range(steps):
        rs = slice(i * TB, (i + 1) * TB)
        tall = (i + 1) * TB
        first = i * (i + 1) // 2
        grad_prob = nt(jnp.concatenate([v[:tall] for v in value_heads], axis=0), grad[rs])
        expos = [e_ref[0, head, first : first + i + 1].reshape(tall, TB) for head in range(2)]
        scores = [
            (expos[head].astype(f32) * (grad_prob[head * tall : (head + 1) * tall] - deltas[head][:, rs])).astype(bf16)
            for head in range(2)
        ]
        value_grad = nn(
            jnp.concatenate(expos, axis=1),
            jnp.concatenate([grad_heads[0][rs], grad_heads[1][rs]], axis=0),
        )
        key_grad = nn(
            jnp.concatenate(scores, axis=1),
            jnp.concatenate([query_heads[0][rs], query_heads[1][rs]], axis=0),
        )
        dqt_ref[:, rs] = nn(
            jnp.concatenate([k[:, :tall] for k in key_heads], axis=1), jnp.concatenate(scores, axis=0)
        )
        last = i * TB
        if i > 0:
            dva_ref[:last, :] += value_grad[:last]
            dka_ref[:last, :] += key_grad[:last]
        dva_ref[last:tall, :] = value_grad[last:]
        dka_ref[last:tall, :] = key_grad[last:]
    dv_ref[...] = dva_ref[...].astype(bf16)
    dk_ref[...] = turn(dka_ref[...], cos_ref[...], -sin_ref[...]).astype(bf16)
    query_grad = dqt_ref[...].T * (HD**-0.5)
    dq_ref[...] = turn(query_grad, cos_ref[...], -sin_ref[...]).astype(bf16)


def attend_back_call(query, key, value, expo, grad, attended, recip, cos_wide, sin_wide):
    rows, width = query.shape
    pairs, _, tiles = expo.shape[:3]
    col = pl.BlockSpec((rows, PAIR), lambda p: (0, p))
    tab = whole((rows, PAIR))
    e_spec = pl.BlockSpec((1,) + expo.shape[1:], lambda p: (p, 0, 0, 0, 0))
    return call(
        attend_back_kernel,
        (pairs,),
        [col, col, col, e_spec, col, col, col, tab, tab],
        [((rows, width), bf16, col)] * 3,
        (query, key, value, expo, grad, attended, recip, cos_wide, sin_wide),
        scratch=[pltpu.VMEM((PAIR, rows), f32)] + [pltpu.VMEM((rows, PAIR), f32)] * 2,
        flops=pairs * 2 * tiles * TB * TB * 8 * PAIR,
        nbytes=pairs * 2 * tiles * TB * TB * 2 + 22 * rows * width,
    )


def padded(count):
    return -(-count // 8) * 8


def filled(rows, count):
    missing = count - sum(row.shape[0] for row in rows)
    if missing:
        rows = [*rows, jnp.zeros((missing, rows[0].shape[1]), f32)]
    return jnp.concatenate(rows, axis=0)


def rows_to_columns(rows):
    return filled(rows, 8).T


def columns_to_rows(columns):
    lane = lanes_of((columns[0].shape[0], WIDE))
    wide = jnp.zeros(lane.shape, f32)
    for k, column in enumerate(columns):
        wide = jnp.where(lane == k, column, wide)
    return wide.T


def route_kernel(
    att_ref, hid_ref, grad_ref, wo_ref, sw_ref, prev_ref, gating_ref, table_ref,
    res_ref, info_ref, nlow_ref, rg_ref,
):
    choices = prev_ref.shape[0]
    residual = hid_ref[...].astype(f32) + nn(att_ref[...], wo_ref[...])
    res_ref[...] = residual
    scale = lax.rsqrt(jnp.mean(residual * residual, axis=-1, keepdims=True) + norm_eps)
    gain = sw_ref[choices + 5 : choices + 6, :].astype(f32)
    high, mid, low = split3(residual * scale * gain)
    some = sw_ref[: padded(choices + 8), :]
    small = nt(some, high) + nt(some, mid) + nt(some, low)
    logits = small[:choices] + tn(gating_ref[...], prev_ref[...])[:choices]
    expo = jnp.exp(logits - jnp.max(logits, axis=0, keepdims=True))
    probs = expo / jnp.sum(expo, axis=0, keepdims=True)
    alphas = []
    for c in range(2):
        pair = [small[choices + 2 * c + k : choices + 2 * c + k + 1] for k in range(2)]
        top = jnp.maximum(pair[0], pair[1])
        pair = [jnp.exp(x - top) for x in pair]
        alphas += [x / (pair[0] + pair[1]) for x in pair]
    choice = lax.broadcasted_iota(i32, logits.shape, 0).astype(f32)
    gates = [
        jnp.sum(jnp.where(choice == table_ref[j : j + 1, :], probs, 0.0), axis=0, keepdims=True)
        for j in range(2)
    ]
    scale_row = columns_to_rows([scale])[0:1]
    info_ref[...] = filled([probs, *alphas, *gates, scale_row], info_ref.shape[0])
    nlow_ref[...] = high
    grad = grad_ref[...].astype(f32)
    gate_cols = rows_to_columns(gates)
    rg_ref[0] = (gate_cols[:, 0:1] * grad).astype(bf16)
    rg_ref[1] = (gate_cols[:, 1:2] * grad).astype(bf16)


def dispatch_kernel(table_ref, nlow_ref, rg_ref, rows_ref, grads_ref):
    rows = nlow_ref.shape[0]
    slot = pl.program_id(0) * CAP + lax.broadcasted_iota(i32, (CAP, rows), 0)
    places = table_ref[...].astype(i32)
    hot = [jnp.where(places[2 + j : 3 + j] == slot, 1.0, 0.0).astype(bf16) for j in range(2)]
    rows_ref[0] = nn(hot[0] + hot[1], nlow_ref[...]).astype(bf16)
    grads_ref[0] = (nn(hot[0], rg_ref[0]) + nn(hot[1], rg_ref[1])).astype(bf16)


def route_call(attended, hidden, grad, w_out, small_weights, prev, gating, table):
    rows, width = attended.shape
    wide = padded(prev.shape[0] + 8)

    def block(cols):
        return pl.BlockSpec((TB, cols), lambda i: (i, 0))

    def across(count):
        return pl.BlockSpec((count, TB), lambda i: (0, i))

    return call(
        route_kernel,
        (rows // TB,),
        [
            block(width), block(width), block(width), whole(w_out.shape), whole(small_weights.shape),
            across(prev.shape[0]), whole(gating.shape), across(8),
        ],
        [
            ((rows, width), f32, block(width)),
            ((wide, rows), f32, across(wide)),
            ((rows, width), bf16, block(width)),
            ((2, rows, width), bf16, pl.BlockSpec((2, TB, width), lambda i: (0, i, 0))),
        ],
        (attended, hidden, grad, w_out, small_weights, prev, gating, table),
        flops=2 * rows * width * width,
        nbytes=16 * rows * width + 2 * width * width,
    )


def dispatch_call(table, nlow, route_grads, experts):
    rows, width = nlow.shape
    out = ((experts, CAP, width), bf16, pl.BlockSpec((1, CAP, width), lambda e: (e, 0, 0)))
    return call(
        dispatch_kernel,
        (experts,),
        [whole(table.shape), whole(nlow.shape), whole(route_grads.shape)],
        [out] * 2,
        (table, nlow, route_grads),
        flops=6 * experts * CAP * rows * width,
        nbytes=6 * rows * width + 4 * experts * CAP * width,
    )


def ring_order(count):
    wide = 1 << ((count.bit_length() - 1) // 2)
    tall = count // wide
    if wide < 2 or wide * tall != count or tall % 2:
        return list(range(count))
    order = [z * wide for z in range(tall)]
    for turn_at in range(tall):
        z = tall - 1 - turn_at
        across = range(1, wide) if turn_at % 2 == 0 else range(wide - 1, 0, -1)
        order.extend(z * wide + y for y in across)
    return order


def ring_send(x, order, step):
    count = len(order)
    pairs = [(order[i], order[(i + step) % count]) for i in range(count)]
    return lax.ppermute(x, "fsdp", pairs)


def swap(x, experts, bit):
    return lax.ppermute(x, "expert", [(e, e ^ bit) for e in range(experts)])


def cut(x, axis):
    size = x.shape[axis]
    half = -(-size // 32) * 16
    return lax.slice_in_dim(x, 0, half, axis=axis), lax.slice_in_dim(x, half, size, axis=axis)


def ring_gather(x, order, axis, ahead_of=()):
    count = len(order)
    half = count // 2
    pieces = [None] * count
    pieces[0] = x
    ahead, back = x, x
    for k in range(half):
        if k < len(ahead_of) and ahead_of[k]:
            ahead, back, _ = lax.optimization_barrier((ahead, back, ahead_of[k]))
        if k < half - 1:
            ahead = ring_send(ahead, order, 1)
            back = ring_send(back, order, -1)
            pieces[count - k - 1] = ahead
            pieces[k + 1] = back
    first = ring_send(cut(ahead, axis)[0], order, 1)
    second = ring_send(cut(back, axis)[1], order, -1)
    pieces[half] = (first, second)
    return pieces


def plus(a, b):
    return (a.astype(f32) + b.astype(f32)).astype(bf16)


class RingReduce:
    def __init__(self, parts, order, axis):
        self.parts, self.order, self.axis = parts, order, axis
        self.left = len(order) // 2 - 1
        self.flight = None

    def start(self):
        farthest = self.parts[len(self.order) // 2]
        first, second = farthest if isinstance(farthest, tuple) else cut(farthest, self.axis)
        self.flight = (ring_send(first, self.order, 1), ring_send(second, self.order, -1))

    def add(self):
        k, axis = self.left, self.axis
        ahead, back = self.flight
        mine, other = self.parts[k], self.parts[len(self.order) - k]
        if k == len(self.order) // 2 - 1:
            low = cut(mine, axis)[0]
            mine = lax.dynamic_update_slice_in_dim(mine, plus(low, ahead), 0, axis)
            at = low.shape[axis]
            high = cut(other, axis)[1]
            other = lax.dynamic_update_slice_in_dim(other, plus(high, back), at, axis)
        else:
            mine, other = plus(mine, ahead), plus(other, back)
        self.ready = (mine, other)
        self.left = k - 1

    def send(self):
        mine, other = self.ready
        self.flight = (ring_send(mine, self.order, 1), ring_send(other, self.order, -1))

    def turn(self):
        self.add()
        self.send()

    def finish(self):
        return finish_experts_call(self.parts[0], *self.flight)

    def result(self):
        return self.parts[0].astype(f32) + self.flight[0].astype(f32) + self.flight[1].astype(f32)


def flat(pieces):
    return [x for piece in pieces for x in (piece if isinstance(piece, tuple) else (piece,))]


def layout_of(pieces):
    return tuple(len(piece) if isinstance(piece, tuple) else 1 for piece in pieces)


def grouped(values, layout):
    values, groups = list(values), []
    for count in layout:
        groups.append(values[:count])
        values = values[count:]
    return groups, values


def chunk_copies(copies, refs, view, units, side, inward):
    made, row = [], side * units
    for ref in refs:
        rows = view.at[:, pl.ds(row, ref.shape[1]), :]
        made.append(copies.make(ref, rows) if inward else copies.make(rows, ref))
        row += ref.shape[1]
    return made


class Copies:
    def __init__(self, sems):
        self.sems, self.count = sems, 0

    def make(self, src, dst):
        self.count += 1
        return pltpu.make_async_copy(src, dst, self.sems.at[self.count - 1])


def expert_kernel(layout, x_ref, *refs):
    pieces, refs = grouped(refs, layout)
    y_ref, inner_ref, fa_ref, fb_ref, acc_ref, buf, sems = refs
    step = pl.program_id(0)
    steps = len(layout) // 2
    units = pieces[0][0].shape[1]
    copies = Copies(sems)
    loads = [
        [
            copy
            for side in range(2)
            for copy in chunk_copies(copies, pieces[2 * at + side], buf.at[at % 2], units, side, True)
        ]
        for at in range(steps)
    ]
    for at in range(steps):

        @pl.when(step == at)
        def _():
            for ahead in (at, at + 1) if at == 0 else (at + 1,):
                if ahead < steps:
                    for copy in loads[ahead]:
                        copy.start()
            for copy in loads[at]:
                copy.wait()

    weights = buf.at[lax.rem(step, 2)]
    rows_in = x_ref[...].reshape(acc_ref.shape[0], x_ref.shape[2])
    gate = nt(rows_in, weights[0])
    up = nt(rows_in, weights[1])
    sig = 0.5 * jnp.tanh(0.5 * gate) + 0.5
    act = gate * sig
    inner = (act * up).astype(bf16)
    inner_ref[0] = inner
    fa_ref[0] = (up * (sig + act * (1.0 - sig))).astype(bf16)
    fb_ref[0] = act.astype(bf16)
    out = nn(inner, weights[2])

    @pl.when(step == 0)
    def _():
        acc_ref[...] = out

    @pl.when((step > 0) & (step < steps - 1))
    def _():
        acc_ref[...] += out

    @pl.when(step == steps - 1)
    def _():
        y_ref[...] = (acc_ref[...] + out).astype(bf16).reshape(y_ref.shape)


def expert_back_kernel(layout, earlier, last, x_ref, g_ref, inner_ref, fa_ref, fb_ref, *refs):
    pieces, refs = grouped(refs, layout)
    first, refs = (refs[0], refs[1:]) if earlier else (None, refs)
    dx_ref = refs[0]
    dw_refs, refs = grouped(refs[1:], layout)
    acc_ref, term_buf, buf, sems = refs
    step = pl.program_id(0)
    steps = len(layout) // 2
    units = pieces[0][0].shape[1]
    rows = acc_ref.shape[0]
    copies = Copies(sems)
    loads, stores = [], []
    for at in range(steps):
        loads.append([])
        stores.append([])
        for side in range(2):
            which = 2 * at + side
            loads[-1] += chunk_copies(copies, pieces[which], buf.at[at % 2], units, side, True)
            stores[-1] += chunk_copies(copies, dw_refs[which], term_buf.at[at % 2], units, side, False)
    for at in range(steps):

        @pl.when(step == at)
        def _():
            for ahead in (at, at + 1) if at == 0 else (at + 1,):
                if ahead < steps:
                    for copy in loads[ahead]:
                        copy.start()
            for copy in loads[at]:
                copy.wait()
            if at >= 2:
                for copy in stores[at - 2]:
                    copy.wait()

    slot = lax.rem(step, 2)
    weights = buf.at[slot]
    rows_in = x_ref[...].reshape(rows, x_ref.shape[2])
    grad_in = g_ref[...].reshape(rows, g_ref.shape[2])
    grad_inner = nt(grad_in, weights[2])
    grads = jnp.concatenate(
        [(grad_inner * ref[0].astype(f32)).astype(bf16) for ref in (fa_ref, fb_ref)], axis=1
    )
    both = (2, 2 * units, rows_in.shape[1])
    term_buf[slot, 0:2] = tn(grads, rows_in).astype(bf16).reshape(both)
    term_buf[slot, 2] = tn(inner_ref[0], grad_in).astype(bf16)
    for at in range(steps):

        @pl.when(step == at)
        def _():
            for copy in stores[at]:
                copy.start()

    out = nn(grads, weights[0:2].reshape(grads.shape[1], grad_in.shape[1]))

    @pl.when(step == 0)
    def _():
        acc_ref[...] = out if first is None else out + first[...]

    @pl.when((step > 0) & (step < steps - 1))
    def _():
        acc_ref[...] += out

    @pl.when(step == steps - 1)
    def _():
        total = acc_ref[...] + out if steps > 1 else acc_ref[...]
        dx_ref[...] = total.astype(bf16).reshape(dx_ref.shape) if last else total
        for at in range(max(0, steps - 2), steps):
            for copy in stores[at]:
                copy.wait()


def expert_specs(sent, pieces):
    experts, _, width = sent.shape
    chunks = len(pieces)
    units = pieces[0].shape[1]
    rows = experts * CAP
    return dict(
        rows=rows,
        steps=chunks // 2,
        units=units,
        width=width,
        layout=layout_of(pieces),
        any=[pl.BlockSpec(memory_space=pl.ANY)] * len(flat(pieces)),
        x=pl.BlockSpec((experts, CAP, width), lambda c: (0, 0, 0)),
        flops=6 * rows * width * chunks * units,
        nbytes=6 * chunks * units * (rows + width) + 4 * rows * width,
        acc=pltpu.VMEM((rows, width), f32),
        buf=pltpu.VMEM((2, 3, 2 * units, width), bf16),
    )


def expert_call(sent, pieces):
    s = expert_specs(sent, pieces)
    unit = pl.BlockSpec((1, s["rows"], 2 * s["units"]), lambda c: (c, 0, 0))
    hidden = ((s["steps"], s["rows"], 2 * s["units"]), bf16, unit)
    return call(
        functools.partial(expert_kernel, s["layout"]),
        (s["steps"],),
        [s["x"], *s["any"]],
        [(sent.shape, bf16, s["x"])] + [hidden] * 3,
        (sent, *flat(pieces)),
        scratch=[s["acc"], s["buf"], pltpu.SemaphoreType.DMA((sum(s["layout"]),))],
        flops=s["flops"],
        nbytes=s["nbytes"],
    )


def expert_back_call(sent, sent_grads, pieces, inner, factor_a, factor_b, at, earlier=None):
    s = expert_specs(sent, pieces)
    steps = s["steps"]
    unit = pl.BlockSpec((1, s["rows"], 2 * s["units"]), lambda c: (c + at, 0, 0))
    sums = (s["rows"], s["width"])
    outs = call(
        functools.partial(expert_back_kernel, s["layout"], earlier is not None, at == 0),
        (steps,),
        [s["x"], s["x"], unit, unit, unit, *s["any"]]
        + ([whole(sums)] if earlier is not None else []),
        [(sent.shape, bf16, s["x"]) if at == 0 else (sums, f32, whole(sums))]
        + [(piece.shape, bf16, pl.BlockSpec(memory_space=pl.ANY)) for piece in flat(pieces)],
        (sent, sent_grads, inner, factor_a, factor_b, *flat(pieces)) + (() if earlier is None else (earlier,)),
        scratch=[s["acc"], s["buf"], s["buf"], pltpu.SemaphoreType.DMA((2 * sum(s["layout"]),))],
        flops=2 * s["flops"],
        nbytes=2 * s["nbytes"],
    )
    found = grouped(outs[1:], s["layout"])[0]
    return outs[0], [tuple(group) if len(group) > 1 else group[0] for group in found]


def combine_kernel(
    y_ref, res_ref, info_ref, table_ref, grad_ref, sw_ref, prev_ref, gating_ref,
    out_ref, part_ref, gprev_ref, gsw_ref, gvec_ref, ggat_ref,
):
    step = pl.program_id(0)
    choices = prev_ref.shape[0]
    experts = y_ref.shape[0]
    slots = experts * CAP
    some = sw_ref[: info_ref.shape[0], :]
    gain = some[choices + 5 : choices + 6].astype(f32)
    vectors = [some[choices + 6 + c : choices + 7 + c].astype(f32) for c in range(2)]

    def info(at):
        return info_ref[at : at + 1, :]

    routes = [table_ref[j : j + 1, :] for j in range(2)]
    gates = [info(choices + 4), info(choices + 5)]
    alphas = [[info(choices + 2 * c + k) for k in range(2)] for c in range(2)]
    is_const = [[jnp.where(r == experts + 2 + c, 1.0, 0.0) for c in range(2)] for r in routes]
    on_normed = [
        jnp.where(routes[j] == experts + 1, 1.0, 0.0)
        + is_const[j][0] * alphas[0][0]
        + is_const[j][1] * alphas[1][0]
        for j in range(2)
    ]
    weight_const = [gates[0] * is_const[0][c] + gates[1] * is_const[1][c] for c in range(2)]
    weight_vector = [weight_const[c] * alphas[c][1] for c in range(2)]
    direct = gates[0] * on_normed[0] + gates[1] * on_normed[1]
    cols = rows_to_columns(
        [*gates, info(choices + 6), direct, *weight_vector, table_ref[2:3, :], table_ref[3:4, :]]
    )

    grad_low = grad_ref[...]
    grad = grad_low.astype(f32)
    residual = res_ref[...]
    normed = residual * cols[:, 2:3] * gain
    normed_high, normed_mid = split2(normed)
    rows_out = y_ref[...].reshape(slots, y_ref.shape[2])
    slot = lanes_of((TB, slots))
    mixed = residual + cols[:, 3:4] * normed
    for c in range(2):
        mixed = mixed + cols[:, 4 + c : 5 + c] * vectors[c]
    dots = []
    for j in range(2):
        hot = jnp.where(cols[:, 6 + j : 7 + j].astype(i32) == slot, 1.0, 0.0).astype(bf16)
        rows_j = nn(hot, rows_out)
        mixed = mixed + cols[:, j : j + 1] * rows_j
        dots.append(jnp.sum(grad * rows_j, axis=-1, keepdims=True))
    out_ref[...] = mixed.astype(bf16)
    dots.append(jnp.sum(grad * normed, axis=-1, keepdims=True))
    dots = columns_to_rows(dots)
    dot_normed = dots[2:3]
    by_small = nt(some, grad_low)
    dot_vectors = [by_small[choices + 6 + c : choices + 7 + c] for c in range(2)]

    probs = info_ref[:choices, :]
    choice = lax.broadcasted_iota(i32, probs.shape, 0).astype(f32)
    grad_probs = jnp.zeros_like(probs)
    for j in range(2):
        grad_gate = dots[j : j + 1] + on_normed[j] * dot_normed
        for c in range(2):
            grad_gate = grad_gate + is_const[j][c] * alphas[c][1] * dot_vectors[c]
        grad_probs = grad_probs + jnp.where(choice == routes[j], grad_gate, 0.0)
    pieces = [probs * (grad_probs - jnp.sum(probs * grad_probs, axis=0, keepdims=True))]
    for c in range(2):
        grad_alpha = (weight_const[c] * dot_normed, weight_const[c] * dot_vectors[c])
        mean = alphas[c][0] * grad_alpha[0] + alphas[c][1] * grad_alpha[1]
        pieces += [alphas[c][k] * (grad_alpha[k] - mean) for k in range(2)]
    high, mid, low = split3(filled(pieces, some.shape[0]))
    part_ref[...] = cols[:, 3:4] * grad + tn(
        jnp.concatenate([high, mid, low], axis=0), jnp.concatenate([some] * 3, axis=0)
    )
    gating = gating_ref[...]
    gprev_ref[...] = (
        tn(gating, high[:choices]) + tn(gating, mid[:choices]) + tn(gating, low[:choices])
    )[:choices]
    grad_sw = nn(high, normed_high) + nn(mid, normed_high) + nn(high, normed_mid)
    coef_high, coef_mid = split2(filled(weight_vector, gvec_ref.shape[0]))
    grad_vec = nn(coef_high, grad_low) + nn(coef_mid, grad_low)
    prev = prev_ref[...]
    grad_gating = nt(prev, high) + nt(prev, mid) + nt(prev, low)

    @pl.when(step == 0)
    def _():
        gsw_ref[...] = grad_sw
        gvec_ref[...] = grad_vec
        ggat_ref[...] = grad_gating

    @pl.when(step > 0)
    def _():
        gsw_ref[...] += grad_sw
        gvec_ref[...] += grad_vec
        ggat_ref[...] += grad_gating


def combine_call(back, residual, info, table, grad, small_weights, prev, gating_back):
    rows, width = residual.shape
    wide = info.shape[0]
    choices = prev.shape[0]
    slots = back.shape[0] * CAP

    def block(cols):
        return pl.BlockSpec((TB, cols), lambda i: (i, 0))

    def across(count):
        return pl.BlockSpec((count, TB), lambda i: (0, i))

    return call(
        combine_kernel,
        (rows // TB,),
        [
            whole(back.shape), block(width), across(wide), across(8), block(width),
            whole(small_weights.shape), across(choices), whole(gating_back.shape),
        ],
        [
            ((rows, width), bf16, block(width)),
            ((rows, width), f32, block(width)),
            ((choices, rows), f32, across(choices)),
            ((wide, width), f32, whole((wide, width))),
            ((8, width), f32, whole((8, width))),
            ((choices, wide), f32, whole((choices, wide))),
        ],
        (back, residual, info, table, grad, small_weights, prev, gating_back),
        flops=1 << 20,
        nbytes=1 << 20,
    )


def residual_kernel(
    gain_at, dx_ref, part_ref, res_ref, table_ref, grad_ref, sw_ref, wo_ref, att_ref,
    gres_ref, gatt_ref, gwo_ref, ggain_ref, acc_ref,
):
    step = pl.program_id(0)
    experts = dx_ref.shape[0]
    slots = experts * CAP
    slot = lanes_of((TB, slots))
    cols = columns_of(table_ref)
    hot = jnp.where((cols[:, 2:3] == slot) | (cols[:, 3:4] == slot), 1.0, 0.0).astype(bf16)
    grad_normed = part_ref[...] + nn(hot, dx_ref[...].reshape(slots, dx_ref.shape[2]))
    residual = res_ref[...]
    scale = lax.rsqrt(jnp.mean(residual * residual, axis=-1, keepdims=True) + norm_eps)
    unit = residual * scale
    grad_gain = jnp.sum(grad_normed * unit, axis=0, keepdims=True)
    scaled = grad_normed * sw_ref[gain_at : gain_at + 1, :].astype(f32)
    grad_residual = grad_ref[...].astype(f32) + scale * (
        scaled - unit * jnp.mean(scaled * unit, axis=-1, keepdims=True)
    )
    gres_ref[...] = grad_residual
    low = grad_residual.astype(bf16)
    gatt_ref[...] = nt(low, wo_ref[...]).astype(bf16)
    grad_out = tn(att_ref[...], low)

    @pl.when(step == 0)
    def _():
        acc_ref[...] = grad_out
        ggain_ref[...] = grad_gain

    @pl.when(step > 0)
    def _():
        acc_ref[...] += grad_out
        ggain_ref[...] += grad_gain

    @pl.when(step == pl.num_programs(0) - 1)
    def _():
        gwo_ref[...] = acc_ref[...].astype(bf16)


def residual_call(dx, part, residual, table, grad, small_weights, gain_at, w_out, attended):
    rows, width = residual.shape
    slots = dx.shape[0] * CAP

    def block(cols):
        return pl.BlockSpec((TB, cols), lambda i: (i, 0))

    return call(
        functools.partial(residual_kernel, gain_at),
        (rows // TB,),
        [
            whole(dx.shape), block(width), block(width), pl.BlockSpec((8, TB), lambda i: (0, i)), block(width),
            whole(small_weights.shape),
            whole(w_out.shape), block(width),
        ],
        [
            ((rows, width), f32, block(width)),
            ((rows, width), bf16, block(width)),
            ((width, width), bf16, whole((width, width))),
            ((1, width), f32, whole((1, width))),
        ],
        (dx, part, residual, table, grad, small_weights, w_out, attended),
        scratch=[pltpu.VMEM((width, width), f32)],
        flops=2 * slots * rows * width + 4 * rows * width * width,
        nbytes=18 * rows * width + 2 * slots * width,
    )


def qkv_weights_kernel(
    gain_at, where_ref, dq_ref, dk_ref, dv_ref, n_ref, w_ref, small_ref, gwo_ref, ggain_ref, gsw_ref, gvec_ref,
    ggat_ref, own_ref, other_ref, acc_ref,
):
    step = pl.program_id(0)
    count, _, width = own_ref.shape
    part = width // count
    half = part // 2
    shards = dq_ref.shape[1] // part
    normed = n_ref[...]
    core = where_ref[count]
    gain_grad = jnp.zeros((1, width), f32)

    def put(side, shard, at, value):
        rel = where_ref[count + 1 + shard]

        @pl.when(core == side)
        def _():
            own_ref[rel, at : at + value.shape[0], :] = value

        @pl.when(core != side)
        def _():
            other_ref[rel, at : at + value.shape[0], :] = value

    for at, ref in enumerate((dq_ref, dk_ref, dv_ref, None)):
        if ref is None:
            term = gwo_ref[...]
        else:
            full = tn(ref[...], normed)
            gain_grad = gain_grad + jnp.sum(full * w_ref[at].astype(f32), axis=0, keepdims=True)
            term = full.astype(bf16)
        for m in range(shards):
            for side in range(2):
                row = m * part + side * half
                put(side, step * shards + m, at * half, term[row : row + half])

    @pl.when(step == 0)
    def _():
        acc_ref[...] = gain_grad

    @pl.when(step > 0)
    def _():
        acc_ref[...] += gain_grad

    @pl.when(step == pl.num_programs(0) - 1)
    def _():
        gain_one = acc_ref[...] / small_ref[gain_at : gain_at + 1, :].astype(f32)
        vectors = jnp.concatenate(
            [gsw_ref[:gain_at, :], gain_one, ggain_ref[...], gvec_ref[:2, :]], axis=0
        )
        gating_high = ggat_ref[...].astype(bf16).astype(f32)
        gating = (gating_high, ggat_ref[...] - gating_high)
        lanes = lanes_of((1, width)) < part
        split = vectors.shape[0] // 2
        spare = jnp.zeros((16 - split - 1, width), f32)
        for m in range(count):
            here = vectors if m == 0 else pltpu.roll(vectors, width - m * part, 1)
            here = jnp.where(lanes, here, 0.0)
            for side in range(2):
                block = jnp.concatenate(
                    [here[side * split : (side + 1) * split], gating[side], spare], axis=0
                )
                put(side, m, 4 * half, block.astype(bf16))


def qkv_weights_call(where, dq, dk, dv, normed, weights, small, gain_at, gwo, ggain, gsw, gvec, ggat, count):
    rows, width = normed.shape
    steps = 2
    cols = width // steps
    col = pl.BlockSpec((rows, cols), lambda c: (0, c))
    part = width // count
    shape = (count, 2 * part + 16, width)
    return call(
        functools.partial(qkv_weights_kernel, gain_at),
        (steps,),
        [
            pl.BlockSpec(memory_space=pltpu.SMEM), col, col, col, whole(normed.shape),
            pl.BlockSpec((3, cols, width), lambda c: (0, c, 0)), whole(small.shape),
            pl.BlockSpec((cols, width), lambda c: (c, 0)), whole(ggain.shape), whole(gsw.shape), whole(gvec.shape),
            whole(ggat.shape),
        ],
        [(shape, bf16, whole(shape))] * 2,
        (where, dq, dk, dv, normed, weights, small, gwo, ggain, gsw, gvec, ggat),
        scratch=[pltpu.VMEM((1, width), f32)],
        flops=6 * rows * width * width,
        nbytes=8 * rows * width + 18 * width * width,
    )


def finish_kernel(
    choices, where_ref, mine_ref, theirs_ref, gq_ref, gk_ref, gv_ref, gwo_ref, g1_ref, g2_ref, router_ref, gat_ref,
    const_ref, vec_ref,
):
    part, width = gwo_ref.shape
    half = part // 2
    core = where_ref[where_ref.shape[0] // 2]

    def side(which, at, size):
        first = mine_ref[at : at + size, :].astype(f32)
        second = theirs_ref[at : at + size, :].astype(f32)
        return jnp.where(core == which, first, second)

    for at, ref in enumerate((gq_ref, gk_ref, gv_ref, gwo_ref)):
        both = jnp.concatenate([side(0, at * half, half), side(1, at * half, half)], axis=0)
        ref[...] = both
    split = (choices + 8) // 2
    low, high = side(0, 4 * half, 16), side(1, 4 * half, 16)
    small = jnp.concatenate([low[:split, :WIDE], high[:split, :WIDE]], axis=0)
    router_ref[...] = small[:choices, :part]
    const_ref[...] = small[choices : choices + 4, :part]
    g1_ref[...] = small[choices + 4 : choices + 5, :part]
    g2_ref[...] = small[choices + 5 : choices + 6, :part]
    vec_ref[...] = small[choices + 6 : choices + 8, :part]
    gating = (low + high)[split : split + 1, :]
    for at in range(choices):
        moved = gating if at == 0 else pltpu.roll(gating, width - at * choices, 1)
        gat_ref[at : at + 1, :] = moved[:, :choices]


def finish_call(where, mine, theirs, part, choices):
    width = mine.shape[1]
    outs = [(part, width)] * 4 + [
        (1, part), (1, part), (choices, part), (choices, choices), (4, part), (2, part),
    ]
    return call(
        functools.partial(finish_kernel, choices),
        (1,),
        [pl.BlockSpec(memory_space=pltpu.SMEM), whole(mine.shape), whole(mine.shape)],
        [(shape, f32, whole(shape)) for shape in outs],
        (where, mine, theirs),
        flops=1 << 20,
        nbytes=20 * part * width,
    )


def plain_weights_kernel(dq_ref, dk_ref, dv_ref, n_ref, out_ref):
    normed = n_ref[...]
    for part, ref in enumerate((dq_ref, dk_ref, dv_ref)):
        out_ref[part] = tn(ref[...], normed)


def plain_weights_call(dq, dk, dv, normed):
    rows, width = normed.shape
    col = pl.BlockSpec((rows, 256), lambda c: (0, c))
    return call(
        plain_weights_kernel,
        (width // 256,),
        [col, col, col, whole((rows, width))],
        [((3, width, width), f32, pl.BlockSpec((3, 256, width), lambda c: (0, c, 0)))],
        (dq, dk, dv, normed),
        flops=6 * rows * width * width,
        nbytes=8 * rows * width + 12 * width * width,
    )[0]


def hidden_kernel(gain_at, dq_ref, dk_ref, dv_ref, w_ref, hid_ref, small_ref, gres_ref, out_ref):
    grad_normed = nn(dq_ref[...], w_ref[0]) + nn(dk_ref[...], w_ref[1]) + nn(dv_ref[...], w_ref[2])
    hidden = hid_ref[...].astype(f32)
    scale = lax.rsqrt(jnp.mean(hidden * hidden, axis=-1, keepdims=True) + norm_eps)
    unit = hidden * scale
    scaled = grad_normed * small_ref[gain_at : gain_at + 1, :].astype(f32)
    out_ref[...] = gres_ref[...] + scale * (
        scaled - unit * jnp.mean(scaled * unit, axis=-1, keepdims=True)
    )


def hidden_call(dq, dk, dv, weights, hidden, small, gain_at, grad_residual):
    rows, width = hidden.shape
    row = pl.BlockSpec((TB, width), lambda i: (i, 0))
    return call(
        functools.partial(hidden_kernel, gain_at),
        (rows // TB,),
        [row, row, row, whole(weights.shape), row, whole(small.shape), row],
        [((rows, width), f32, row)],
        (dq, dk, dv, weights, hidden, small, grad_residual),
        flops=1 << 20,
        nbytes=1 << 20,
    )[0]


def rope_wide(length):
    inverse = rope_base ** (-(2.0 * jnp.arange(HD // 2, dtype=f32)) / HD)
    angles = jnp.arange(length, dtype=f32)[:, None] * inverse[None, :]
    cosine, sine = jnp.cos(angles), jnp.sin(angles)
    return (
        jnp.concatenate([cosine] * 4, axis=1),
        jnp.concatenate([-sine, sine, -sine, sine], axis=1),
    )


def to_rows(flat, width):
    count = -(-flat.shape[1] // width)
    return jnp.pad(flat, ((0, 0), (0, count * width - flat.shape[1]))).reshape(
        flat.shape[0], count, width
    )


def per_device(
    hidden_in,
    prev_logits,
    seq_lengths,
    seq_order,
    routes,
    w_query,
    w_key,
    w_value,
    w_output,
    gain_attn,
    gain_moe,
    w_router,
    w_gating,
    w_const,
    v_const,
    w_gate,
    w_up,
    w_down,
    out_grad,
):
    rows, width = hidden_in.shape[1:]
    experts = lax.axis_size("expert")
    shards = lax.axis_size("fsdp")
    choices = w_router.shape[1]
    part = width // shards
    hidden = hidden_in.reshape(rows, width)
    grad = out_grad.reshape(rows, width)
    prev = prev_logits.reshape(rows, choices).T

    fsdp_here = lax.axis_index("fsdp")
    own = lax.axis_index("expert") * shards + fsdp_here
    live = lax.dynamic_slice(seq_lengths, (own,), (1,))
    dealt = lax.all_gather(routes.reshape(rows, 2).T, "expert", axis=0, tiled=False)
    peers = jnp.arange(experts, dtype=i32) * shards + fsdp_here
    table = deal_call((seq_order[peers] == own).astype(i32), dealt)
    cos_wide, sin_wide = rope_wide(rows)

    gain_at = choices + 4
    small_count = choices + 8
    order = ring_order(shards)
    place = jnp.asarray([order.index(m) for m in range(shards)], dtype=i32)
    spot = place[fsdp_here]
    core = lax.rem(lax.axis_index("expert"), 2)
    paired = part % 32 == 0 and small_count == 16 and shards % 2 == 0 and experts & (experts - 1) == 0
    ring = jnp.asarray(order, dtype=i32)
    where = jnp.concatenate(
        [ring[(spot + jnp.arange(shards, dtype=i32)) % shards], core[None], (place - spot) % shards]
    )
    expert_pack = pack_experts_call(w_gate, w_up, w_down)
    if paired:
        pack, spare = pack_call(
            core[None], w_query.T, w_key.T, w_value.T, w_output, w_router.T, w_const.T, gain_attn[None], gain_moe[None], v_const
        )
        own = ring_gather(pack, order, 0, [(), (cos_wide, sin_wide), (dealt,), (expert_pack, table)])
        own[shards // 2] = jnp.concatenate(own[shards // 2], axis=0)
        other = [spare] + [swap(piece, experts, 1) for piece in own[1:]]
        expert_pack, _ = lax.optimization_barrier((expert_pack, own[shards // 2]))
        query, key, value, normed_one, qkv_weights, w_out, small = qkv_pieces_call(
            hidden, where, own, other, gain_at, part, cos_wide, sin_wide
        )
    else:
        small_parts = jnp.concatenate(
            [w_router.T, w_const.T, gain_attn[None], gain_moe[None], v_const], axis=0
        )
        first_pack = jnp.concatenate(
            [w_query.T, w_key.T, w_value.T, to_rows(small_parts.reshape(1, -1), width)[0]], axis=0
        )
        first = lax.all_gather(first_pack, "fsdp", axis=0, tiled=False)
        w_out = lax.all_gather(w_output, "fsdp", axis=0, tiled=True)
        qkv_weights = (
            first[:, : 3 * part]
            .reshape(shards, 3, part, width)
            .transpose(1, 0, 2, 3)
            .reshape(3, width, width)
        )
        small = (
            first[:, 3 * part :]
            .reshape(shards, -1)[:, : small_count * part]
            .reshape(shards, small_count, part)
            .transpose(1, 0, 2)
            .reshape(small_count, width)
        )
        small = jnp.pad(small, ((0, WIDE - small_count), (0, 0)))
        query, key, value, normed_one = qkv_call(
            hidden, small, gain_at, qkv_weights, cos_wide, sin_wide
        )
    pairs = width // PAIR
    some = pairs // 2
    early = attend_call(live, query, key, value, 0, some)
    expert_weights = ring_gather(expert_pack, order, 1, [()] + [early[:1]])
    farthest = shards // 2
    turns = [0] + [r for k in range(1, farthest) for r in (k, shards - k)] + [farthest]
    by_turn = [expert_weights[r] for r in turns]

    def after(value, step):
        if step >= farthest:
            return value
        return lax.optimization_barrier((value, expert_weights[step], expert_weights[-step]))[0]

    gating_wide = jnp.pad(w_gating, ((0, 0), (0, WIDE - choices)))
    gating_back = jnp.pad(w_gating.T, ((0, 0), (0, WIDE - choices)))

    attended, recip, expo = attend_call(
        live, after(query, 1), key, value, some, pairs - some, early
    )
    residual, info, normed_low, route_grads = route_call(
        attended, hidden, grad, w_out, small, prev, gating_wide, table
    )
    send_rows, send_grads = dispatch_call(table, after(normed_low, 2), route_grads, experts)
    sent = lax.all_to_all(send_rows, "expert", split_axis=0, concat_axis=0, tiled=True)
    sent_grads = lax.all_to_all(send_grads, "expert", split_axis=0, concat_axis=0, tiled=True)
    expert_out, inner, factor_a, factor_b = expert_call(sent, by_turn)
    returned = lax.all_to_all(expert_out, "expert", split_axis=0, concat_axis=0, tiled=True)
    lead = shards // 4
    cuts = [(lead, shards // 2), (0, lead)] if lead else [(0, shards // 2)]
    terms, sofar = [None] * shards, None
    for low, high in cuts:
        chosen = slice(2 * low, 2 * high)
        sofar, found = expert_back_call(
            sent, sent_grads, by_turn[chosen], inner, factor_a, factor_b, low, sofar
        )
        terms[chosen] = found
    sums = RingReduce([terms[turns.index(r)] for r in range(shards)], order, 1)
    sums.start()
    sums.flight, sofar = lax.optimization_barrier((sums.flight, sofar))
    returned_dx = lax.all_to_all(sofar, "expert", split_axis=0, concat_axis=0, tiled=True)

    def before(value):
        if not sums.left:
            return value
        sums.add()
        value, sums.ready = lax.optimization_barrier((value, sums.ready))
        sums.send()
        return value

    hidden_out, part_grad, grad_prev, grad_sw, grad_vec, grad_gating = combine_call(
        before(returned), residual, info, table, grad, small, prev, gating_back
    )
    grad_residual, grad_attended, grad_wo, grad_gain_two = residual_call(
        returned_dx, part_grad, residual, table, grad, small, gain_at + 1, w_out, attended
    )
    dq, dk, dv = attend_back_call(
        query, key, value, expo, before(grad_attended), attended, recip, cos_wide, sin_wide
    )
    while sums.left:
        dq = before(dq)
    grad_hidden = hidden_call(dq, dk, dv, qkv_weights, hidden, small, gain_at, grad_residual)
    if paired:
        own, other = qkv_weights_call(
            where, dq, dk, dv, normed_one, qkv_weights, small, gain_at, grad_wo, grad_gain_two, grad_sw, grad_vec,
            jnp.pad(grad_gating[:, :choices].reshape(1, -1), ((0, 0), (0, width - choices * choices))), shards,
        )
        got = swap(other, experts, 1)
        sums.flight, grad_hidden = lax.optimization_barrier((sums.flight, grad_hidden))
        expert_grads = sums.finish()
        got, expert_grads = lax.optimization_barrier((got, expert_grads))
        shared = RingReduce([plus(own[r], got[r]) for r in range(shards)], order, 0)
        shared.start()
        while shared.left:
            shared.turn()
        mine = shared.result().astype(bf16)
        bit = 2
        while bit < experts:
            mine = plus(mine, swap(mine, experts, bit))
            bit *= 2
        theirs = swap(mine, experts, 1)
        shared_grads = finish_call(where, mine, theirs, part, choices)
        shared_grads = [
            g[0] if at in (4, 5) else g.T if at in (0, 1, 2, 6, 8) else g
            for at, g in enumerate(shared_grads)
        ]
    else:
        grad_qkv = plain_weights_call(dq, dk, dv, normed_one)
        grad_gain_one = jnp.sum(grad_qkv * qkv_weights.astype(f32), axis=(0, 1))[None] / small[
            gain_at : gain_at + 1
        ].astype(f32)
        small_grads = jnp.concatenate(
            [grad_sw[:gain_at], grad_gain_one, grad_gain_two, grad_vec[:2]], axis=0
        )
        small_flat = (
            small_grads.reshape(small_count, shards, part).transpose(1, 0, 2).reshape(shards, -1)
        )
        gating_flat = grad_gating[:, :choices].reshape(1, -1)
        gating_both = jnp.concatenate(split2(gating_flat), axis=1)
        flat = jnp.concatenate(
            [small_flat.astype(bf16), jnp.broadcast_to(gating_both, (shards, gating_both.shape[1]))], axis=1
        )
        shared = jnp.concatenate(
            [
                grad_qkv.astype(bf16)
                .reshape(3, shards, part, width)
                .transpose(1, 0, 2, 3)
                .reshape(shards, 3 * part, width),
                grad_wo.reshape(shards, part, width),
                to_rows(flat, width),
            ],
            axis=1,
        )
        scattered = lax.psum_scatter(shared, "fsdp", scatter_dimension=0, tiled=False)
        total = lax.psum(scattered, "expert").astype(f32)
        flat_total = total[4 * part :].reshape(-1)
        small_total = flat_total[: small_count * part].reshape(small_count, part)
        at = small_count * part
        gating_total = flat_total[at : at + 2 * choices * choices].reshape(2, choices, choices)
        shared_grads = [total[at * part : (at + 1) * part].T for at in range(3)] + [
            total[3 * part : 4 * part],
            small_total[gain_at],
            small_total[gain_at + 1],
            small_total[:choices].T,
            jnp.sum(gating_total, axis=0),
            small_total[choices:gain_at].T,
            small_total[gain_at + 2 :],
        ]
        expert_grads = sums.finish()
    return (hidden_out[None], grad_hidden[None], grad_prev.T[None], *shared_grads, *expert_grads)


def solution(mesh):
    rows = P(("expert", "fsdp"), None, None)
    ins = (
        rows, rows, P(), P(), rows,
        P(None, "fsdp"), P(None, "fsdp"), P(None, "fsdp"), P("fsdp", None),
        P("fsdp"), P("fsdp"), P("fsdp", None), P(), P("fsdp", None), P(None, "fsdp"),
        P("expert", None, "fsdp"), P("expert", None, "fsdp"), P("expert", "fsdp", None), rows,
    )
    outs = (
        rows, rows, rows,
        P(None, "fsdp"), P(None, "fsdp"), P(None, "fsdp"), P("fsdp", None),
        P("fsdp"), P("fsdp"), P("fsdp", None), P(), P("fsdp", None), P(None, "fsdp"),
        P("expert", None, "fsdp"), P("expert", None, "fsdp"), P("expert", "fsdp", None),
    )
    return jax.shard_map(per_device, mesh=mesh, in_specs=ins, out_specs=outs, check_vma=False)
```
